32 devices in a mesh: view: 4 (over x, core), depth: 8 (over z, y).
Axes of the slice: x: 2, y: 2, z: 4, core: 2. Of those that a mesh axis runs over, the one named last changes fastest.
Arguments:
- features: float32 [4, 8, 32, 3, 4096], P('view', 'depth'), may hold values from -6 to 6
- spacing: float32 [4, 8, 3, 4096], P('view', 'depth'), may hold values from 0.01 to 0.15
- counts: int32 [4, 8, 4096], P('view', 'depth'), may hold values from 0 to 3
- depth_rank: int32 [4, 8], P('view', 'depth'), may hold values from 0 to 7, as said below
- target: float32 [4, 64, 4096], P('view', None, 'depth'), may hold values from 0 to 1
- first_weight: float32 [32, 256], replicated, may hold values from -1 to 1
- first_bias: float32 [256], replicated, may hold values from -3 to 3
- second_weight: float32 [256, 256], replicated, may hold values from -0.375 to 0.375
- second_bias: float32 [256], replicated, may hold values from -3 to 3
- last_weight: float32 [256, 65], replicated, may hold values from -0.375 to 0.375
- last_bias: float32 [65], replicated, may hold values from -3 to 3
Outputs:
- pixels: float32 [4, 64, 4096], P('view', None, 'depth')
- first_update: float32 [32, 256], replicated
- first_shift: float32 [256], replicated
- second_update: float32 [256, 256], replicated
- second_shift: float32 [256], replicated
- last_update: float32 [256, 65], replicated
- last_shift: float32 [65], replicated
The draws below stay inside these ranges and needn't reach their ends.
Inputs may be any that keep to these rules, and one draw needn't show every extreme that they name: depth_rank[v, d] equals d XOR a number fixed for view group v, so each view group's ranks are a permutation in which every aligned block of 2^k regions takes consecutive positions. Sample slots s with s < counts[v, d, r] are live.
All inputs are finite; a program needn't handle non-finite values.
Results may differ from the reference program's by a relative error of at most 0.0003.
Values sent between devices are 32-bit elements; how exact they have to be, the bound alone decides.
A program may use at most 128 MiB of HBM per device.

```python
import math
import jax
import jax.numpy as jnp
from jax import lax

FEAT = 32
HIDDEN_SIZE = 256
CHANNELS = 64
SAMPLES = 3
RAYS = 4096
OUT = 65
VIEWS = 4
REGIONS = 8


def draw_depth_rank(key, part):
    region_ids = jnp.arange(REGIONS, dtype=jnp.int32)
    flips = jax.random.randint(jax.random.fold_in(key, 17), (VIEWS, 1), 0, REGIONS).astype(jnp.int32)
    return jnp.bitwise_xor(region_ids[None, :], flips).astype(jnp.int32)


def plant(entries, key, low, high):
    longest = entries.shape.index(max(entries.shape))
    spots = []
    for shift in (0, 1):
        where = [jax.random.randint(jax.random.fold_in(key, axis), (), 0, length) for axis, length in enumerate(entries.shape)]
        where[longest] = (where[longest] + shift) % entries.shape[longest]
        spots.append(tuple(where))
    return entries.at[spots[0]].set(low).at[spots[1]].set(high)


def block_scale(rng, extent, shards, low, high):
    gain = 1.0
    for dim, shards_of in shards:
        steps = jax.random.uniform(jax.random.fold_in(jax.random.fold_in(rng, 6), dim), (shards_of,), jnp.float32, low / len(shards), high / len(shards))
        gain = gain * jnp.repeat(jnp.exp(steps), extent[dim] // shards_of).reshape((-1,) + (1,) * (len(extent) - 1 - dim))
    return gain


def normal_values(own_key, shape, deviation, most, pieces=(), kind=jnp.bfloat16):
    entries = jax.random.normal(own_key, shape, jnp.float32) * deviation
    if len(pieces) > 0:
        entries = block_scale(own_key, shape, pieces, -0.22, 0.18) * entries
    return jnp.clip(entries, min=-most, max=most).astype(kind)


def setup_inputs(seed: int = 0) -> dict:
    key_of = jax.random.split(jax.random.key(seed), 12)
    features = normal_values(key_of[0], (VIEWS, REGIONS, FEAT, SAMPLES, RAYS), 1.0, 6.0, ((0, 4), (1, 8)), jnp.float32)
    spacing = jnp.clip(jnp.exp(math.log(0.15) - 2.7080503 * jax.random.uniform(key_of[1], (VIEWS, REGIONS, SAMPLES, RAYS), jnp.float32) ** block_scale(key_of[1], (VIEWS, REGIONS, SAMPLES, RAYS), ((0, 4), (1, 8)), -0.2, 0.2)), 0.01, 0.15)
    counts = plant(jax.random.randint(key_of[2], (VIEWS, REGIONS, RAYS), 0, SAMPLES + 1), jax.random.fold_in(key_of[2], 1), 0, SAMPLES).astype(jnp.int32)
    depth_rank = draw_depth_rank(jax.random.fold_in(key_of[11], 71), 0)
    target = jnp.clip(1.0 * jax.random.uniform(key_of[4], (VIEWS, CHANNELS, RAYS), jnp.float32) ** block_scale(key_of[4], (VIEWS, CHANNELS, RAYS), ((0, 4), (2, 8)), -0.2, 0.2), 0.0, 1.0)
    first_weight = normal_values(key_of[5], (FEAT, HIDDEN_SIZE), FEAT ** -0.5, 1.0, (), jnp.float32)
    first_bias = normal_values(key_of[6], (HIDDEN_SIZE,), 0.5, 3.0, (), jnp.float32)
    second_weight = normal_values(key_of[7], (HIDDEN_SIZE, HIDDEN_SIZE), HIDDEN_SIZE ** -0.5, 0.375, (), jnp.float32)
    second_bias = normal_values(key_of[8], (HIDDEN_SIZE,), 0.5, 3.0, (), jnp.float32)
    last_weight = normal_values(key_of[9], (HIDDEN_SIZE, OUT), HIDDEN_SIZE ** -0.5, 0.375, (), jnp.float32)
    last_bias = normal_values(key_of[10], (OUT,), 0.5, 3.0, (), jnp.float32)
    return {"features": features, "spacing": spacing, "counts": counts, "depth_rank": depth_rank, "target": target, "first_weight": first_weight, "first_bias": first_bias, "second_weight": second_weight, "second_bias": second_bias, "last_weight": last_weight, "last_bias": last_bias}


precise = lax.Precision.HIGHEST
epsilon = 1e-05

def project(weight, inputs):
    return lax.dot_general(weight, inputs, (((0,), (0,)), ((), ())), precision=precise, preferred_element_type=jnp.float32)

def render(params, sample_feats, sample_spacing, live_mask):
    first_weight, first_bias, second_weight, second_bias, last_weight, last_bias = params
    columns = sample_feats.reshape(sample_feats.shape[0], -1)
    first_act = jax.nn.relu(project(first_weight, columns) + first_bias[:, None])
    second_act = jax.nn.relu(project(second_weight, first_act) + second_bias[:, None])
    raw_output = project(last_weight, second_act) + last_bias[:, None]
    raw_output = raw_output.reshape(raw_output.shape[0], sample_spacing.shape[0], sample_spacing.shape[1])
    channels = raw_output.shape[0] - 1
    sample_color = jax.nn.sigmoid(raw_output[:channels])
    density = jax.nn.softplus(raw_output[channels])
    optical = density * sample_spacing * live_mask
    before = jnp.cumsum(optical, axis=0) - optical
    weight = jnp.exp(-before) * (1.0 - jnp.exp(-optical))
    region_color = lax.optimization_barrier(jnp.sum(weight[None] * sample_color, axis=1))
    region_depth = lax.optimization_barrier(jnp.sum(optical, axis=0))
    return (region_color, region_depth)

def normalize(gradient):
    return gradient / jnp.sqrt(jnp.mean(gradient * gradient) + epsilon)

def reference(features, spacing, counts, depth_rank, target, first_weight, first_bias, second_weight, second_bias, last_weight, last_bias):
    params = (first_weight, first_bias, second_weight, second_bias, last_weight, last_bias)
    sample_ids = jnp.arange(SAMPLES, dtype=jnp.int32)
    live_mask = (sample_ids[None, None, :, None] < counts[:, :, None, :]).astype(jnp.float32)
    flat_feats = features.reshape(VIEWS * REGIONS, FEAT, SAMPLES, RAYS)
    flat_spacing = spacing.reshape(VIEWS * REGIONS, SAMPLES, RAYS)
    flat_live = live_mask.reshape(VIEWS * REGIONS, SAMPLES, RAYS)

    def forward(scan_items):
        return render(params, scan_items[0], scan_items[1], scan_items[2])
    colors, depths = lax.map(forward, (flat_feats, flat_spacing, flat_live))
    colors = colors.reshape(VIEWS, REGIONS, CHANNELS, RAYS)
    depths = depths.reshape(VIEWS, REGIONS, RAYS)
    earlier = (depth_rank[:, None, :] < depth_rank[:, :, None]).astype(jnp.float32)
    later_mask = (depth_rank[:, None, :] > depth_rank[:, :, None]).astype(jnp.float32)
    passed = jnp.exp(-jnp.einsum('vde,ver->vdr', earlier, depths, precision=precise))
    weighted = passed[:, :, None, :] * colors
    pixels = lax.optimization_barrier(jnp.sum(weighted, axis=1))
    misfit = pixels - target
    color_grad = passed[:, :, None, :] * misfit[:, None]
    behind = jnp.einsum('vde,vecr->vdcr', later_mask, weighted, precision=precise)
    depth_grad = -lax.optimization_barrier(jnp.sum(misfit[:, None] * behind, axis=2))

    def accumulate(running, scan_items):
        sample_feats, sample_spacing, live_part, color_part, depth_part = scan_items
        unused, pullback = jax.vjp(lambda weights: render(weights, sample_feats, sample_spacing, live_part), params)
        gradients = pullback((color_part, depth_part))[0]
        return (jax.tree.map(jnp.add, running, gradients), None)
    zero_grads = jax.tree.map(jnp.zeros_like, params)
    totals, unused_out = lax.scan(accumulate, zero_grads, (flat_feats, flat_spacing, flat_live, color_grad.reshape(VIEWS * REGIONS, CHANNELS, RAYS), depth_grad.reshape(VIEWS * REGIONS, RAYS)))
    return (pixels, normalize(totals[0]), normalize(totals[1]), normalize(totals[2]), normalize(totals[3]), normalize(totals[4]), normalize(totals[5]))
```

```python
import functools

import jax
import jax.numpy as jnp
from jax import lax
from jax.experimental import pallas as pl
from jax.experimental.pallas import tpu as pltpu
from jax.sharding import PartitionSpec as P

epsilon = 1e-05
PAD = 80
MESH = pl.DeviceIdType.MESH
f32 = jnp.float32
bf16 = jnp.bfloat16


def split(value):
    high = value.astype(bf16)
    low = (value - high.astype(f32)).astype(bf16)
    return high, low


def mm(left, right):
    return lax.dot_general(left, right, (((1,), (0,)), ((), ())), preferred_element_type=f32)


def mm_nt(left, right):
    return lax.dot_general(left, right, (((1,), (1,)), ((), ())), preferred_element_type=f32)


def opticals(raw, channels, spacing, counts, samples, rays):
    out = []
    for s in range(samples):
        logit = raw[channels : channels + 1, s * rays : (s + 1) * rays]
        density = jnp.maximum(logit, 0.0) + jnp.log1p(jnp.exp(-jnp.abs(logit)))
        length = jnp.where(s < counts, spacing[s], 0.0)
        out.append((logit, density * length, length))
    return out


def remote(src, dst, sems, slot, device):
    return pltpu.make_async_remote_copy(
        src_ref=src,
        dst_ref=dst,
        send_sem=sems[0].at[slot],
        recv_sem=sems[1].at[slot],
        device_id=device,
        device_id_type=MESH,
    )


def lanes(value):
    total = value[:, 0:128]
    for lane in range(128, value.shape[1], 128):
        total = total + value[:, lane : lane + 128]
    return total


def round_up(blocks, devices):
    return -(-blocks // devices) * devices


def block_counts(feat, hidden, devices):
    across = hidden // 128
    late = feat // 8 * across + 1
    early = (hidden + PAD) // 8 * across + 1
    return round_up(early, devices), round_up(late, devices)


def fill(grads, accs, rows):
    at = 0
    for acc in accs:
        blocks = acc.shape[0] // 8
        for lane in range(0, acc.shape[1], 128):
            grads[at : at + blocks] = acc[:, lane : lane + 128].reshape(blocks, 8, 128)
            at += blocks
    grads[at:] = jnp.zeros((grads.shape[0] - at, 8, 128), f32)
    added = jnp.sum(rows.T, axis=0, keepdims=True)
    for i, lane in enumerate(range(0, rows.shape[0], 128)):
        grads[at, i : i + 1, :] = added[:, lane : lane + 128]


def total_stages(views, regions, grads, total, sums, sems):
    me = lax.axis_index("depth")
    view = lax.axis_index("view")
    vlevels = views.bit_length() - 1
    blocks = grads.shape[0]
    small = blocks // (views * regions)
    landing = sums[2 * vlevels]

    def bit_of(b):
        return lax.rem(view // (1 << b), 2)

    def view_partner(b):
        return {"view": view + (1 - 2 * bit_of(b)) * (1 << b)}

    def peer(r):
        return {"depth": lax.rem(me + r, regions)}

    def held(b):
        return grads if b == 0 else sums[2 * b - 1]

    def base(b):
        start = 0
        for c in range(b):
            start = start + bit_of(c) * (blocks >> (c + 1))
        return start

    def scatter_view(b):
        size = blocks >> (b + 1)
        part = pl.ds((1 - bit_of(b)) * size, size)
        return [remote(held(b).at[part], sums[2 * b], sems, b, view_partner(b))]

    def add_view(b):
        size = blocks >> (b + 1)
        sums[2 * b + 1][...] = held(b)[pl.ds(bit_of(b) * size, size)] + sums[2 * b][...]

    def scatter_depth():
        return [
            remote(
                held(vlevels).at[pl.ds(lax.rem(me + r, regions) * small, small)],
                landing.at[r - 1], sems, vlevels + r - 1, peer(r),
            )
            for r in range(1, regions)
        ]

    def spot():
        return pl.ds(base(vlevels) + me * small, small)

    def add_depth():
        mine = held(vlevels)[pl.ds(me * small, small)]
        for r in range(1, regions):
            mine = mine + landing[r - 1]
        total[spot()] = mine

    def gather_depth():
        part = total.at[spot()]
        first = vlevels + regions - 1
        return [remote(part, part, sems, first + r - 1, peer(r)) for r in range(1, regions)]

    def gather_view(b):
        part = total.at[pl.ds(base(b + 1), blocks >> (b + 1))]
        slot = vlevels + 2 * (regions - 1) + b
        return [remote(part, part, sems, slot, view_partner(b))]

    moves = [
        (functools.partial(scatter_view, b), functools.partial(add_view, b))
        for b in range(vlevels)
    ]
    moves.append((scatter_depth, add_depth))
    moves.append((gather_depth, None))
    moves += [(functools.partial(gather_view, b), None) for b in reversed(range(vlevels))]

    def stage(n):
        if n > 0:
            copies, after = moves[n - 1]
            for copy in copies():
                copy.wait()
            if after is not None:
                after()
        if n < len(moves):
            for copy in moves[n][0]():
                copy.start()

    return [functools.partial(stage, n) for n in range(len(moves) + 1)]


def prepare(feat, w1_ref, b1_ref, w2_ref, b2_ref, w3_ref, b3_ref, w1s, w2f, w2b, w3f, w3b, cols):
    hidden = w2_ref.shape[0]
    outs = w3_ref.shape[0]
    high, low = split(w1_ref[...])
    bias = b1_ref[...]
    bias_a = bias.astype(bf16).astype(f32)
    bias_b = (bias - bias_a).astype(bf16).astype(f32)
    cols[...] = jnp.zeros_like(cols)
    cols[0:feat, :] = high.astype(f32)
    cols[feat : 2 * feat, :] = high.astype(f32)
    cols[2 * feat : 3 * feat, :] = low.astype(f32)
    cols[3 * feat : 3 * feat + 1, :] = bias_a
    cols[3 * feat + 1 : 3 * feat + 2, :] = bias_b
    cols[3 * feat + 2 : 3 * feat + 3, :] = bias - bias_a - bias_b
    cols[3 * feat + 3 : 3 * feat + 4, :] = b2_ref[...]
    cols[3 * feat + 4 : 3 * feat + 5, 0:outs] = b3_ref[...]
    turned = cols[0:128, :].T
    w1s[...] = turned.astype(bf16)
    cols[:, 0:128] = turned
    high, low = split(w2_ref[...].T)
    w2f[:, 0:hidden] = high
    w2f[:, hidden : 2 * hidden] = high
    w2f[:, 2 * hidden : 3 * hidden] = low
    high, low = split(w2_ref[...])
    w2b[:, 0:hidden] = high
    w2b[:, hidden : 2 * hidden] = low
    tall = jnp.concatenate([w3_ref[...], jnp.zeros((PAD - outs, hidden), f32)], axis=0)
    high, low = split(tall)
    w3f[0:PAD, :] = high
    w3f[PAD : 2 * PAD, :] = low
    high = high.astype(f32)
    stack = jnp.concatenate(
        [high, high, tall - high, jnp.zeros((256 - 3 * PAD, hidden), f32)], axis=0
    )
    w3b[...] = stack.T.astype(bf16)


def forward_tile(feat, channels, x, spacing, counts, w1s, w2f, w3f, cols, keep_x, keep_h, keep_raw):
    samples = len(spacing)
    rays = spacing[0].shape[1]
    xh, xl = split(x)
    keep_x[0] = xh
    keep_x[1] = xl
    rows = lax.broadcasted_iota(jnp.int32, x.shape, 0)
    ones = jnp.where(rows < 3, 1.0, 0.0).astype(bf16)
    z1 = mm(w1s[...], jnp.concatenate([xh, xl, xh, ones], axis=0))
    h1h, h1l = split(jnp.maximum(z1, 0.0))
    keep_h[0] = h1h
    z2 = mm(w2f[...], jnp.concatenate([h1h, h1l, h1h], axis=0))
    z2 = z2 + cols[:, 3 * feat + 3 : 3 * feat + 4]
    h2h, h2l = split(jnp.maximum(z2, 0.0))
    keep_h[1] = h2h
    both = mm(w3f[...], h2h)
    raw = both[0:PAD] + both[PAD:] + mm(w3f[0:PAD, :], h2l)
    raw = raw + cols[0:PAD, 3 * feat + 4 : 3 * feat + 5]
    keep_raw[...] = raw
    before = None
    color = None
    parts = opticals(raw, channels, spacing, counts, samples, rays)
    for s, (_, optical, _) in enumerate(parts):
        weight = 1.0 - jnp.exp(-optical)
        if s:
            weight = jnp.exp(-before) * weight
        shade = weight * jax.nn.sigmoid(raw[0:channels, s * rays : (s + 1) * rays])
        color = shade if s == 0 else color + shade
        before = optical if s == 0 else before + optical
    return color, before


def backward_tile(
    channels, raw, misfit, state, spacing, counts, keep_h, w3b, acc2, acc3, bias,
):
    samples = len(spacing)
    rays = spacing[0].shape[1]
    hidden = w3b.shape[0]
    passed = state[0:1]
    parts = opticals(raw, channels, spacing, counts, samples, rays)
    befores, before = [], None
    for s in range(samples):
        befores.append(before)
        before = parts[s][1] if s == 0 else before + parts[s][1]
    tail = -state[1:2]
    pieces = [None] * samples
    for s in reversed(range(samples)):
        logit, optical, length = parts[s]
        gone = jnp.exp(-optical)
        ahead = 1.0 if s == 0 else jnp.exp(-befores[s])
        weight = ahead * (1.0 - gone)
        color = jax.nn.sigmoid(raw[0:channels, s * rays : (s + 1) * rays])
        weight_grad = passed * jnp.sum(misfit * color, axis=0, keepdims=True)
        optical_grad = weight_grad * (ahead * gone) + tail
        tail = tail - weight_grad * weight
        color_grad = (weight * passed) * misfit * (color * (1.0 - color))
        logit_grad = optical_grad * length * jax.nn.sigmoid(logit)
        row = lax.broadcasted_iota(jnp.int32, (PAD - channels, rays), 0)
        rest = jnp.where(row == 0, jnp.broadcast_to(logit_grad, row.shape), 0.0)
        pieces[s] = jnp.concatenate([color_grad, rest], axis=0)
    draw = jnp.concatenate(pieces, axis=1)
    bias[2 * hidden : 2 * hidden + PAD, :] += lanes(draw)
    dh, dl = split(draw)
    h2h = keep_h[1]
    both = mm_nt(jnp.concatenate([dh, dl], axis=0), h2h)
    acc3[...] += both[0:PAD] + both[PAD:]
    zero = jnp.zeros((256 - 3 * PAD, draw.shape[1]), bf16)
    dh2 = mm(w3b[...], jnp.concatenate([dh, dl, dh, zero], axis=0))
    dz2 = jnp.where(h2h > 0, dh2, 0.0)
    bias[hidden : 2 * hidden, :] += lanes(dz2)
    zh = dz2.astype(bf16)
    h1h = keep_h[0]
    acc2[...] += mm_nt(h1h, zh)
    keep_h[1] = zh


def first_layer_tile(keep_x, keep_h, w2b, acc1, bias):
    hidden = w2b.shape[0]
    feat = keep_x.shape[1]
    h1h = keep_h[0]
    zh = keep_h[1]
    dh1 = mm(w2b[...], jnp.concatenate([zh, zh], axis=0))
    dz1 = jnp.where(h1h > 0, dh1, 0.0)
    bias[0:hidden, :] += lanes(dz1)
    xh = keep_x[0]
    xl = keep_x[1]
    both = mm_nt(jnp.concatenate([xh, xl], axis=0), dz1.astype(bf16))
    acc1[...] += both[0:feat] + both[feat:]


def step_kernel(
    views, regions,
    feats, spacing, counts, target, rank_ref, w1, b1, w2, b2, w3, b3,
    pixels, total, total_late,
    w1s, w2f, w2b, w3f, w3b, cols, keep_x, keep_h, keep_raw, back, grads, grads_late,
    acc1, acc2, acc3, bias, fsend, frecv, msend, mrecv, nsend, nrecv, gsend, grecv, lsend, lrecv,
    *scratch,
):
    samples, feat, rays = feats.shape
    channels, seg = target.shape
    levels = regions.bit_length() - 1
    rows = back.shape[1]
    hidden = w2.shape[0]
    me = lax.axis_index("depth")
    view = lax.axis_index("view")
    vlevels = views.bit_length() - 1
    work = scratch[0 : levels + 1]
    got = scratch[levels + 1 : 2 * levels + 1]
    notes = scratch[2 * levels + 1 : 3 * levels + 1]
    sums = scratch[3 * levels + 1 :]

    def bit_of(value, b):
        return lax.rem(value // (1 << b), 2)

    def partner(b):
        return {"depth": me + (1 - 2 * bit_of(me, b)) * (1 << b)}

    def view_partner(b):
        return {"view": view + (1 - 2 * bit_of(view, b)) * (1 << b)}

    def peer(r):
        return {"depth": lax.rem(me + r, regions)}

    barrier = pltpu.get_barrier_semaphore()
    for b in range(vlevels):
        pl.semaphore_signal(barrier, inc=1, device_id=view_partner(b), device_id_type=MESH)
    for r in range(1, regions):
        pl.semaphore_signal(barrier, inc=1, device_id=peer(r), device_id_type=MESH)

    prepare(feat, w1, b1, w2, b2, w3, b3, w1s, w2f, w2b, w3f, w3b, cols)

    def span_of(k):
        where = 0
        for b in range(levels):
            where = where + lax.rem(bit_of(me, b) + bit_of(k, levels - 1 - b), 2) * (1 << b)
        return pl.ds(pl.multiple_of(where * seg, seg), seg)

    rank = rank_ref[0:1, 0:1]

    def first(b):
        return lax.rem(lax.div(rank, jnp.full_like(rank, 1 << b)), jnp.full_like(rank, 2)) == 0

    def color_copy(j, kk):
        n2 = regions >> (j + 1)
        return remote(work[j].at[n2 + kk], got[j].at[kk], (fsend, frecv), n2 + kk, partner(j))

    def misfit_copy(j, kk):
        n2 = regions >> (j + 1)
        part = pl.ds(0, channels)
        return remote(
            back.at[kk, part], back.at[n2 + kk, part], (msend, mrecv), n2 + kk, partner(j)
        )

    def note_copy(j, kk):
        n2 = regions >> (j + 1)
        return remote(
            notes[j].at[kk], back.at[n2 + kk, pl.ds(channels, rows - channels)],
            (nsend, nrecv), n2 + kk, partner(j),
        )

    def gather_x(span):
        return jnp.concatenate([feats[s, :, span] for s in range(samples)], axis=1)

    def forward_step(i, carry):
        k = regions - 1 - i
        span = span_of(k)
        color, depth = forward_tile(
            feat, channels, gather_x(span), [spacing[s, :, span] for s in range(samples)], counts[:, span],
            w1s, w2f, w3f, cols, keep_x.at[k], keep_h.at[k], keep_raw.at[k],
        )
        @pl.when(i == 0)
        def _():
            pl.semaphore_wait(barrier, vlevels + regions - 1)

        work[0][k, 0:channels] = color
        work[0][k, channels:rows] = jnp.broadcast_to(depth, (rows - channels, seg))
        for j in range(levels):
            n2 = regions >> (j + 1)

            @pl.when((k >= n2) & (k < 2 * n2))
            def _():
                color_copy(j, k - n2).start()

            @pl.when(k < n2)
            def _():
                color_copy(j, k).wait_recv()
                ahead = first(j)
                mine, other = work[j][k], got[j][k]
                mine_depth = mine[channels : channels + 1]
                other_depth = other[channels : channels + 1]
                mine_clear = jnp.where(ahead, 1.0, jnp.exp(-other_depth))
                other_clear = jnp.where(ahead, jnp.exp(-mine_depth), 1.0)
                work[j + 1][k, 0:channels] = (
                    mine_clear * mine[0:channels] + other_clear * other[0:channels]
                )
                work[j + 1][k, channels:rows] = mine[channels:rows] + other[channels:rows]

        return carry

    lax.fori_loop(0, regions, forward_step, 0)
    color = work[levels][0, 0:channels]
    pixels[...] = color
    row = lax.broadcasted_iota(jnp.int32, (rows - channels, seg), 0)
    back[0, 0:channels] = color - target[...]
    back[0, channels:rows] = jnp.where(row == 0, 1.0, 0.0)
    for acc in (acc1, acc2, acc3, bias):
        acc[...] = jnp.zeros_like(acc)
    order = sorted(range(regions), key=lambda k: (bin(k).count("1"), -k))
    if regions >= 8:
        order = [{3: 5, 5: 3}.get(k, k) for k in order]

    def tile_at(i):
        k = 0
        for at, value in enumerate(order):
            k = k + jnp.where(i == at, value, 0)
        return k

    defer = regions // 2

    def backward_step(i, carry):
        k = tile_at(i)
        for j in range(levels):
            n2 = regions >> (j + 1)

            @pl.when((k >= n2) & (k < 2 * n2))
            def _():
                misfit_copy(j, k - n2).wait_recv()
                note_copy(j, k - n2).wait_recv()

        for j in reversed(range(levels)):
            n2 = regions >> (j + 1)

            @pl.when(k < n2)
            def _():
                misfit_copy(j, k).start()

        for j in reversed(range(levels)):
            n2 = regions >> (j + 1)

            @pl.when(k < n2)
            def _():
                ahead = first(j)
                mine, other = work[j][k], got[j][k]
                misfit = back[k, 0:channels]
                state = back[k, channels:rows]
                passed, behind = state[0:1], state[1:2]
                mine_depth = mine[channels : channels + 1]
                other_depth = other[channels : channels + 1]
                hind = jnp.where(ahead, other[0:channels], mine[0:channels])
                later = passed * jnp.exp(-jnp.where(ahead, mine_depth, other_depth))
                glow = behind + later * jnp.sum(misfit * hind, axis=0, keepdims=True)
                mine_state = (jnp.where(ahead, passed, later), jnp.where(ahead, glow, behind))
                other_state = (jnp.where(ahead, later, passed), jnp.where(ahead, behind, glow))
                notes[j][k] = jnp.where(row == 0, *other_state)
                note_copy(j, k).start()
                back[k, channels:rows] = jnp.where(row == 0, *mine_state)

        span = span_of(k)
        backward_tile(
            channels, keep_raw[k], back[k, 0:channels], back[k, channels:rows],
            [spacing[s, :, span] for s in range(samples)], counts[:, span], keep_h.at[k], w3b,
            acc2, acc3, bias,
        )

        @pl.when(i < defer)
        def _():
            first_layer_tile(keep_x.at[k], keep_h.at[k], w2b, acc1, bias)

        return carry

    lax.fori_loop(0, regions, backward_step, 0)
    for j in range(levels):
        n2 = regions >> (j + 1)
        for kk in range(n2):
            color_copy(j, kk).wait_send()
            misfit_copy(j, kk).wait_send()
            note_copy(j, kk).wait_send()

    count = 2 * vlevels + 1
    early = total_stages(views, regions, grads, total, sums[0:count], (gsend, grecv))
    late = total_stages(views, regions, grads_late, total_late, sums[count:], (lsend, lrecv))
    fill(grads, (acc2, acc3), bias[hidden:, :])
    early[0]()

    def first_layer_step(i, carry):
        k = tile_at(i)
        first_layer_tile(keep_x.at[k], keep_h.at[k], w2b, acc1, bias)

        @pl.when(i == defer)
        def _():
            early[1]()

        return carry

    lax.fori_loop(defer, regions, first_layer_step, 0)
    fill(grads_late, (acc1,), bias[0:hidden, :])
    early = early[2:]
    for which in "LELLELELELL" + "EL" * (2 * len(late)):
        queue = early if which == "E" else late
        if queue:
            queue.pop(0)()


def whole_step(views, regions, feats, spacing, counts, target, rank, weights):
    samples, feat, rays = feats.shape
    channels, seg = target.shape
    hidden = weights[2].shape[0]
    levels = regions.bit_length() - 1
    vlevels = views.bit_length() - 1
    rows = channels + 8
    wide = samples * seg
    devices = views * regions
    sizes = block_counts(feat, hidden, devices)
    scratch = [
        pltpu.VMEM((hidden, 128), bf16),
        pltpu.VMEM((hidden, 3 * hidden), bf16),
        pltpu.VMEM((hidden, 2 * hidden), bf16),
        pltpu.VMEM((2 * PAD, hidden), bf16),
        pltpu.VMEM((hidden, 256), bf16),
        pltpu.VMEM((hidden, hidden), f32),
        pltpu.VMEM((regions, 2, feat, wide), bf16),
        pltpu.VMEM((regions, 2, hidden, wide), bf16),
        pltpu.VMEM((regions, PAD, wide), f32),
        pltpu.VMEM((regions, rows, seg), f32),
        pltpu.VMEM((sizes[0], 8, 128), f32),
        pltpu.VMEM((sizes[1], 8, 128), f32),
        pltpu.VMEM((feat, hidden), f32),
        pltpu.VMEM((hidden, hidden), f32),
        pltpu.VMEM((PAD, hidden), f32),
        pltpu.VMEM((3 * hidden, 128), f32),
    ]
    scratch += [pltpu.SemaphoreType.DMA((regions,))] * 6
    scratch += [pltpu.SemaphoreType.DMA((2 * (vlevels + regions - 1),))] * 4
    scratch += [pltpu.VMEM((regions >> j, rows, seg), f32) for j in range(levels + 1)]
    scratch += [pltpu.VMEM((regions >> (j + 1), rows, seg), f32) for j in range(levels)]
    scratch += [pltpu.VMEM((regions >> (j + 1), 8, seg), f32) for j in range(levels)]
    for blocks in sizes:
        for b in range(vlevels):
            scratch += [pltpu.VMEM((blocks >> (b + 1), 8, 128), f32)] * 2
        scratch.append(pltpu.VMEM((regions - 1, blocks // devices, 8, 128), f32))
    vmem = pl.BlockSpec(memory_space=pltpu.VMEM)
    return pl.pallas_call(
        functools.partial(step_kernel, views, regions),
        in_specs=[vmem] * 11,
        out_specs=[vmem] * 3,
        out_shape=[
            jax.ShapeDtypeStruct((channels, seg), f32),
            jax.ShapeDtypeStruct((sizes[0], 8, 128), f32),
            jax.ShapeDtypeStruct((sizes[1], 8, 128), f32),
        ],
        scratch_shapes=scratch,
        compiler_params=pltpu.CompilerParams(
            collective_id=0, has_side_effects=True, vmem_limit_bytes=66000000
        ),
        name="whole_step",
    )(feats, spacing, counts, target, rank, *weights)


def finish_kernel(
    feat, hidden, outs,
    pixels_in, total, late,
    pixels, first_update, first_shift, second_update, second_shift, last_update, last_shift,
):
    def scaled(value, count):
        square = jnp.sum(jnp.sum(value * value, axis=0, keepdims=True), axis=1, keepdims=True)
        return value / jnp.sqrt(square / count + epsilon)

    pixels[...] = pixels_in[...]

    def join(source, at, rows):
        halves = []
        for _ in range(0, hidden, 128):
            halves.append(source[at : at + rows // 8].reshape(rows, 128))
            at += rows // 8
        return jnp.concatenate(halves, axis=1), at

    second, at = join(total, 0, hidden)
    last, at = join(total, at, PAD)
    first, late_at = join(late, 0, feat)
    second_update[...] = scaled(second, hidden * hidden)
    first_update[...] = scaled(first, feat * hidden)
    last_update[...] = scaled(last, hidden * outs)[0:outs]
    across = hidden // 128
    rows = total[at]
    late_rows = late[late_at]
    wide = lambda rows: jnp.concatenate([rows[i : i + 1] for i in range(across)], axis=1)
    first_shift[...] = scaled(wide(late_rows), hidden)
    second_shift[...] = scaled(wide(rows), hidden)
    last_shift[...] = scaled(rows[across : across + 1], outs)[:, 0:outs]


def finish(pixels, total, late, feat, hidden, outs):
    vmem = pl.BlockSpec(memory_space=pltpu.VMEM)
    shapes = [
        pixels.shape, (feat, hidden), (1, hidden), (hidden, hidden), (1, hidden),
        (outs, hidden), (1, outs),
    ]
    return pl.pallas_call(
        functools.partial(finish_kernel, feat, hidden, outs),
        in_specs=[vmem] * 3,
        out_specs=[vmem] * len(shapes),
        out_shape=[jax.ShapeDtypeStruct(shape, f32) for shape in shapes],
        name="normalize_all",
    )(pixels, total, late)


def local(
    features, spacing, counts, depth_rank, target,
    first_weight, first_bias, second_weight, second_bias, last_weight, last_bias,
):
    regions = lax.axis_size("depth")
    views = lax.axis_size("view")
    feat, hidden = first_weight.shape
    outs = last_weight.shape[1]
    feats, gaps, live = jnp.transpose(features[0, 0], (1, 0, 2)), jnp.transpose(spacing[0], (1, 0, 2)), counts[0]
    weights = (
        first_weight, first_bias[None], second_weight, second_bias[None],
        last_weight.T, last_bias[None],
    )
    pixels, total, late = whole_step(views, regions, feats, gaps, live, target[0], depth_rank, weights)
    results = finish(pixels, total, late, feat, hidden, outs)
    return (
        results[0][None], results[1], results[2][0], results[3], results[4][0],
        results[5].T, results[6][0],
    )


def solution(mesh):
    return jax.shard_map(
        local,
        mesh=mesh,
        in_specs=(
            P("view", "depth", None, None, None),
            P("view", "depth", None, None),
            P("view", "depth", None),
            P("view", "depth"),
            P("view", None, "depth"),
            P(), P(), P(), P(), P(), P(),
        ),
        out_specs=(P("view", None, "depth"), P(), P(), P(), P(), P(), P()),
        check_vma=False,
    )
```

```python
import functools

import jax
import jax.numpy as jnp
from jax import lax
from jax.experimental import pallas as pl
from jax.experimental.pallas import tpu as pltpu
from jax.sharding import PartitionSpec as P

epsilon = 1e-05
PAD = 80
PARTS = 2
MESH = pl.DeviceIdType.MESH
f32 = jnp.float32
bf16 = jnp.bfloat16


def split(value):
    high = value.astype(bf16)
    low = (value - high.astype(f32)).astype(bf16)
    return high, low


def mm(left, right):
    return lax.dot_general(left, right, (((1,), (0,)), ((), ())), preferred_element_type=f32)


def mm_nt(left, right):
    return lax.dot_general(left, right, (((1,), (1,)), ((), ())), preferred_element_type=f32)


def opticals(raw, channels, spacing, counts, samples, rays):
    out = []
    for s in range(samples):
        logit = raw[channels : channels + 1, s * rays : (s + 1) * rays]
        density = jnp.maximum(logit, 0.0) + jnp.log1p(jnp.exp(-jnp.abs(logit)))
        length = jnp.where(s < counts, spacing[s], 0.0)
        out.append((logit, density * length, length))
    return out


def remote(src, dst, sems, slot, device):
    return pltpu.make_async_remote_copy(
        src_ref=src,
        dst_ref=dst,
        send_sem=sems[0].at[slot],
        recv_sem=sems[1].at[slot],
        device_id=device,
        device_id_type=MESH,
    )


def lanes(value):
    total = value[:, 0:128]
    for lane in range(128, value.shape[1], 128):
        total = total + value[:, lane : lane + 128]
    return total


def round_up(blocks, devices):
    return -(-blocks // devices) * devices


def block_counts(feat, hidden, views, regions):
    early = (hidden + PAD) // 8 * (hidden // 128) + 1
    return round_up(early, views * regions), round_up(feat + 1, regions)


def fill_blocks(grads, accs, rows):
    at = 0
    for acc in accs:
        blocks = acc.shape[0] // 8
        for lane in range(0, acc.shape[1], 128):
            grads[at : at + blocks] = acc[:, lane : lane + 128].reshape(blocks, 8, 128)
            at += blocks
    grads[at:] = jnp.zeros((grads.shape[0] - at, 8, 128), f32)
    added = jnp.sum(rows.T, axis=0, keepdims=True)
    for i, lane in enumerate(range(0, rows.shape[0], 128)):
        grads[at, i : i + 1, :] = added[:, lane : lane + 128]


def fill_rows(grads, acc, rows):
    feat = acc.shape[0]
    grads[feat:] = jnp.zeros((grads.shape[0] - feat,) + grads.shape[1:], f32)
    added = jnp.sum(rows.T, axis=0, keepdims=True)
    for i, lane in enumerate(range(0, acc.shape[1], 128)):
        grads[0:feat, i, :] = acc[:, lane : lane + 128]
        grads[feat, i : i + 1, :] = added[:, lane : lane + 128]


def stages(moves):
    def stage(n):
        if n > 0:
            copies, after = moves[n - 1]
            for copy in copies():
                copy.wait()
            if after is not None:
                after()
        if n < len(moves):
            for copy in moves[n][0]():
                copy.start()

    return [functools.partial(stage, n) for n in range(len(moves) + 1)]


def wide_stages(views, regions, grads, total, came, held, landing, sems):
    me = lax.axis_index("depth")
    view = lax.axis_index("view")
    pairs = views // 2
    half = grads.shape[0] // 2
    piece = half // (pairs * regions)
    core = lax.rem(view, 2)
    chip = view // 2
    partner = {"view": view + 1 - 2 * core}
    others = [(a, r) for a in range(pairs) for r in range(regions)][1:]
    others.sort(key=lambda at: -min(at[1], regions - at[1]))

    def other(a, r):
        return lax.rem(chip + a, pairs), lax.rem(me + r, regions)

    def device(a, r):
        pair, depth = other(a, r)
        return {"view": pair * 2 + core, "depth": depth}

    def swap_half():
        return [remote(grads.at[pl.ds((1 - core) * half, half)], came, sems, 0, partner)]

    def add_half():
        held[...] = grads[pl.ds(core * half, half)] + came[...]

    def scatter():
        out = []
        for n, (a, r) in enumerate(others):
            pair, depth = other(a, r)
            part = held.at[pl.ds((pair * regions + depth) * piece, piece)]
            out.append(remote(part, landing.at[n], sems, 1 + n, device(a, r)))
        return out

    def mine():
        return pl.ds(core * half + (chip * regions + me) * piece, piece)

    def add_pieces():
        value = held[pl.ds((chip * regions + me) * piece, piece)]
        for n in range(len(others)):
            value = value + landing[n]
        total[mine()] = value

    def gather():
        part = total.at[mine()]
        first = 1 + len(others)
        return [remote(part, part, sems, first + n, device(a, r)) for n, (a, r) in enumerate(others)]

    def gather_half():
        part = total.at[pl.ds(core * half, half)]
        return [remote(part, part, sems, 1 + 2 * len(others), partner)]

    return stages([(swap_half, add_half), (scatter, add_pieces), (gather, None), (gather_half, None)])


def small_stages(views, regions, grads, total, landing, slots, sems):
    me = lax.axis_index("depth")
    view = lax.axis_index("view")
    piece = grads.shape[0] // regions

    def peer(r):
        return {"depth": lax.rem(me + r, regions)}

    def scatter():
        return [
            remote(
                grads.at[pl.ds(lax.rem(me + r, regions) * piece, piece)],
                landing.at[r - 1], sems, r - 1, peer(r),
            )
            for r in range(1, regions)
        ]

    def add_depth():
        value = grads[pl.ds(me * piece, piece)]
        for r in range(1, regions):
            value = value + landing[r - 1]
        slots[view] = value

    def exchange():
        part = slots.at[view]
        return [
            remote(part, part, sems, regions - 2 + a, {"view": lax.rem(view + a, views)})
            for a in range(1, views)
        ]

    def add_view():
        value = slots[0]
        for a in range(1, views):
            value = value + slots[a]
        total[pl.ds(me * piece, piece)] = value

    def gather():
        part = total.at[pl.ds(me * piece, piece)]
        first = regions + views - 3
        return [remote(part, part, sems, first + r, peer(r)) for r in range(1, regions)]

    return stages([(scatter, add_depth), (exchange, add_view), (gather, None)])


def make_plan(regions, parts):
    levels = regions.bit_length() - 1
    ahead, back, first = 3.0 / parts, 2.7 / parts, 1.7 / parts
    load = [1.8 / parts * (1 if j < 2 else 2) for j in range(levels)]
    lag = [1.4 + 0.3 * (j > 1) for j in range(levels)]
    free = [0.0] * levels
    clock = 0.0
    came = {}
    left = [(h, k) for h in range(parts) for k in forward_order(regions)]
    done, ended, shown, told, walked, closed = [], set(), {}, [], [], []
    steps = []

    def halves(k):
        return [(j, regions >> (j + 1)) for j in range(levels) if k < regions >> (j + 1)]

    def send(j, key):
        free[j] = max(free[j], clock) + load[j]
        came[key] = free[j] + lag[j]

    while len(closed) < parts * regions:
        choices = []
        for h, k in done:
            needs = [came.get(("color", h, k + n2)) for _, n2 in halves(k)]
            if (h, k) not in ended and None not in needs:
                choices.append((max([clock] + needs), 0, h, -k, "fold", [(h, k)]))
        for h in range(parts):
            for k in range(regions):
                when = shown.get(h) if k == 0 else came.get(("misfit", h, k))
                if when is not None and (h, k) not in told:
                    choices.append((max(clock, when), 1, h, k, "tell", [(h, k)]))
        if left:
            choices.append((clock, 2, 0, 0, "forward", left[:2]))
        open_tiles = [at for at in told if at not in walked]
        if len(open_tiles) > 1:
            choices.append((clock, 3, 0, 0, "backward", open_tiles[:2]))
        open_tiles = [at for at in walked if at not in closed]
        if len(open_tiles) > 1:
            choices.append((clock, 4, 0, 0, "first", open_tiles[:2]))
        when, _, _, _, what, tiles = min(choices)
        clock = max(clock, when)
        steps.append((what, tiles))
        h, k = tiles[0]
        if what == "forward":
            clock += ahead
            done += tiles
            left = left[2:]
        elif what == "fold":
            clock += 0.1 * len(halves(k))
            ended.add((h, k))
            if k == 0:
                shown[h] = clock
            else:
                j = levels - k.bit_length()
                send(j, ("color", h, k))
        elif what == "tell":
            told.append((h, k))
            for j, n2 in reversed(halves(k)):
                clock += 0.1
                send(j, ("misfit", h, k + n2))
        elif what == "backward":
            clock += back
            walked += tiles
        else:
            clock += first
            closed += tiles
    return steps


def forward_order(regions):
    return sorted(range(regions), key=lambda k: (k == 0, k % 2 == 0, -k))


def pick(i, values):
    out = 0
    for at, value in enumerate(values):
        if value:
            out = out + jnp.where(i == at, value, 0)
    return out


def prepare(feat, w1_ref, b1_ref, w2_ref, b2_ref, w3_ref, b3_ref, w1s, w2f, w2b, w3f, w3b, cols):
    hidden = w2_ref.shape[0]
    outs = w3_ref.shape[0]
    high, low = split(w1_ref[...])
    bias = b1_ref[...]
    bias_a = bias.astype(bf16).astype(f32)
    bias_b = (bias - bias_a).astype(bf16).astype(f32)
    cols[...] = jnp.zeros_like(cols)
    cols[0:feat, :] = high.astype(f32)
    cols[feat : 2 * feat, :] = high.astype(f32)
    cols[2 * feat : 3 * feat, :] = low.astype(f32)
    cols[3 * feat : 3 * feat + 1, :] = bias_a
    cols[3 * feat + 1 : 3 * feat + 2, :] = bias_b
    cols[3 * feat + 2 : 3 * feat + 3, :] = bias - bias_a - bias_b
    cols[3 * feat + 3 : 3 * feat + 4, :] = b2_ref[...]
    cols[3 * feat + 4 : 3 * feat + 5, 0:outs] = b3_ref[...]
    turned = cols[0:128, :].T
    w1s[...] = turned.astype(bf16)
    cols[:, 0:128] = turned
    high, low = split(w2_ref[...].T)
    w2f[:, 0:hidden] = high
    w2f[:, hidden : 2 * hidden] = high
    w2f[:, 2 * hidden : 3 * hidden] = low
    high, low = split(w2_ref[...])
    w2b[:, 0:hidden] = high
    w2b[:, hidden : 2 * hidden] = low
    tall = jnp.concatenate([w3_ref[...], jnp.zeros((PAD - outs, hidden), f32)], axis=0)
    high, low = split(tall)
    w3f[0:PAD, :] = high
    w3f[PAD : 2 * PAD, :] = low
    high = high.astype(f32)
    stack = jnp.concatenate(
        [high, high, tall - high, jnp.zeros((256 - 3 * PAD, hidden), f32)], axis=0
    )
    w3b[...] = stack.T.astype(bf16)


def columns(value, n, wide):
    return value[:, n * wide : (n + 1) * wide]


def forward_tile(feat, channels, x, spacing, counts, w1s, w2f, w3f, cols, keep_x, keep_h, keep_raw):
    samples = len(spacing[0])
    rays = spacing[0][0].shape[1]
    wide = samples * rays
    xh, xl = split(x)
    rows = lax.broadcasted_iota(jnp.int32, x.shape, 0)
    ones = jnp.where(rows < 3, 1.0, 0.0).astype(bf16)
    z1 = mm(w1s[...], jnp.concatenate([xh, xl, xh, ones], axis=0))
    h1h, h1l = split(jnp.maximum(z1, 0.0))
    z2 = mm(w2f[...], jnp.concatenate([h1h, h1l, h1h], axis=0))
    z2 = z2 + cols[:, 3 * feat + 3 : 3 * feat + 4]
    h2h, h2l = split(jnp.maximum(z2, 0.0))
    both = mm(w3f[...], h2h)
    raw = both[0:PAD] + both[PAD:] + mm(w3f[0:PAD, :], h2l)
    raw = raw + cols[0:PAD, 3 * feat + 4 : 3 * feat + 5]
    out = []
    for n in range(len(spacing)):
        keep_x[n][0] = columns(xh, n, wide)
        keep_x[n][1] = columns(xl, n, wide)
        keep_h[n][0] = columns(h1h, n, wide)
        keep_h[n][1] = columns(h2h, n, wide)
        own = columns(raw, n, wide)
        keep_raw[n][...] = own
        before = None
        color = None
        for s, (_, optical, _) in enumerate(opticals(own, channels, spacing[n], counts[n], samples, rays)):
            weight = 1.0 - jnp.exp(-optical)
            if s:
                weight = jnp.exp(-before) * weight
            shade = weight * jax.nn.sigmoid(own[0:channels, s * rays : (s + 1) * rays])
            color = shade if s == 0 else color + shade
            before = optical if s == 0 else before + optical
        out.append((color, before))
    return out


def raw_grad(channels, raw, misfit, state, spacing, counts):
    samples = len(spacing)
    rays = spacing[0].shape[1]
    passed = state[0:1]
    parts = opticals(raw, channels, spacing, counts, samples, rays)
    befores, before = [], None
    for s in range(samples):
        befores.append(before)
        before = parts[s][1] if s == 0 else before + parts[s][1]
    tail = -state[1:2]
    pieces = [None] * samples
    for s in reversed(range(samples)):
        logit, optical, length = parts[s]
        gone = jnp.exp(-optical)
        ahead = 1.0 if s == 0 else jnp.exp(-befores[s])
        weight = ahead * (1.0 - gone)
        color = jax.nn.sigmoid(raw[0:channels, s * rays : (s + 1) * rays])
        weight_grad = passed * jnp.sum(misfit * color, axis=0, keepdims=True)
        optical_grad = weight_grad * (ahead * gone) + tail
        tail = tail - weight_grad * weight
        color_grad = (weight * passed) * misfit * (color * (1.0 - color))
        logit_grad = optical_grad * length * jax.nn.sigmoid(logit)
        row = lax.broadcasted_iota(jnp.int32, (PAD - channels, rays), 0)
        rest = jnp.where(row == 0, jnp.broadcast_to(logit_grad, row.shape), 0.0)
        pieces[s] = jnp.concatenate([color_grad, rest], axis=0)
    return pieces


def backward_tile(channels, raws, misfits, states, spacing, counts, keep_h, w3b, acc2, acc3, bias):
    hidden = w3b.shape[0]
    pieces = []
    for at in zip(raws, misfits, states, spacing, counts):
        pieces += raw_grad(channels, *at)
    draw = jnp.concatenate(pieces, axis=1)
    bias[2 * hidden : 2 * hidden + PAD, :] += lanes(draw)
    dh, dl = split(draw)
    h2h = jnp.concatenate([keep[1] for keep in keep_h], axis=1)
    both = mm_nt(jnp.concatenate([dh, dl], axis=0), h2h)
    acc3[...] += both[0:PAD] + both[PAD:]
    zero = jnp.zeros((256 - 3 * PAD, draw.shape[1]), bf16)
    dh2 = mm(w3b[...], jnp.concatenate([dh, dl, dh, zero], axis=0))
    dz2 = jnp.where(h2h > 0, dh2, 0.0)
    bias[hidden : 2 * hidden, :] += lanes(dz2)
    zh = dz2.astype(bf16)
    h1h = jnp.concatenate([keep[0] for keep in keep_h], axis=1)
    acc2[...] += mm_nt(h1h, zh)
    wide = zh.shape[1] // len(keep_h)
    for n, keep in enumerate(keep_h):
        keep[1] = columns(zh, n, wide)


def first_layer_tile(keep_x, keep_h, w2b, acc1, bias):
    hidden = w2b.shape[0]
    h1h = jnp.concatenate([keep[0] for keep in keep_h], axis=1)
    zh = jnp.concatenate([keep[1] for keep in keep_h], axis=1)
    feat = keep_x[0].shape[1]
    dh1 = mm(w2b[...], jnp.concatenate([zh, zh], axis=0))
    dz1 = jnp.where(h1h > 0, dh1, 0.0)
    bias[0:hidden, :] += lanes(dz1)
    x = [jnp.concatenate([keep[i] for keep in keep_x], axis=1) for i in (0, 1)]
    both = mm_nt(jnp.concatenate(x, axis=0), dz1.astype(bf16))
    acc1[...] += both[0:feat] + both[feat:]


def step_kernel(
    views, regions,
    feats, spacing, counts, target, rank_ref, w1, b1, w2, b2, w3, b3,
    pixels, total, total_late,
    w1s, w2f, w2b, w3f, w3b, cols, keep_x, keep_h, keep_raw, back, grads, grads_late,
    acc1, acc2, acc3, bias, fsend, frecv, msend, mrecv, nsend, nrecv, gsend, grecv, lsend, lrecv,
    *scratch,
):
    samples, feat, rays = feats.shape
    channels, seg = target.shape
    levels = regions.bit_length() - 1
    rows = back.shape[1]
    hidden = w2.shape[0]
    me = lax.axis_index("depth")
    view = lax.axis_index("view")
    work = scratch[0 : levels + 1]
    got = scratch[levels + 1 : 2 * levels + 1]
    notes = scratch[2 * levels + 1 : 3 * levels + 1]
    sums = scratch[3 * levels + 1 :]

    def bit_of(value, b):
        return lax.rem(value // (1 << b), 2)

    def partner(b):
        return {"depth": me + (1 - 2 * bit_of(me, b)) * (1 << b)}

    barrier = pltpu.get_barrier_semaphore()
    greeted = [(a, r) for a in range(views) for r in range(regions) if r == 0 or a % 2 == 0][1:]
    for a, r in greeted:
        where = {"view": lax.rem(view + a, views), "depth": lax.rem(me + r, regions)}
        pl.semaphore_signal(barrier, inc=1, device_id=where, device_id_type=MESH)

    prepare(feat, w1, b1, w2, b2, w3, b3, w1s, w2f, w2b, w3f, w3b, cols)

    parts = PARTS
    wide = seg // parts

    def span_of(h, k):
        where = 0
        for b in range(levels):
            where = where + lax.rem(bit_of(me, b) + bit_of(k, levels - 1 - b), 2) * (1 << b)
        return pl.ds(pl.multiple_of(where * seg + h * wide, wide), wide)

    rank = rank_ref[0:1, 0:1]
    row = lax.broadcasted_iota(jnp.int32, (rows - channels, wide), 0)

    def first(b):
        return lax.rem(lax.div(rank, jnp.full_like(rank, 1 << b)), jnp.full_like(rank, 2)) == 0

    def halves(k):
        return [(j, regions >> (j + 1)) for j in range(levels) if k < regions >> (j + 1)]

    def color_copy(j, h, kk):
        n2 = regions >> (j + 1)
        return remote(
            work[j].at[h * 2 * n2 + n2 + kk], got[j].at[h * n2 + kk],
            (fsend, frecv), h * regions + n2 + kk, partner(j),
        )

    def misfit_copy(j, h, kk):
        n2 = regions >> (j + 1)
        part = pl.ds(0, channels)
        return remote(
            back.at[h * regions + kk, part], back.at[h * regions + n2 + kk, part],
            (msend, mrecv), h * regions + n2 + kk, partner(j),
        )

    def note_copy(j, h, kk):
        n2 = regions >> (j + 1)
        return remote(
            notes[j].at[h * n2 + kk], back.at[h * regions + n2 + kk, pl.ds(channels, rows - channels)],
            (nsend, nrecv), h * regions + n2 + kk, partner(j),
        )

    def gather_x(span):
        return jnp.concatenate([feats[s, :, span] for s in range(samples)], axis=1)

    def fold(h, k):
        for j, n2 in halves(k):
            color_copy(j, h, k).wait_recv()
            ahead = first(j)
            mine, other = work[j][h * 2 * n2 + k], got[j][h * n2 + k]
            mine_depth = mine[channels : channels + 1]
            other_depth = other[channels : channels + 1]
            mine_clear = jnp.where(ahead, 1.0, jnp.exp(-other_depth))
            other_clear = jnp.where(ahead, jnp.exp(-mine_depth), 1.0)
            at = h * n2 + k
            work[j + 1][at, 0:channels] = mine_clear * mine[0:channels] + other_clear * other[0:channels]
            work[j + 1][at, channels:rows] = mine[channels:rows] + other[channels:rows]
        if k:
            j = levels - k.bit_length()
            color_copy(j, h, k - (regions >> (j + 1))).start()

    def tell(h, k):
        at = h * regions + k
        if k == 0:
            span = pl.ds(h * wide, wide)
            color = work[levels][h, 0:channels]
            pixels[:, span] = color
            back[at, 0:channels] = color - target[:, span]
            back[at, channels:rows] = jnp.where(row == 0, 1.0, 0.0)
        else:
            j = levels - k.bit_length()
            misfit_copy(j, h, k - (regions >> (j + 1))).wait_recv()
        for j, n2 in reversed(halves(k)):
            misfit_copy(j, h, k).start()
        if k:
            j = levels - k.bit_length()
            note_copy(j, h, k - (regions >> (j + 1))).wait_recv()
        for j, n2 in reversed(halves(k)):
            ahead = first(j)
            mine, other = work[j][h * 2 * n2 + k], got[j][h * n2 + k]
            misfit = back[at, 0:channels]
            state = back[at, channels:rows]
            passed, behind = state[0:1], state[1:2]
            mine_depth = mine[channels : channels + 1]
            other_depth = other[channels : channels + 1]
            hind = jnp.where(ahead, other[0:channels], mine[0:channels])
            later = passed * jnp.exp(-jnp.where(ahead, mine_depth, other_depth))
            glow = behind + later * jnp.sum(misfit * hind, axis=0, keepdims=True)
            mine_state = (jnp.where(ahead, passed, later), jnp.where(ahead, glow, behind))
            other_state = (jnp.where(ahead, later, passed), jnp.where(ahead, behind, glow))
            notes[j][h * n2 + k] = jnp.where(row == 0, *other_state)
            note_copy(j, h, k).start()
            back[at, channels:rows] = jnp.where(row == 0, *mine_state)

    plan = make_plan(regions, parts)
    half = regions // 2
    tiles = [at for what, at in plan if what == "forward"]
    passes, events = [], {}
    ready = 0
    for what, at in plan:
        if what == "forward":
            ready += 1
        elif what in ("backward", "first"):
            passes.append((what, at))
        elif at[0][1] < half:
            key = ("ahead", ready - 1) if ready < len(tiles) else ("back", len(passes))
            events.setdefault(key, []).append((fold if what == "fold" else tell,) + at[0])
    last = max(n for n, at in enumerate(passes) if at[0] == "backward")
    passes, lasts = passes[: last + 1], [at for _, at in passes[last + 1 :]]

    def pick_tiles(i, table):
        out = []
        for n in range(2):
            h = pick(i, [at[n][0] for at in table])
            k = pick(i, [at[n][1] for at in table])
            out.append((h, k, h * regions + k))
        return out

    def lengths(span):
        return [spacing[s, :, span] for s in range(samples)]

    def run_events(name, i):
        for (kind, at), calls in events.items():
            if kind == name:

                @pl.when(i == at)
                def _():
                    for call, h, k in calls:
                        call(h, k)

    def forward_step(i, carry):
        pair = pick_tiles(i, tiles)
        spans = [span_of(h, k) for h, k, _ in pair]
        results = forward_tile(
            feat, channels, jnp.concatenate([gather_x(span) for span in spans], axis=1),
            [lengths(span) for span in spans], [counts[:, span] for span in spans], w1s, w2f, w3f, cols,
            [keep_x.at[at] for _, _, at in pair], [keep_h.at[at] for _, _, at in pair],
            [keep_raw.at[at] for _, _, at in pair],
        )
        for (_, _, at), (color, depth) in zip(pair, results):
            work[0][at, 0:channels] = color
            work[0][at, channels:rows] = jnp.broadcast_to(depth, (rows - channels, wide))

        @pl.when(i == 0)
        def _():
            pl.semaphore_wait(barrier, len(greeted))

        for h, k, _ in pair:

            @pl.when(k >= half)
            def _():
                color_copy(0, h, k - half).start()

        run_events("ahead", i)
        return carry

    lax.fori_loop(0, len(tiles), forward_step, 0)
    for acc in (acc1, acc2, acc3, bias):
        acc[...] = jnp.zeros_like(acc)

    def backward_step(i, carry):
        run_events("back", i)
        pair = pick_tiles(i, [at[1] for at in passes])
        turn = pick(i, [int(at[0] == "backward") for at in passes])
        for h, k, _ in pair:

            @pl.when((turn == 1) & (k >= half))
            def _():
                misfit_copy(0, h, k - half).wait_recv()
                note_copy(0, h, k - half).wait_recv()

        @pl.when(turn == 1)
        def _():
            spans = [span_of(h, k) for h, k, _ in pair]
            backward_tile(
                channels, [keep_raw.at[at] for _, _, at in pair],
                [back[at, 0:channels] for _, _, at in pair], [back[at, channels:rows] for _, _, at in pair],
                [lengths(span) for span in spans], [counts[:, span] for span in spans],
                [keep_h.at[at] for _, _, at in pair], w3b, acc2, acc3, bias,
            )

        @pl.when(turn == 0)
        def _():
            first_layer_tile(
                [keep_x.at[at] for _, _, at in pair], [keep_h.at[at] for _, _, at in pair], w2b, acc1, bias
            )

        return carry

    lax.fori_loop(0, len(passes), backward_step, 0)
    for h in range(parts):
        for j in range(levels):
            for kk in range(regions >> (j + 1)):
                color_copy(j, h, kk).wait_send()
                misfit_copy(j, h, kk).wait_send()
                note_copy(j, h, kk).wait_send()

    early = wide_stages(views, regions, grads, total, *sums[0:3], (gsend, grecv))
    late = small_stages(views, regions, grads_late, total_late, *sums[3:5], (lsend, lrecv))
    fill_blocks(grads, (acc2, acc3), bias[hidden:, :])
    early[0]()

    def first_layer_step(i, carry):
        pair = pick_tiles(i, lasts)
        first_layer_tile(
            [keep_x.at[at] for _, _, at in pair], [keep_h.at[at] for _, _, at in pair], w2b, acc1, bias
        )

        @pl.when(i == min(1, len(lasts) - 1))
        def _():
            early[1]()

        return carry

    lax.fori_loop(0, len(lasts), first_layer_step, 0)
    fill_rows(grads_late, acc1, bias[0:hidden, :])
    early = early[2:]
    for which in "LLELLEE":
        (early if which == "E" else late).pop(0)()


def whole_step(views, regions, feats, spacing, counts, target, rank, weights):
    samples, feat, rays = feats.shape
    channels, seg = target.shape
    hidden = weights[2].shape[0]
    levels = regions.bit_length() - 1
    rows = channels + 8
    parts = PARTS
    tiles = parts * regions
    seg = seg // parts
    wide = samples * seg
    across = hidden // 128
    pairs = views // 2 * regions
    sizes = block_counts(feat, hidden, views, regions)
    scratch = [
        pltpu.VMEM((hidden, 128), bf16),
        pltpu.VMEM((hidden, 3 * hidden), bf16),
        pltpu.VMEM((hidden, 2 * hidden), bf16),
        pltpu.VMEM((2 * PAD, hidden), bf16),
        pltpu.VMEM((hidden, 256), bf16),
        pltpu.VMEM((hidden, hidden), f32),
        pltpu.VMEM((tiles, 2, feat, wide), bf16),
        pltpu.VMEM((tiles, 2, hidden, wide), bf16),
        pltpu.VMEM((tiles, PAD, wide), f32),
        pltpu.VMEM((tiles, rows, seg), f32),
        pltpu.VMEM((sizes[0], 8, 128), f32),
        pltpu.VMEM((sizes[1], across, 128), f32),
        pltpu.VMEM((feat, hidden), f32),
        pltpu.VMEM((hidden, hidden), f32),
        pltpu.VMEM((PAD, hidden), f32),
        pltpu.VMEM((3 * hidden, 128), f32),
    ]
    scratch += [pltpu.SemaphoreType.DMA((tiles,))] * 6
    scratch += [pltpu.SemaphoreType.DMA((2 * pairs,))] * 2
    scratch += [pltpu.SemaphoreType.DMA((2 * regions + views - 3,))] * 2
    scratch += [pltpu.VMEM((tiles >> j, rows, seg), f32) for j in range(levels + 1)]
    scratch += [pltpu.VMEM((tiles >> (j + 1), rows, seg), f32) for j in range(levels)]
    scratch += [pltpu.VMEM((tiles >> (j + 1), 8, seg), f32) for j in range(levels)]
    half = sizes[0] // 2
    scratch += [pltpu.VMEM((half, 8, 128), f32)] * 2
    scratch.append(pltpu.VMEM((pairs - 1, half // pairs, 8, 128), f32))
    part = sizes[1] // regions
    scratch.append(pltpu.VMEM((regions - 1, part, across, 128), f32))
    scratch.append(pltpu.VMEM((views, part, across, 128), f32))
    vmem = pl.BlockSpec(memory_space=pltpu.VMEM)
    return pl.pallas_call(
        functools.partial(step_kernel, views, regions),
        in_specs=[vmem] * 11,
        out_specs=[vmem] * 3,
        out_shape=[
            jax.ShapeDtypeStruct(target.shape, f32),
            jax.ShapeDtypeStruct((sizes[0], 8, 128), f32),
            jax.ShapeDtypeStruct((sizes[1], across, 128), f32),
        ],
        scratch_shapes=scratch,
        compiler_params=pltpu.CompilerParams(
            collective_id=0, has_side_effects=True, vmem_limit_bytes=66000000
        ),
        name="whole_step",
    )(feats, spacing, counts, target, rank, *weights)


def finish_kernel(
    feat, hidden, outs,
    pixels_in, total, late,
    pixels, first_update, first_shift, second_update, second_shift, last_update, last_shift,
):
    def scaled(value, count):
        square = jnp.sum(jnp.sum(value * value, axis=0, keepdims=True), axis=1, keepdims=True)
        return value / jnp.sqrt(square / count + epsilon)

    pixels[...] = pixels_in[...]

    def join(source, at, rows):
        halves = []
        for _ in range(0, hidden, 128):
            halves.append(source[at : at + rows // 8].reshape(rows, 128))
            at += rows // 8
        return jnp.concatenate(halves, axis=1), at

    second, at = join(total, 0, hidden)
    last, at = join(total, at, PAD)
    across = hidden // 128
    first = jnp.concatenate([late[0:feat, i, :] for i in range(across)], axis=1)
    second_update[...] = scaled(second, hidden * hidden)
    first_update[...] = scaled(first, feat * hidden)
    last_update[...] = scaled(last, hidden * outs)[0:outs]
    rows = total[at]
    late_rows = late[feat]
    wide = lambda rows: jnp.concatenate([rows[i : i + 1] for i in range(across)], axis=1)
    first_shift[...] = scaled(wide(late_rows), hidden)
    second_shift[...] = scaled(wide(rows), hidden)
    last_shift[...] = scaled(rows[across : across + 1], outs)[:, 0:outs]


def finish(pixels, total, late, feat, hidden, outs):
    vmem = pl.BlockSpec(memory_space=pltpu.VMEM)
    shapes = [
        pixels.shape, (feat, hidden), (1, hidden), (hidden, hidden), (1, hidden),
        (outs, hidden), (1, outs),
    ]
    return pl.pallas_call(
        functools.partial(finish_kernel, feat, hidden, outs),
        in_specs=[vmem] * 3,
        out_specs=[vmem] * len(shapes),
        out_shape=[jax.ShapeDtypeStruct(shape, f32) for shape in shapes],
        name="normalize_all",
    )(pixels, total, late)


def local(
    features, spacing, counts, depth_rank, target,
    first_weight, first_bias, second_weight, second_bias, last_weight, last_bias,
):
    regions = lax.axis_size("depth")
    views = lax.axis_size("view")
    feat, hidden = first_weight.shape
    outs = last_weight.shape[1]
    feats, gaps, live = jnp.transpose(features[0, 0], (1, 0, 2)), jnp.transpose(spacing[0], (1, 0, 2)), counts[0]
    weights = (
        first_weight, first_bias[None], second_weight, second_bias[None],
        last_weight.T, last_bias[None],
    )
    pixels, total, late = whole_step(views, regions, feats, gaps, live, target[0], depth_rank, weights)
    results = finish(pixels, total, late, feat, hidden, outs)
    return (
        results[0][None], results[1], results[2][0], results[3], results[4][0],
        results[5].T, results[6][0],
    )


def solution(mesh):
    return jax.shard_map(
        local,
        mesh=mesh,
        in_specs=(
            P("view", "depth", None, None, None),
            P("view", "depth", None, None),
            P("view", "depth", None),
            P("view", "depth"),
            P("view", None, "depth"),
            P(), P(), P(), P(), P(), P(),
        ),
        out_specs=(P("view", None, "depth"), P(), P(), P(), P(), P(), P()),
        check_vma=False,
    )
```

```python
import functools

import jax
import jax.numpy as jnp
from jax import lax
from jax.experimental import pallas as pl
from jax.experimental.pallas import tpu as pltpu
from jax.sharding import PartitionSpec as P

epsilon = 1e-05
PAD = 80
PARTS = 2
MESH = pl.DeviceIdType.MESH
f32 = jnp.float32
bf16 = jnp.bfloat16


def split(value):
    high = value.astype(bf16)
    low = (value - high.astype(f32)).astype(bf16)
    return high, low


def mm(left, right):
    return lax.dot_general(left, right, (((1,), (0,)), ((), ())), preferred_element_type=f32)


def mm_nt(left, right):
    return lax.dot_general(left, right, (((1,), (1,)), ((), ())), preferred_element_type=f32)


def opticals(raw, channels, spacing, counts, samples, rays):
    out = []
    for s in range(samples):
        logit = raw[channels : channels + 1, s * rays : (s + 1) * rays]
        density = jnp.maximum(logit, 0.0) + jnp.log1p(jnp.exp(-jnp.abs(logit)))
        length = jnp.where(s < counts, spacing[s], 0.0)
        out.append((logit, density * length, length))
    return out


def remote(src, dst, sems, slot, device):
    return pltpu.make_async_remote_copy(
        src_ref=src,
        dst_ref=dst,
        send_sem=sems[0].at[slot],
        recv_sem=sems[1].at[slot],
        device_id=device,
        device_id_type=MESH,
    )


def lanes(value):
    total = value[:, 0:128]
    for lane in range(128, value.shape[1], 128):
        total = total + value[:, lane : lane + 128]
    return total


def round_up(blocks, devices):
    return -(-blocks // devices) * devices


def block_counts(feat, hidden, views, regions):
    early = (hidden + PAD) // 8 * (hidden // 128) + 1
    return round_up(early, views * regions), round_up(feat + 1, regions)


def fill_blocks(grads, acc2, acc3, bias):
    hidden = acc2.shape[1]
    at = 0
    for acc, blocks in ((acc2, hidden // 8), (acc3, acc3.shape[0] // 8)):
        for lane in range(0, hidden, 128):
            grads[at : at + blocks] = acc[0 : blocks * 8, lane : lane + 128].reshape(blocks, 8, 128)
            at += blocks
    grads[at:] = jnp.zeros((grads.shape[0] - at, 8, 128), f32)
    for i, lane in enumerate(range(0, hidden, 128)):
        grads[at, i : i + 1, :] = acc2[hidden : hidden + 1, lane : lane + 128]
    tall = jnp.concatenate([bias[...], jnp.zeros((128 - bias.shape[0], 128), f32)], axis=0)
    grads[at, hidden // 128 : hidden // 128 + 1, :] = jnp.sum(tall.T, axis=0, keepdims=True)


def fill_rows(grads, acc, feat):
    grads[feat:] = jnp.zeros((grads.shape[0] - feat,) + grads.shape[1:], f32)
    for i, lane in enumerate(range(0, acc.shape[1], 128)):
        part = slice(lane, lane + 128)
        grads[0:feat, i, :] = acc[0:feat, part] + acc[feat : 2 * feat, part]
        grads[feat, i : i + 1, :] = acc[2 * feat : 2 * feat + 1, part]


def stages(moves):
    def stage(n):
        if n > 0:
            copies, after = moves[n - 1]
            for copy in copies():
                copy.wait()
            if after is not None:
                after()
        if n < len(moves):
            for copy in moves[n][0]():
                copy.start()

    return [functools.partial(stage, n) for n in range(len(moves) + 1)]


def wide_stages(views, regions, grads, total, came, held, landing, sems):
    me = lax.axis_index("depth")
    view = lax.axis_index("view")
    pairs = views // 2
    half = grads.shape[0] // 2
    piece = half // (pairs * regions)
    core = lax.rem(view, 2)
    chip = view // 2
    partner = {"view": view + 1 - 2 * core}
    others = [(a, r) for a in range(pairs) for r in range(regions)][1:]

    def other(a, r):
        return lax.rem(chip + a, pairs), lax.rem(me + r, regions)

    def device(a, r):
        pair, depth = other(a, r)
        return {"view": pair * 2 + core, "depth": depth}

    def swap_half():
        return [remote(grads.at[pl.ds((1 - core) * half, half)], came, sems, 0, partner)]

    def add_half():
        held[...] = grads[pl.ds(core * half, half)] + came[...]

    def scatter():
        out = []
        for n, (a, r) in enumerate(others):
            pair, depth = other(a, r)
            part = held.at[pl.ds((pair * regions + depth) * piece, piece)]
            out.append(remote(part, landing.at[n], sems, 1 + n, device(a, r)))
        return out

    def mine():
        return pl.ds(core * half + (chip * regions + me) * piece, piece)

    def add_pieces():
        value = held[pl.ds((chip * regions + me) * piece, piece)]
        for n in range(len(others)):
            value = value + landing[n]
        total[mine()] = value

    def gather():
        part = total.at[mine()]
        first = 1 + len(others)
        return [remote(part, part, sems, first + n, device(a, r)) for n, (a, r) in enumerate(others)]

    def gather_half():
        part = total.at[pl.ds(core * half, half)]
        return [remote(part, part, sems, 1 + 2 * len(others), partner)]

    return stages([(swap_half, add_half), (scatter, add_pieces), (gather, None), (gather_half, None)])


def small_stages(views, regions, grads, total, landing, slots, sems):
    me = lax.axis_index("depth")
    view = lax.axis_index("view")
    piece = grads.shape[0] // regions

    def peer(r):
        return {"depth": lax.rem(me + r, regions)}

    def scatter():
        return [
            remote(
                grads.at[pl.ds(lax.rem(me + r, regions) * piece, piece)],
                landing.at[r - 1], sems, r - 1, peer(r),
            )
            for r in range(1, regions)
        ]

    def add_depth():
        value = grads[pl.ds(me * piece, piece)]
        for r in range(1, regions):
            value = value + landing[r - 1]
        slots[view] = value

    def exchange():
        part = slots.at[view]
        return [
            remote(part, part, sems, regions - 2 + a, {"view": lax.rem(view + a, views)})
            for a in range(1, views)
        ]

    def add_view():
        value = slots[0]
        for a in range(1, views):
            value = value + slots[a]
        total[pl.ds(me * piece, piece)] = value

    def gather():
        part = total.at[pl.ds(me * piece, piece)]
        first = regions + views - 3
        return [remote(part, part, sems, first + r, peer(r)) for r in range(1, regions)]

    return stages([(scatter, add_depth), (exchange, add_view), (gather, None)])


def make_plan(regions, parts):
    levels = regions.bit_length() - 1
    ahead, back, first = 1.5, 1.35, 0.85
    group = parts
    load = [1.8 / parts * (1 if j < 2 else 2) for j in range(levels)]
    lag = [1.7 + 0.3 * (j > 1) for j in range(levels)]
    free = [0.0] * levels
    clock = 0.0
    came = {}
    left = [(h, k) for h in range(parts) for k in forward_order(regions)]
    done, ended, shown, told, walked, closed = [], set(), {}, [], [], []
    steps = []

    def halves(k):
        return [(j, regions >> (j + 1)) for j in range(levels) if k < regions >> (j + 1)]

    def send(j, key):
        free[j] = max(free[j], clock) + load[j]
        came[key] = free[j] + lag[j]

    while len(closed) < parts * regions:
        choices = []
        for h, k in done:
            needs = [came.get(("color", h, k + n2)) for _, n2 in halves(k)]
            if (h, k) not in ended and None not in needs:
                choices.append((max([clock] + needs), 0, h, -k, "fold", [(h, k)]))
        for h in range(parts):
            for k in range(regions):
                when = shown.get(h) if k == 0 else came.get(("misfit", h, k))
                if when is not None and (h, k) not in told:
                    choices.append((max(clock, when), 1, h, k, "tell", [(h, k)]))
        if left:
            choices.append((clock, 2, 0, 0, "forward", left[:group]))
        open_tiles = [at for at in told if at not in walked]
        if len(open_tiles) >= group:
            choices.append((clock, 3, 0, 0, "backward", open_tiles[:group]))
        open_tiles = [at for at in walked if at not in closed]
        if len(open_tiles) >= group:
            choices.append((clock, 4, 0, 0, "first", open_tiles[:group]))
        when, _, _, _, what, tiles = min(choices)
        clock = max(clock, when)
        steps.append((what, tiles))
        h, k = tiles[0]
        if what == "forward":
            clock += ahead
            done += tiles
            left = left[group:]
        elif what == "fold":
            clock += 0.1 * len(halves(k))
            ended.add((h, k))
            if k == 0:
                shown[h] = clock
            else:
                j = levels - k.bit_length()
                send(j, ("color", h, k))
        elif what == "tell":
            told.append((h, k))
            for j, n2 in reversed(halves(k)):
                clock += 0.1
                send(j, ("misfit", h, k + n2))
        elif what == "backward":
            clock += back
            walked += tiles
        else:
            clock += first
            closed += tiles
    return steps


def forward_order(regions):
    return sorted(range(regions), key=lambda k: (k == 0, k % 2 == 0, -k))


def pick(i, values):
    out = 0
    for at, value in enumerate(values):
        if value:
            out = out + jnp.where(i == at, value, 0)
    return out


def prepare(feat, w1_ref, b1_ref, w2_ref, b2_ref, w3_ref, b3_ref, w1s, w2f, w2b, w3f, w3b, cols):
    hidden = w2_ref.shape[0]
    outs = w3_ref.shape[0]
    high, low = split(w1_ref[...])
    bias = b1_ref[...]
    bias_a = bias.astype(bf16).astype(f32)
    bias_b = (bias - bias_a).astype(bf16).astype(f32)
    cols[...] = jnp.zeros_like(cols)
    cols[0:feat, :] = high.astype(f32)
    cols[feat : 2 * feat, :] = high.astype(f32)
    cols[2 * feat : 3 * feat, :] = low.astype(f32)
    cols[3 * feat : 3 * feat + 1, :] = bias_a
    cols[3 * feat + 1 : 3 * feat + 2, :] = bias_b
    cols[3 * feat + 2 : 3 * feat + 3, :] = bias - bias_a - bias_b
    cols[3 * feat + 3 : 3 * feat + 4, :] = b2_ref[...]
    cols[3 * feat + 4 : 3 * feat + 5, 0:outs] = b3_ref[...]
    turned = cols[0:128, :].T
    w1s[...] = turned.astype(bf16)
    cols[:, 0:128] = turned
    high, low = split(w2_ref[...].T)
    w2f[:, 0:hidden] = high
    w2f[:, hidden : 2 * hidden] = high
    w2f[:, 2 * hidden : 3 * hidden] = low
    high, low = split(w2_ref[...])
    w2b[:, 0:hidden] = high
    w2b[:, hidden : 2 * hidden] = low
    tall = jnp.concatenate([w3_ref[...], jnp.zeros((PAD - outs, hidden), f32)], axis=0)
    high, low = split(tall)
    w3f[0:PAD, :] = high
    w3f[PAD : 2 * PAD, :] = low
    high = high.astype(f32)
    stack = jnp.concatenate(
        [high, high, tall - high, jnp.zeros((256 - 3 * PAD, hidden), f32)], axis=0
    )
    w3b[...] = stack.T.astype(bf16)


def columns(value, n, wide):
    return value[:, n * wide : (n + 1) * wide]


def forward_tile(feat, channels, x, spacing, counts, w1s, w2f, w3f, cols, keep_x, keep_h, keep_raw):
    samples = len(spacing[0])
    rays = spacing[0][0].shape[1]
    wide = samples * rays
    xh, xl = split(x)
    rows = lax.broadcasted_iota(jnp.int32, x.shape, 0)
    ones = jnp.where(rows < 3, 1.0, 0.0).astype(bf16)
    z1 = mm(w1s[...], jnp.concatenate([xh, xl, xh, ones], axis=0))
    h1h, h1l = split(jnp.maximum(z1, 0.0))
    z2 = mm(w2f[...], jnp.concatenate([h1h, h1l, h1h], axis=0))
    z2 = z2 + cols[:, 3 * feat + 3 : 3 * feat + 4]
    h2h, h2l = split(jnp.maximum(z2, 0.0))
    both = mm(w3f[...], h2h)
    raw = both[0:PAD] + both[PAD:] + mm(w3f[0:PAD, :], h2l)
    raw = raw + cols[0:PAD, 3 * feat + 4 : 3 * feat + 5]
    out = []
    for n in range(len(spacing)):
        keep_x[n][0] = columns(xh, n, wide)
        keep_x[n][1] = columns(xl, n, wide)
        keep_h[n][0] = columns(h1h, n, wide)
        keep_h[n][1] = columns(h2h, n, wide)
        own = columns(raw, n, wide)
        shown = jax.nn.sigmoid(own[0:channels])
        keep_raw[n][0:channels] = shown
        keep_raw[n][channels:PAD] = own[channels:PAD]
        before = None
        color = None
        for s, (_, optical, _) in enumerate(opticals(own, channels, spacing[n], counts[n], samples, rays)):
            weight = 1.0 - jnp.exp(-optical)
            if s:
                weight = jnp.exp(-before) * weight
            shade = weight * shown[:, s * rays : (s + 1) * rays]
            color = shade if s == 0 else color + shade
            before = optical if s == 0 else before + optical
        out.append((color, before))
    return out


def raw_grad(channels, raw, misfit, state, spacing, counts):
    samples = len(spacing)
    rays = spacing[0].shape[1]
    passed = state[0:1]
    parts = opticals(raw, channels, spacing, counts, samples, rays)
    befores, before = [], None
    for s in range(samples):
        befores.append(before)
        before = parts[s][1] if s == 0 else before + parts[s][1]
    tail = -state[1:2]
    pieces = [None] * samples
    for s in reversed(range(samples)):
        logit, optical, length = parts[s]
        gone = jnp.exp(-optical)
        ahead = 1.0 if s == 0 else jnp.exp(-befores[s])
        weight = ahead * (1.0 - gone)
        color = raw[0:channels, s * rays : (s + 1) * rays]
        weight_grad = passed * jnp.sum(misfit * color, axis=0, keepdims=True)
        optical_grad = weight_grad * (ahead * gone) + tail
        tail = tail - weight_grad * weight
        color_grad = (weight * passed) * misfit * (color * (1.0 - color))
        logit_grad = optical_grad * length * jax.nn.sigmoid(logit)
        row = lax.broadcasted_iota(jnp.int32, (PAD - channels, rays), 0)
        rest = jnp.where(row == 0, jnp.broadcast_to(logit_grad, row.shape), 0.0)
        pieces[s] = jnp.concatenate([color_grad, rest], axis=0)
    return pieces


def backward_tile(channels, raws, misfits, states, spacing, counts, keep_h, w3b, acc2, acc3, bias):
    pieces = []
    for at in zip(raws, misfits, states, spacing, counts):
        pieces += raw_grad(channels, *at)
    draw = jnp.concatenate(pieces, axis=1)
    bias[0:PAD, :] += lanes(draw)
    dh, dl = split(draw)
    h2h = jnp.concatenate([keep[1] for keep in keep_h], axis=1)
    both = mm_nt(jnp.concatenate([dh, dl], axis=0), h2h)
    acc3[...] += both[0:PAD] + both[PAD:]
    zero = jnp.zeros((256 - 3 * PAD, draw.shape[1]), bf16)
    dh2 = mm(w3b[...], jnp.concatenate([dh, dl, dh, zero], axis=0))
    zh = jnp.where(h2h > 0, dh2.astype(bf16), jnp.zeros_like(h2h))
    h1h = jnp.concatenate([keep[0] for keep in keep_h], axis=1)
    acc2[...] += mm_nt(jnp.concatenate([h1h, jnp.ones((16, h1h.shape[1]), bf16)], axis=0), zh)
    wide = zh.shape[1] // len(keep_h)
    for n, keep in enumerate(keep_h):
        keep[1] = columns(zh, n, wide)


def first_layer_tile(keep_x, keep_h, w2b, acc1):
    h1h = jnp.concatenate([keep[0] for keep in keep_h], axis=1)
    zh = jnp.concatenate([keep[1] for keep in keep_h], axis=1)
    dh1 = mm(w2b[...], jnp.concatenate([zh, zh], axis=0))
    zh = jnp.where(h1h > 0, dh1.astype(bf16), jnp.zeros_like(h1h))
    x = [jnp.concatenate([keep[i] for keep in keep_x], axis=1) for i in (0, 1)]
    x.append(jnp.ones((16, zh.shape[1]), bf16))
    acc1[...] += mm_nt(jnp.concatenate(x, axis=0), zh)


def step_kernel(
    views, regions,
    feats_in, spacing_in, counts_in, target_in, rank_ref, w1_in, b1_in, w2_in, b2_in, w3_in, b3_in,
    pixels, total, total_late,
    feats, spacing, counts, target, w1, b1, w2, b2, w3, b3, load_sem,
    w1s, w2f, w2b, w3f, w3b, cols, keep_x, keep_h, keep_raw, back, grads, grads_late,
    acc1, acc2, acc3, bias, fsend, frecv, msend, mrecv, nsend, nrecv, gsend, grecv, lsend, lrecv,
    *scratch,
):
    samples, feat, rays = feats.shape
    channels, seg = target.shape
    levels = regions.bit_length() - 1
    rows = back.shape[1]
    hidden = w2.shape[0]
    me = lax.axis_index("depth")
    view = lax.axis_index("view")
    work = scratch[0 : levels + 1]
    got = scratch[levels + 1 : 2 * levels + 1]
    notes = scratch[2 * levels + 1 : 3 * levels + 1]
    sums = scratch[3 * levels + 1 :]

    def bit_of(value, b):
        return lax.rem(value // (1 << b), 2)

    def partner(b):
        return {"depth": me + (1 - 2 * bit_of(me, b)) * (1 << b)}

    loads = [
        pltpu.make_async_copy(source, place, load_sem.at[n])
        for n, (source, place) in enumerate(
            (
                (w1_in, w1), (b1_in, b1), (w2_in, w2), (b2_in, b2), (w3_in, w3), (b3_in, b3),
                (feats_in, feats), (spacing_in, spacing), (counts_in, counts), (target_in, target),
            )
        )
    ]
    for load in loads:
        load.start()
    barrier = pltpu.get_barrier_semaphore()
    greeted = [(a, r) for a in range(views) for r in range(regions) if r == 0 or a % 2 == 0][1:]
    for a, r in greeted:
        where = {"view": lax.rem(view + a, views), "depth": lax.rem(me + r, regions)}
        pl.semaphore_signal(barrier, inc=1, device_id=where, device_id_type=MESH)

    for load in loads[:6]:
        load.wait()
    prepare(feat, w1, b1, w2, b2, w3, b3, w1s, w2f, w2b, w3f, w3b, cols)
    for load in loads[6:]:
        load.wait()

    parts = min(PARTS, seg // 128)
    wide = seg // parts

    def span_of(h, k):
        where = 0
        for b in range(levels):
            where = where + lax.rem(bit_of(me, b) + bit_of(k, levels - 1 - b), 2) * (1 << b)
        return pl.ds(pl.multiple_of(where * seg + h * wide, wide), wide)

    rank = rank_ref[0:1, 0:1]
    row = lax.broadcasted_iota(jnp.int32, (rows - channels, wide), 0)

    def first(b):
        return lax.rem(lax.div(rank, jnp.full_like(rank, 1 << b)), jnp.full_like(rank, 2)) == 0

    def halves(k):
        return [(j, regions >> (j + 1)) for j in range(levels) if k < regions >> (j + 1)]

    def color_copy(j, h, kk):
        n2 = regions >> (j + 1)
        return remote(
            work[j].at[h * 2 * n2 + n2 + kk], got[j].at[h * n2 + kk],
            (fsend, frecv), h * regions + n2 + kk, partner(j),
        )

    def misfit_copy(j, h, kk):
        n2 = regions >> (j + 1)
        part = pl.ds(0, channels)
        return remote(
            back.at[h * regions + kk, part], back.at[h * regions + n2 + kk, part],
            (msend, mrecv), h * regions + n2 + kk, partner(j),
        )

    def note_copy(j, h, kk):
        n2 = regions >> (j + 1)
        return remote(
            notes[j].at[h * n2 + kk], back.at[h * regions + n2 + kk, pl.ds(channels, rows - channels)],
            (nsend, nrecv), h * regions + n2 + kk, partner(j),
        )

    def gather_x(span):
        return jnp.concatenate([feats[s, :, span] for s in range(samples)], axis=1)

    def fold(h, k):
        for j, n2 in halves(k):
            color_copy(j, h, k).wait_recv()
            ahead = first(j)
            mine, other = work[j][h * 2 * n2 + k], got[j][h * n2 + k]
            mine_depth = mine[channels : channels + 1]
            other_depth = other[channels : channels + 1]
            mine_clear = jnp.where(ahead, 1.0, jnp.exp(-other_depth))
            other_clear = jnp.where(ahead, jnp.exp(-mine_depth), 1.0)
            at = h * n2 + k
            work[j + 1][at, 0:channels] = mine_clear * mine[0:channels] + other_clear * other[0:channels]
            work[j + 1][at, channels:rows] = mine[channels:rows] + other[channels:rows]
        if k:
            j = levels - k.bit_length()
            color_copy(j, h, k - (regions >> (j + 1))).start()

    def tell(h, k):
        at = h * regions + k
        if k == 0:
            span = pl.ds(h * wide, wide)
            color = work[levels][h, 0:channels]
            pixels[:, span] = color
            back[at, 0:channels] = color - target[:, span]
            back[at, channels:rows] = jnp.where(row == 0, 1.0, 0.0)
        else:
            j = levels - k.bit_length()
            misfit_copy(j, h, k - (regions >> (j + 1))).wait_recv()
        for j, n2 in reversed(halves(k)):
            misfit_copy(j, h, k).start()
        if k:
            j = levels - k.bit_length()
            note_copy(j, h, k - (regions >> (j + 1))).wait_recv()
        for j, n2 in reversed(halves(k)):
            ahead = first(j)
            mine, other = work[j][h * 2 * n2 + k], got[j][h * n2 + k]
            misfit = back[at, 0:channels]
            state = back[at, channels:rows]
            passed, behind = state[0:1], state[1:2]
            mine_depth = mine[channels : channels + 1]
            other_depth = other[channels : channels + 1]
            hind = jnp.where(ahead, other[0:channels], mine[0:channels])
            later = passed * jnp.exp(-jnp.where(ahead, mine_depth, other_depth))
            glow = behind + later * jnp.sum(misfit * hind, axis=0, keepdims=True)
            mine_state = (jnp.where(ahead, passed, later), jnp.where(ahead, glow, behind))
            other_state = (jnp.where(ahead, later, passed), jnp.where(ahead, behind, glow))
            notes[j][h * n2 + k] = jnp.where(row == 0, *other_state)
            note_copy(j, h, k).start()
            back[at, channels:rows] = jnp.where(row == 0, *mine_state)

    plan = make_plan(regions, parts)
    half = regions // 2
    tiles = [at for what, at in plan if what == "forward"]
    passes, events = [], {}
    ready = 0
    for what, at in plan:
        if what == "forward":
            ready += 1
        elif what in ("backward", "first"):
            passes.append((what, at))
        elif at[0][1] < half:
            key = ("ahead", ready - 1) if ready < len(tiles) else ("back", len(passes))
            events.setdefault(key, []).append((fold if what == "fold" else tell,) + at[0])
    last = max(n for n, at in enumerate(passes) if at[0] == "backward")
    passes, lasts = passes[: last + 1], [at for _, at in passes[last + 1 :]]

    def pick_tiles(i, table):
        out = []
        for n in range(parts):
            h = pick(i, [at[n][0] for at in table])
            k = pick(i, [at[n][1] for at in table])
            out.append((h, k, h * regions + k))
        return out

    def lengths(span):
        return [spacing[s, :, span] for s in range(samples)]

    def run_events(name, i):
        for (kind, at), calls in events.items():
            if kind == name:

                @pl.when(i == at)
                def _():
                    for call, h, k in calls:
                        call(h, k)

    def forward_step(i, carry):
        pair = pick_tiles(i, tiles)
        spans = [span_of(h, k) for h, k, _ in pair]
        results = forward_tile(
            feat, channels, jnp.concatenate([gather_x(span) for span in spans], axis=1),
            [lengths(span) for span in spans], [counts[:, span] for span in spans], w1s, w2f, w3f, cols,
            [keep_x.at[at] for _, _, at in pair], [keep_h.at[at] for _, _, at in pair],
            [keep_raw.at[at] for _, _, at in pair],
        )
        for (_, _, at), (color, depth) in zip(pair, results):
            work[0][at, 0:channels] = color
            work[0][at, channels:rows] = jnp.broadcast_to(depth, (rows - channels, wide))

        @pl.when(i == 0)
        def _():
            pl.semaphore_wait(barrier, len(greeted))

        for h, k, _ in pair:

            @pl.when(k >= half)
            def _():
                color_copy(0, h, k - half).start()

        run_events("ahead", i)
        return carry

    lax.fori_loop(0, len(tiles), forward_step, 0)
    for acc in (acc1, acc2, acc3, bias):
        acc[...] = jnp.zeros_like(acc)

    def backward_step(i, carry):
        run_events("back", i)
        pair = pick_tiles(i, [at[1] for at in passes])
        turn = pick(i, [int(at[0] == "backward") for at in passes])
        for h, k, _ in pair:

            @pl.when((turn == 1) & (k >= half))
            def _():
                misfit_copy(0, h, k - half).wait_recv()
                note_copy(0, h, k - half).wait_recv()

        @pl.when(turn == 1)
        def _():
            spans = [span_of(h, k) for h, k, _ in pair]
            backward_tile(
                channels, [keep_raw.at[at] for _, _, at in pair],
                [back[at, 0:channels] for _, _, at in pair], [back[at, channels:rows] for _, _, at in pair],
                [lengths(span) for span in spans], [counts[:, span] for span in spans],
                [keep_h.at[at] for _, _, at in pair], w3b, acc2, acc3, bias,
            )

        @pl.when(turn == 0)
        def _():
            first_layer_tile(
                [keep_x.at[at] for _, _, at in pair], [keep_h.at[at] for _, _, at in pair], w2b, acc1
            )

        return carry

    lax.fori_loop(0, len(passes), backward_step, 0)
    for h in range(parts):
        for j in range(levels):
            for kk in range(regions >> (j + 1)):
                color_copy(j, h, kk).wait_send()
                misfit_copy(j, h, kk).wait_send()
                note_copy(j, h, kk).wait_send()

    early = wide_stages(views, regions, grads, total, *sums[0:3], (gsend, grecv))
    late = small_stages(views, regions, grads_late, total_late, *sums[3:5], (lsend, lrecv))
    fill_blocks(grads, acc2, acc3, bias)
    early[0]()

    def first_layer_step(i, carry):
        pair = pick_tiles(i, lasts)
        first_layer_tile(
            [keep_x.at[at] for _, _, at in pair], [keep_h.at[at] for _, _, at in pair], w2b, acc1
        )

        @pl.when(i == min(1, len(lasts) - 1))
        def _():
            early[1]()

        return carry

    lax.fori_loop(0, len(lasts), first_layer_step, 0)
    fill_rows(grads_late, acc1, feat)
    early = early[2:]
    for which in "LLELLEE":
        (early if which == "E" else late).pop(0)()


def whole_step(views, regions, feats, spacing, counts, target, rank, weights):
    samples, feat, rays = feats.shape
    channels, seg = target.shape
    hidden = weights[2].shape[0]
    levels = regions.bit_length() - 1
    rows = channels + 8
    parts = min(PARTS, seg // 128)
    tiles = parts * regions
    seg = seg // parts
    wide = samples * seg
    across = hidden // 128
    pairs = views // 2 * regions
    sizes = block_counts(feat, hidden, views, regions)
    inputs = (feats, spacing, counts, target) + tuple(weights)
    scratch = [pltpu.VMEM(value.shape, value.dtype) for value in inputs]
    scratch.append(pltpu.SemaphoreType.DMA((len(inputs),)))
    scratch += [
        pltpu.VMEM((hidden, 128), bf16),
        pltpu.VMEM((hidden, 3 * hidden), bf16),
        pltpu.VMEM((hidden, 2 * hidden), bf16),
        pltpu.VMEM((2 * PAD, hidden), bf16),
        pltpu.VMEM((hidden, 256), bf16),
        pltpu.VMEM((hidden, hidden), f32),
        pltpu.VMEM((tiles, 2, feat, wide), bf16),
        pltpu.VMEM((tiles, 2, hidden, wide), bf16),
        pltpu.VMEM((tiles, PAD, wide), f32),
        pltpu.VMEM((tiles, rows, seg), f32),
        pltpu.VMEM((sizes[0], 8, 128), f32),
        pltpu.VMEM((sizes[1], across, 128), f32),
        pltpu.VMEM((2 * feat + 16, hidden), f32),
        pltpu.VMEM((hidden + 16, hidden), f32),
        pltpu.VMEM((PAD, hidden), f32),
        pltpu.VMEM((PAD, 128), f32),
    ]
    scratch += [pltpu.SemaphoreType.DMA((tiles,))] * 6
    scratch += [pltpu.SemaphoreType.DMA((2 * pairs,))] * 2
    scratch += [pltpu.SemaphoreType.DMA((2 * regions + views - 3,))] * 2
    scratch += [pltpu.VMEM((tiles >> j, rows, seg), f32) for j in range(levels + 1)]
    scratch += [pltpu.VMEM((tiles >> (j + 1), rows, seg), f32) for j in range(levels)]
    scratch += [pltpu.VMEM((tiles >> (j + 1), 8, seg), f32) for j in range(levels)]
    half = sizes[0] // 2
    scratch += [pltpu.VMEM((half, 8, 128), f32)] * 2
    scratch.append(pltpu.VMEM((pairs - 1, half // pairs, 8, 128), f32))
    part = sizes[1] // regions
    scratch.append(pltpu.VMEM((regions - 1, part, across, 128), f32))
    scratch.append(pltpu.VMEM((views, part, across, 128), f32))
    vmem = pl.BlockSpec(memory_space=pltpu.VMEM)
    hbm = pl.BlockSpec(memory_space=pltpu.HBM)
    return pl.pallas_call(
        functools.partial(step_kernel, views, regions),
        in_specs=[hbm] * 4 + [vmem] + [hbm] * 6,
        out_specs=[vmem] * 3,
        out_shape=[
            jax.ShapeDtypeStruct(target.shape, f32),
            jax.ShapeDtypeStruct((sizes[0], 8, 128), f32),
            jax.ShapeDtypeStruct((sizes[1], across, 128), f32),
        ],
        scratch_shapes=scratch,
        compiler_params=pltpu.CompilerParams(
            collective_id=0, has_side_effects=True, vmem_limit_bytes=66000000
        ),
        name="whole_step",
    )(feats, spacing, counts, target, rank, *weights)


def finish_kernel(
    feat, hidden, outs,
    pixels_in, total, late,
    pixels, first_update, first_shift, second_update, second_shift, last_update, last_shift,
):
    def scaled(value, count):
        square = jnp.sum(jnp.sum(value * value, axis=0, keepdims=True), axis=1, keepdims=True)
        return value / jnp.sqrt(square / count + epsilon)

    pixels[...] = pixels_in[...]

    def join(source, at, rows):
        halves = []
        for _ in range(0, hidden, 128):
            halves.append(source[at : at + rows // 8].reshape(rows, 128))
            at += rows // 8
        return jnp.concatenate(halves, axis=1), at

    second, at = join(total, 0, hidden)
    last, at = join(total, at, PAD)
    across = hidden // 128
    first = jnp.concatenate([late[0:feat, i, :] for i in range(across)], axis=1)
    second_update[...] = scaled(second, hidden * hidden)
    first_update[...] = scaled(first, feat * hidden)
    last_update[...] = scaled(last, hidden * outs)[0:outs]
    rows = total[at]
    late_rows = late[feat]
    wide = lambda rows: jnp.concatenate([rows[i : i + 1] for i in range(across)], axis=1)
    first_shift[...] = scaled(wide(late_rows), hidden)
    second_shift[...] = scaled(wide(rows), hidden)
    last_shift[...] = scaled(rows[across : across + 1], outs)[:, 0:outs]


def finish(pixels, total, late, feat, hidden, outs):
    vmem = pl.BlockSpec(memory_space=pltpu.VMEM)
    shapes = [
        pixels.shape, (feat, hidden), (1, hidden), (hidden, hidden), (1, hidden),
        (outs, hidden), (1, outs),
    ]
    return pl.pallas_call(
        functools.partial(finish_kernel, feat, hidden, outs),
        in_specs=[vmem] * 3,
        out_specs=[vmem] * len(shapes),
        out_shape=[jax.ShapeDtypeStruct(shape, f32) for shape in shapes],
        name="normalize_all",
    )(pixels, total, late)


def local(
    features, spacing, counts, depth_rank, target,
    first_weight, first_bias, second_weight, second_bias, last_weight, last_bias,
):
    regions = lax.axis_size("depth")
    views = lax.axis_size("view")
    feat, hidden = first_weight.shape
    outs = last_weight.shape[1]
    feats, gaps, live = jnp.transpose(features[0, 0], (1, 0, 2)), jnp.transpose(spacing[0], (1, 0, 2)), counts[0]
    weights = (
        first_weight, first_bias[None], second_weight, second_bias[None],
        last_weight.T, last_bias[None],
    )
    pixels, total, late = whole_step(views, regions, feats, gaps, live, target[0], depth_rank, weights)
    results = finish(pixels, total, late, feat, hidden, outs)
    return (
        results[0][None], results[1], results[2][0], results[3], results[4][0],
        results[5].T, results[6][0],
    )


def solution(mesh):
    return jax.shard_map(
        local,
        mesh=mesh,
        in_specs=(
            P("view", "depth", None, None, None),
            P("view", "depth", None, None),
            P("view", "depth", None),
            P("view", "depth"),
            P("view", None, "depth"),
            P(), P(), P(), P(), P(), P(),
        ),
        out_specs=(P("view", None, "depth"), P(), P(), P(), P(), P(), P()),
        check_vma=False,
    )
```

```python
import functools

import jax
import jax.numpy as jnp
from jax import lax
from jax.experimental import pallas as pl
from jax.experimental.pallas import tpu as pltpu
from jax.sharding import PartitionSpec as P

epsilon = 1e-05
PAD = 80
PARTS = 2
TURN = ((14, 8, 2, 4, 10, 3, 5, 0), (15, 11, 13, 6, 12, 7, 9, 1))
MESH = pl.DeviceIdType.MESH
f32 = jnp.float32
bf16 = jnp.bfloat16


def split(value):
    high = value.astype(bf16)
    low = (value - high.astype(f32)).astype(bf16)
    return high, low


def mm(left, right):
    return lax.dot_general(left, right, (((1,), (0,)), ((), ())), preferred_element_type=f32)


def mm_nt(left, right):
    return lax.dot_general(left, right, (((1,), (1,)), ((), ())), preferred_element_type=f32)


def opticals(raw, channels, spacing, counts, samples, rays):
    out = []
    for s in range(samples):
        logit = raw[channels : channels + 1, s * rays : (s + 1) * rays]
        density = jnp.maximum(logit, 0.0) + jnp.log1p(jnp.exp(-jnp.abs(logit)))
        length = jnp.where(s < counts, spacing[s], 0.0)
        out.append((logit, density * length, length))
    return out


def remote(src, dst, sems, slot, device):
    return pltpu.make_async_remote_copy(
        src_ref=src,
        dst_ref=dst,
        send_sem=sems[0].at[slot],
        recv_sem=sems[1].at[slot],
        device_id=device,
        device_id_type=MESH,
    )


def lanes(value):
    total = value[:, 0:128]
    for lane in range(128, value.shape[1], 128):
        total = total + value[:, lane : lane + 128]
    return total


def round_up(blocks, devices):
    return -(-blocks // devices) * devices


def block_counts(feat, hidden, views, regions):
    early = (hidden + PAD) // 8 * (hidden // 128) + 1
    return round_up(early, views * regions), round_up(feat + 1, regions)


def fill_blocks(grads, acc2, acc3, bias):
    hidden = acc2.shape[1]
    at = 0
    for acc, blocks in ((acc2, hidden // 8), (acc3, acc3.shape[0] // 8)):
        for lane in range(0, hidden, 128):
            grads[at : at + blocks] = acc[0 : blocks * 8, lane : lane + 128].reshape(blocks, 8, 128)
            at += blocks
    grads[at:] = jnp.zeros((grads.shape[0] - at, 8, 128), f32)
    for i, lane in enumerate(range(0, hidden, 128)):
        grads[at, i : i + 1, :] = acc2[hidden : hidden + 1, lane : lane + 128]
    tall = jnp.concatenate([bias[...], jnp.zeros((128 - bias.shape[0], 128), f32)], axis=0)
    grads[at, hidden // 128 : hidden // 128 + 1, :] = jnp.sum(tall.T, axis=0, keepdims=True)


def fill_rows(grads, acc, feat):
    grads[feat:] = jnp.zeros((grads.shape[0] - feat,) + grads.shape[1:], f32)
    for i, lane in enumerate(range(0, acc.shape[1], 128)):
        part = slice(lane, lane + 128)
        grads[0:feat, i, :] = acc[0:feat, part] + acc[feat : 2 * feat, part]
        grads[feat, i : i + 1, :] = acc[2 * feat : 2 * feat + 1, part]


def stages(moves):
    def stage(n):
        if n > 0:
            copies, after = moves[n - 1]
            for copy in copies():
                copy.wait_recv()
            if after is not None:
                after()
        if n < len(moves):
            for copy in moves[n][0]():
                copy.start()

    def close():
        for copies, _ in moves:
            for copy in copies():
                copy.wait_send()

    return [functools.partial(stage, n) for n in range(len(moves) + 1)] + [close]


def wide_stages(views, regions, grads, total, came, held, landing, sems):
    me = lax.axis_index("depth")
    view = lax.axis_index("view")
    pairs = views // 2
    half = grads.shape[0] // 2
    piece = half // (pairs * regions)
    core = lax.rem(view, 2)
    chip = view // 2
    partner = {"view": view + 1 - 2 * core}
    others = [(a, r) for a in range(pairs) for r in range(regions)][1:]

    def other(a, r):
        return lax.rem(chip + a, pairs), lax.rem(me + r, regions)

    def device(a, r):
        pair, depth = other(a, r)
        return {"view": pair * 2 + core, "depth": depth}

    def swap_half():
        return [remote(grads.at[pl.ds((1 - core) * half, half)], came, sems, 0, partner)]

    def add_half():
        held[...] = grads[pl.ds(core * half, half)] + came[...]

    def scatter():
        out = []
        for n, (a, r) in enumerate(others):
            pair, depth = other(a, r)
            part = held.at[pl.ds((pair * regions + depth) * piece, piece)]
            out.append(remote(part, landing.at[n], sems, 1 + n, device(a, r)))
        return out

    def mine():
        return pl.ds(core * half + (chip * regions + me) * piece, piece)

    def add_pieces():
        value = held[pl.ds((chip * regions + me) * piece, piece)]
        for n in range(len(others)):
            value = value + landing[n]
        total[mine()] = value

    def gather():
        part = total.at[mine()]
        first = 1 + len(others)
        return [remote(part, part, sems, first + n, device(a, r)) for n, (a, r) in enumerate(others)]

    def gather_half():
        part = total.at[pl.ds(core * half, half)]
        return [remote(part, part, sems, 1 + 2 * len(others), partner)]

    return stages([(swap_half, add_half), (scatter, add_pieces), (gather, None), (gather_half, None)])


def small_stages(views, regions, grads, total, landing, slots, sems):
    me = lax.axis_index("depth")
    view = lax.axis_index("view")
    piece = grads.shape[0] // regions

    def peer(r):
        return {"depth": lax.rem(me + r, regions)}

    def scatter():
        return [
            remote(
                grads.at[pl.ds(lax.rem(me + r, regions) * piece, piece)],
                landing.at[r - 1], sems, r - 1, peer(r),
            )
            for r in range(1, regions)
        ]

    def add_depth():
        value = grads[pl.ds(me * piece, piece)]
        for r in range(1, regions):
            value = value + landing[r - 1]
        slots[view] = value

    def exchange():
        part = slots.at[view]
        return [
            remote(part, part, sems, regions - 2 + a, {"view": lax.rem(view + a, views)})
            for a in range(1, views)
        ]

    def add_view():
        value = slots[0]
        for a in range(1, views):
            value = value + slots[a]
        total[pl.ds(me * piece, piece)] = value

    def gather():
        part = total.at[pl.ds(me * piece, piece)]
        first = regions + views - 3
        return [remote(part, part, sems, first + r, peer(r)) for r in range(1, regions)]

    return stages([(scatter, add_depth), (exchange, add_view), (gather, None)])


def make_plan(regions, parts):
    levels = regions.bit_length() - 1
    ahead, back, first = 1.5, 1.1, 0.7
    group = parts
    load = [1.8 / parts * (1 if j < 2 else 1.8) for j in range(levels)]
    lag = [1.7 + 0.3 * (j > 1) for j in range(levels)]
    free = [0.0] * levels
    clock = 0.0
    came = {}
    left = forward_order(regions, parts)
    done, ended, shown, told, walked, closed = [], set(), {}, [], [], []
    steps = []

    def halves(k):
        return [(j, regions >> (j + 1)) for j in range(levels) if k < regions >> (j + 1)]

    def send(j, key):
        free[j] = max(free[j], clock) + load[j]
        came[key] = free[j] + lag[j]

    while len(closed) < parts * regions:
        choices = []
        for h, k in done:
            needs = [came.get(("color", h, k + n2)) for _, n2 in halves(k)]
            if (h, k) not in ended and None not in needs:
                choices.append((max([clock] + needs), 0, h, -k, "fold", [(h, k)]))
        for h in range(parts):
            for k in range(regions):
                when = shown.get(h) if k == 0 else came.get(("misfit", h, k))
                if when is not None and (h, k) not in told:
                    choices.append((max(clock, when), 1, h, k, "tell", [(h, k)]))
        if left:
            choices.append((clock, 2, 0, 0, "forward", left[:group]))
        open_tiles = [at for at in told if at not in walked]
        if len(open_tiles) >= group:
            choices.append((clock, 3, 0, 0, "backward", open_tiles[:group]))
        open_tiles = [at for at in walked if at not in closed]
        if len(open_tiles) >= group:
            choices.append((clock, 4, 0, 0, "first", open_tiles[:group]))
        when, _, _, _, what, tiles = min(choices)
        clock = max(clock, when)
        steps.append((what, tiles))
        h, k = tiles[0]
        if what == "forward":
            clock += ahead
            done += tiles
            left = left[group:]
        elif what == "fold":
            clock += 0.1 * len(halves(k))
            ended.add((h, k))
            if k == 0:
                shown[h] = clock
            else:
                j = levels - k.bit_length()
                send(j, ("color", h, k))
        elif what == "tell":
            told.append((h, k))
            for j, n2 in reversed(halves(k)):
                clock += 0.1
                send(j, ("misfit", h, k + n2))
        elif what == "backward":
            clock += back
            walked += tiles
        else:
            clock += first
            closed += tiles
    return steps


def forward_order(regions, parts):
    tiles = [(h, k) for h in range(parts) for k in range(regions)]
    return sorted(tiles, key=lambda at: (TURN[at[0]][at[1] * len(TURN[0]) // regions], -at[1]))


def pick(i, values):
    out = 0
    for at, value in enumerate(values):
        if value:
            out = out + jnp.where(i == at, value, 0)
    return out


def prepare(feat, w1_ref, b1_ref, w2_ref, b2_ref, w3_ref, b3_ref, w1s, w2f, w2b, w3f, w3b, cols):
    hidden = w2_ref.shape[0]
    outs = w3_ref.shape[0]
    high, low = split(w1_ref[...])
    bias = b1_ref[...]
    bias_a = bias.astype(bf16).astype(f32)
    bias_b = (bias - bias_a).astype(bf16).astype(f32)
    cols[...] = jnp.zeros_like(cols)
    cols[0:feat, :] = high.astype(f32)
    cols[feat : 2 * feat, :] = high.astype(f32)
    cols[2 * feat : 3 * feat, :] = low.astype(f32)
    cols[3 * feat : 3 * feat + 1, :] = bias_a
    cols[3 * feat + 1 : 3 * feat + 2, :] = bias_b
    cols[3 * feat + 2 : 3 * feat + 3, :] = bias - bias_a - bias_b
    cols[3 * feat + 3 : 3 * feat + 4, :] = b2_ref[...]
    cols[3 * feat + 4 : 3 * feat + 5, 0:outs] = b3_ref[...]
    turned = cols[0:128, :].T
    w1s[...] = turned.astype(bf16)
    cols[:, 0:128] = turned
    high, low = split(w2_ref[...].T)
    w2f[:, 0:hidden] = high
    w2f[:, hidden : 2 * hidden] = high
    w2f[:, 2 * hidden : 3 * hidden] = low
    high, low = split(w2_ref[...])
    w2b[:, 0:hidden] = high
    w2b[:, hidden : 2 * hidden] = low
    tall = jnp.concatenate([w3_ref[...], jnp.zeros((PAD - outs, hidden), f32)], axis=0)
    high, low = split(tall)
    w3f[0:PAD, :] = high
    w3f[PAD : 2 * PAD, :] = low
    high = high.astype(f32)
    stack = jnp.concatenate(
        [high, high, tall - high, jnp.zeros((256 - 3 * PAD, hidden), f32)], axis=0
    )
    w3b[...] = stack.T.astype(bf16)


def columns(value, n, wide):
    return value[:, n * wide : (n + 1) * wide]


def forward_tile(feat, channels, x, spacing, counts, w1s, w2f, w3f, cols, keep_x, keep_h, keep_raw):
    samples = len(spacing[0])
    rays = spacing[0][0].shape[1]
    wide = samples * rays
    xh, xl = split(x)
    rows = lax.broadcasted_iota(jnp.int32, x.shape, 0)
    ones = jnp.where(rows < 3, 1.0, 0.0).astype(bf16)
    z1 = mm(w1s[...], jnp.concatenate([xh, xl, xh, ones], axis=0))
    h1h, h1l = split(jnp.maximum(z1, 0.0))
    z2 = mm(w2f[...], jnp.concatenate([h1h, h1l, h1h], axis=0))
    z2 = z2 + cols[:, 3 * feat + 3 : 3 * feat + 4]
    h2h, h2l = split(jnp.maximum(z2, 0.0))
    both = mm(w3f[...], h2h)
    raw = both[0:PAD] + both[PAD:] + mm(w3f[0:PAD, :], h2l)
    raw = raw + cols[0:PAD, 3 * feat + 4 : 3 * feat + 5]
    out = []
    for n in range(len(spacing)):
        keep_x[n][0] = columns(xh, n, wide)
        keep_x[n][1] = columns(xl, n, wide)
        keep_h[n][0] = columns(h1h, n, wide)
        keep_h[n][1] = columns(h2h, n, wide)
        own = columns(raw, n, wide)
        shown = jax.nn.sigmoid(own[0:channels])
        keep_raw[n][0:channels] = shown
        keep_raw[n][channels:PAD] = own[channels:PAD]
        before = None
        color = None
        for s, (_, optical, _) in enumerate(opticals(own, channels, spacing[n], counts[n], samples, rays)):
            weight = 1.0 - jnp.exp(-optical)
            if s:
                weight = jnp.exp(-before) * weight
            shade = weight * shown[:, s * rays : (s + 1) * rays]
            color = shade if s == 0 else color + shade
            before = optical if s == 0 else before + optical
        out.append((color, before))
    return out


def raw_grad(channels, raw, misfit, state, spacing, counts):
    samples = len(spacing)
    rays = spacing[0].shape[1]
    passed = state[0:1]
    parts = opticals(raw, channels, spacing, counts, samples, rays)
    befores, before = [], None
    for s in range(samples):
        befores.append(before)
        before = parts[s][1] if s == 0 else before + parts[s][1]
    tail = -state[1:2]
    pieces = [None] * samples
    for s in reversed(range(samples)):
        logit, optical, length = parts[s]
        gone = jnp.exp(-optical)
        ahead = 1.0 if s == 0 else jnp.exp(-befores[s])
        weight = ahead * (1.0 - gone)
        color = raw[0:channels, s * rays : (s + 1) * rays]
        weight_grad = passed * jnp.sum(misfit * color, axis=0, keepdims=True)
        optical_grad = weight_grad * (ahead * gone) + tail
        tail = tail - weight_grad * weight
        color_grad = (weight * passed) * misfit * (color * (1.0 - color))
        logit_grad = optical_grad * length * jax.nn.sigmoid(logit)
        row = lax.broadcasted_iota(jnp.int32, (PAD - channels, rays), 0)
        rest = jnp.where(row == 0, jnp.broadcast_to(logit_grad, row.shape), 0.0)
        pieces[s] = jnp.concatenate([color_grad, rest], axis=0)
    return pieces


def backward_tile(channels, raws, misfits, states, spacing, counts, keep_h, w3b, acc2, acc3, bias):
    pieces = []
    for at in zip(raws, misfits, states, spacing, counts):
        pieces += raw_grad(channels, *at)
    draw = jnp.concatenate(pieces, axis=1)
    bias[0:PAD, :] += lanes(draw)
    dh, dl = split(draw)
    h2h = jnp.concatenate([keep[1] for keep in keep_h], axis=1)
    both = mm_nt(jnp.concatenate([dh, dl], axis=0), h2h)
    acc3[...] += both[0:PAD] + both[PAD:]
    zero = jnp.zeros((256 - 3 * PAD, draw.shape[1]), bf16)
    dh2 = mm(w3b[...], jnp.concatenate([dh, dl, dh, zero], axis=0))
    zh = jnp.where(h2h > 0, dh2.astype(bf16), jnp.zeros_like(h2h))
    h1h = jnp.concatenate([keep[0] for keep in keep_h], axis=1)
    acc2[...] += mm_nt(jnp.concatenate([h1h, jnp.ones((16, h1h.shape[1]), bf16)], axis=0), zh)
    wide = zh.shape[1] // len(keep_h)
    for n, keep in enumerate(keep_h):
        keep[1] = columns(zh, n, wide)


def first_layer_tile(keep_x, keep_h, w2b, acc1):
    h1h = jnp.concatenate([keep[0] for keep in keep_h], axis=1)
    zh = jnp.concatenate([keep[1] for keep in keep_h], axis=1)
    dh1 = mm(w2b[...], jnp.concatenate([zh, zh], axis=0))
    zh = jnp.where(h1h > 0, dh1.astype(bf16), jnp.zeros_like(h1h))
    x = [jnp.concatenate([keep[i] for keep in keep_x], axis=1) for i in (0, 1)]
    x.append(jnp.ones((16, zh.shape[1]), bf16))
    acc1[...] += mm_nt(jnp.concatenate(x, axis=0), zh)


def step_kernel(
    views, regions,
    feats_in, spacing_in, counts_in, target_in, rank_ref, w1_in, b1_in, w2_in, b2_in, w3_in, b3_in,
    pixels, total, total_late,
    feats, spacing, counts, target, w1, b1, w2, b2, w3, b3, load_sem,
    w1s, w2f, w2b, w3f, w3b, cols, keep_x, keep_h, keep_raw, back, grads, grads_late,
    acc1, acc2, acc3, bias, fsend, frecv, msend, mrecv, nsend, nrecv, gsend, grecv, lsend, lrecv,
    *scratch,
):
    samples, feat, rays = feats.shape
    channels, seg = target.shape
    levels = regions.bit_length() - 1
    rows = back.shape[1]
    hidden = w2.shape[0]
    me = lax.axis_index("depth")
    view = lax.axis_index("view")
    work = scratch[0 : levels + 1]
    got = scratch[levels + 1 : 2 * levels + 1]
    notes = scratch[2 * levels + 1 : 3 * levels + 1]
    sums = scratch[3 * levels + 1 :]

    def bit_of(value, b):
        return lax.rem(value // (1 << b), 2)

    def partner(b):
        return {"depth": me + (1 - 2 * bit_of(me, b)) * (1 << b)}

    loads = [
        pltpu.make_async_copy(source, place, load_sem.at[n])
        for n, (source, place) in enumerate(
            (
                (w1_in, w1), (b1_in, b1), (w2_in, w2), (b2_in, b2), (w3_in, w3), (b3_in, b3),
                (feats_in, feats), (spacing_in, spacing), (counts_in, counts), (target_in, target),
            )
        )
    ]
    for load in loads:
        load.start()
    barrier = pltpu.get_barrier_semaphore()
    greeted = [(a, r) for a in range(views) for r in range(regions) if r == 0 or a % 2 == 0][1:]
    for a, r in greeted:
        where = {"view": lax.rem(view + a, views), "depth": lax.rem(me + r, regions)}
        pl.semaphore_signal(barrier, inc=1, device_id=where, device_id_type=MESH)

    for load in loads[:6]:
        load.wait()
    prepare(feat, w1, b1, w2, b2, w3, b3, w1s, w2f, w2b, w3f, w3b, cols)
    for load in loads[6:]:
        load.wait()

    parts = min(PARTS, seg // 128)
    wide = seg // parts

    def span_of(h, k):
        where = 0
        for b in range(levels):
            where = where + lax.rem(bit_of(me, b) + bit_of(k, levels - 1 - b), 2) * (1 << b)
        return pl.ds(pl.multiple_of(where * seg + h * wide, wide), wide)

    rank = rank_ref[0:1, 0:1]
    row = lax.broadcasted_iota(jnp.int32, (rows - channels, wide), 0)

    def first(b):
        return lax.rem(lax.div(rank, jnp.full_like(rank, 1 << b)), jnp.full_like(rank, 2)) == 0

    def halves(k):
        return [(j, regions >> (j + 1)) for j in range(levels) if k < regions >> (j + 1)]

    def color_copy(j, h, kk):
        n2 = regions >> (j + 1)
        return remote(
            work[j].at[h * 2 * n2 + n2 + kk], got[j].at[h * n2 + kk],
            (fsend, frecv), h * regions + n2 + kk, partner(j),
        )

    def misfit_copy(j, h, kk):
        n2 = regions >> (j + 1)
        part = pl.ds(0, channels)
        return remote(
            back.at[h * regions + kk, part], back.at[h * regions + n2 + kk, part],
            (msend, mrecv), h * regions + n2 + kk, partner(j),
        )

    def note_copy(j, h, kk):
        n2 = regions >> (j + 1)
        return remote(
            notes[j].at[h * n2 + kk], back.at[h * regions + n2 + kk, pl.ds(channels, rows - channels)],
            (nsend, nrecv), h * regions + n2 + kk, partner(j),
        )

    def gather_x(span):
        return jnp.concatenate([feats[s, :, span] for s in range(samples)], axis=1)

    def fold(h, k):
        for j, n2 in halves(k):
            color_copy(j, h, k).wait_recv()
            ahead = first(j)
            mine, other = work[j][h * 2 * n2 + k], got[j][h * n2 + k]
            mine_depth = mine[channels : channels + 1]
            other_depth = other[channels : channels + 1]
            mine_clear = jnp.where(ahead, 1.0, jnp.exp(-other_depth))
            other_clear = jnp.where(ahead, jnp.exp(-mine_depth), 1.0)
            at = h * n2 + k
            work[j + 1][at, 0:channels] = mine_clear * mine[0:channels] + other_clear * other[0:channels]
            work[j + 1][at, channels:rows] = mine[channels:rows] + other[channels:rows]
        if k:
            j = levels - k.bit_length()
            color_copy(j, h, k - (regions >> (j + 1))).start()

    def tell(h, k):
        at = h * regions + k
        if k == 0:
            span = pl.ds(h * wide, wide)
            color = work[levels][h, 0:channels]
            pixels[:, span] = color
            back[at, 0:channels] = color - target[:, span]
            back[at, channels:rows] = jnp.where(row == 0, 1.0, 0.0)
        else:
            j = levels - k.bit_length()
            misfit_copy(j, h, k - (regions >> (j + 1))).wait_recv()
        for j, n2 in reversed(halves(k)):
            misfit_copy(j, h, k).start()
        if k:
            j = levels - k.bit_length()
            note_copy(j, h, k - (regions >> (j + 1))).wait_recv()
        for j, n2 in reversed(halves(k)):
            ahead = first(j)
            mine, other = work[j][h * 2 * n2 + k], got[j][h * n2 + k]
            misfit = back[at, 0:channels]
            state = back[at, channels:rows]
            passed, behind = state[0:1], state[1:2]
            mine_depth = mine[channels : channels + 1]
            other_depth = other[channels : channels + 1]
            hind = jnp.where(ahead, other[0:channels], mine[0:channels])
            later = passed * jnp.exp(-jnp.where(ahead, mine_depth, other_depth))
            glow = behind + later * jnp.sum(misfit * hind, axis=0, keepdims=True)
            mine_state = (jnp.where(ahead, passed, later), jnp.where(ahead, glow, behind))
            other_state = (jnp.where(ahead, later, passed), jnp.where(ahead, behind, glow))
            notes[j][h * n2 + k] = jnp.where(row == 0, *other_state)
            note_copy(j, h, k).start()
            back[at, channels:rows] = jnp.where(row == 0, *mine_state)

    plan = make_plan(regions, parts)
    half = regions // 2
    tiles = [at for what, at in plan if what == "forward"]
    passes, events = [], {}
    ready = 0
    for what, at in plan:
        if what == "forward":
            ready += 1
        elif what in ("backward", "first"):
            passes.append((what, at))
        elif at[0][1] < half:
            key = ("ahead", ready - 1) if ready < len(tiles) else ("back", len(passes))
            events.setdefault(key, []).append((fold if what == "fold" else tell,) + at[0])
    last = max(n for n, at in enumerate(passes) if at[0] == "backward")
    passes, lasts = passes[: last + 1], [at for _, at in passes[last + 1 :]]

    def pick_tiles(i, table):
        out = []
        for n in range(parts):
            h = pick(i, [at[n][0] for at in table])
            k = pick(i, [at[n][1] for at in table])
            out.append((h, k, h * regions + k))
        return out

    def lengths(span):
        return [spacing[s, :, span] for s in range(samples)]

    def run_events(name, i):
        for (kind, at), calls in events.items():
            if kind == name:

                @pl.when(i == at)
                def _():
                    for call, h, k in calls:
                        call(h, k)

    def forward_step(i, carry):
        pair = pick_tiles(i, tiles)
        spans = [span_of(h, k) for h, k, _ in pair]
        results = forward_tile(
            feat, channels, jnp.concatenate([gather_x(span) for span in spans], axis=1),
            [lengths(span) for span in spans], [counts[:, span] for span in spans], w1s, w2f, w3f, cols,
            [keep_x.at[at] for _, _, at in pair], [keep_h.at[at] for _, _, at in pair],
            [keep_raw.at[at] for _, _, at in pair],
        )
        for (_, _, at), (color, depth) in zip(pair, results):
            work[0][at, 0:channels] = color
            work[0][at, channels:rows] = jnp.broadcast_to(depth, (rows - channels, wide))

        @pl.when(i == 0)
        def _():
            pl.semaphore_wait(barrier, len(greeted))

        for h, k, _ in pair:

            @pl.when(k >= half)
            def _():
                color_copy(0, h, k - half).start()

        run_events("ahead", i)
        return carry

    lax.fori_loop(0, len(tiles), forward_step, 0)
    for acc in (acc1, acc2, acc3, bias):
        acc[...] = jnp.zeros_like(acc)

    def backward_step(i, carry):
        run_events("back", i)
        pair = pick_tiles(i, [at[1] for at in passes])
        turn = pick(i, [int(at[0] == "backward") for at in passes])
        for h, k, _ in pair:

            @pl.when((turn == 1) & (k >= half))
            def _():
                misfit_copy(0, h, k - half).wait_recv()
                note_copy(0, h, k - half).wait_recv()

        @pl.when(turn == 1)
        def _():
            spans = [span_of(h, k) for h, k, _ in pair]
            backward_tile(
                channels, [keep_raw.at[at] for _, _, at in pair],
                [back[at, 0:channels] for _, _, at in pair], [back[at, channels:rows] for _, _, at in pair],
                [lengths(span) for span in spans], [counts[:, span] for span in spans],
                [keep_h.at[at] for _, _, at in pair], w3b, acc2, acc3, bias,
            )

        @pl.when(turn == 0)
        def _():
            first_layer_tile(
                [keep_x.at[at] for _, _, at in pair], [keep_h.at[at] for _, _, at in pair], w2b, acc1
            )

        return carry

    lax.fori_loop(0, len(passes), backward_step, 0)
    early = wide_stages(views, regions, grads, total, *sums[0:3], (gsend, grecv))
    late = small_stages(views, regions, grads_late, total_late, *sums[3:5], (lsend, lrecv))
    fill_blocks(grads, acc2, acc3, bias)
    early[0]()

    def first_layer_step(i, carry):
        pair = pick_tiles(i, lasts)
        first_layer_tile(
            [keep_x.at[at] for _, _, at in pair], [keep_h.at[at] for _, _, at in pair], w2b, acc1
        )

        @pl.when(i == min(1, len(lasts) - 1))
        def _():
            early[1]()

        return carry

    lax.fori_loop(0, len(lasts), first_layer_step, 0)
    fill_rows(grads_late, acc1, feat)
    early = early[2:]
    for which in "LLELLEE":
        (early if which == "E" else late).pop(0)()
    for h in range(parts):
        for j in range(levels):
            for kk in range(regions >> (j + 1)):
                color_copy(j, h, kk).wait_send()
                misfit_copy(j, h, kk).wait_send()
                note_copy(j, h, kk).wait_send()
    for close in early + late:
        close()


def whole_step(views, regions, feats, spacing, counts, target, rank, weights):
    samples, feat, rays = feats.shape
    channels, seg = target.shape
    hidden = weights[2].shape[0]
    levels = regions.bit_length() - 1
    rows = channels + 8
    parts = min(PARTS, seg // 128)
    tiles = parts * regions
    seg = seg // parts
    wide = samples * seg
    across = hidden // 128
    pairs = views // 2 * regions
    sizes = block_counts(feat, hidden, views, regions)
    inputs = (feats, spacing, counts, target) + tuple(weights)
    scratch = [pltpu.VMEM(value.shape, value.dtype) for value in inputs]
    scratch.append(pltpu.SemaphoreType.DMA((len(inputs),)))
    scratch += [
        pltpu.VMEM((hidden, 128), bf16),
        pltpu.VMEM((hidden, 3 * hidden), bf16),
        pltpu.VMEM((hidden, 2 * hidden), bf16),
        pltpu.VMEM((2 * PAD, hidden), bf16),
        pltpu.VMEM((hidden, 256), bf16),
        pltpu.VMEM((hidden, hidden), f32),
        pltpu.VMEM((tiles, 2, feat, wide), bf16),
        pltpu.VMEM((tiles, 2, hidden, wide), bf16),
        pltpu.VMEM((tiles, PAD, wide), f32),
        pltpu.VMEM((tiles, rows, seg), f32),
        pltpu.VMEM((sizes[0], 8, 128), f32),
        pltpu.VMEM((sizes[1], across, 128), f32),
        pltpu.VMEM((2 * feat + 16, hidden), f32),
        pltpu.VMEM((hidden + 16, hidden), f32),
        pltpu.VMEM((PAD, hidden), f32),
        pltpu.VMEM((PAD, 128), f32),
    ]
    scratch += [pltpu.SemaphoreType.DMA((tiles,))] * 6
    scratch += [pltpu.SemaphoreType.DMA((2 * pairs,))] * 2
    scratch += [pltpu.SemaphoreType.DMA((2 * regions + views - 3,))] * 2
    scratch += [pltpu.VMEM((tiles >> j, rows, seg), f32) for j in range(levels + 1)]
    scratch += [pltpu.VMEM((tiles >> (j + 1), rows, seg), f32) for j in range(levels)]
    scratch += [pltpu.VMEM((tiles >> (j + 1), 8, seg), f32) for j in range(levels)]
    half = sizes[0] // 2
    scratch += [pltpu.VMEM((half, 8, 128), f32)] * 2
    scratch.append(pltpu.VMEM((pairs - 1, half // pairs, 8, 128), f32))
    part = sizes[1] // regions
    scratch.append(pltpu.VMEM((regions - 1, part, across, 128), f32))
    scratch.append(pltpu.VMEM((views, part, across, 128), f32))
    vmem = pl.BlockSpec(memory_space=pltpu.VMEM)
    hbm = pl.BlockSpec(memory_space=pltpu.HBM)
    return pl.pallas_call(
        functools.partial(step_kernel, views, regions),
        in_specs=[hbm] * 4 + [vmem] + [hbm] * 6,
        out_specs=[vmem] * 3,
        out_shape=[
            jax.ShapeDtypeStruct(target.shape, f32),
            jax.ShapeDtypeStruct((sizes[0], 8, 128), f32),
            jax.ShapeDtypeStruct((sizes[1], across, 128), f32),
        ],
        scratch_shapes=scratch,
        compiler_params=pltpu.CompilerParams(
            collective_id=0, has_side_effects=True, vmem_limit_bytes=66000000
        ),
        name="whole_step",
    )(feats, spacing, counts, target, rank, *weights)


def finish_kernel(
    feat, hidden, outs,
    pixels_in, total, late,
    pixels, first_update, first_shift, second_update, second_shift, last_update, last_shift,
):
    def scaled(value, count):
        square = jnp.sum(jnp.sum(value * value, axis=0, keepdims=True), axis=1, keepdims=True)
        return value / jnp.sqrt(square / count + epsilon)

    pixels[...] = pixels_in[...]

    def join(source, at, rows):
        halves = []
        for _ in range(0, hidden, 128):
            halves.append(source[at : at + rows // 8].reshape(rows, 128))
            at += rows // 8
        return jnp.concatenate(halves, axis=1), at

    second, at = join(total, 0, hidden)
    last, at = join(total, at, PAD)
    across = hidden // 128
    first = jnp.concatenate([late[0:feat, i, :] for i in range(across)], axis=1)
    second_update[...] = scaled(second, hidden * hidden)
    first_update[...] = scaled(first, feat * hidden)
    last_update[...] = scaled(last, hidden * outs)[0:outs]
    rows = total[at]
    late_rows = late[feat]
    wide = lambda rows: jnp.concatenate([rows[i : i + 1] for i in range(across)], axis=1)
    first_shift[...] = scaled(wide(late_rows), hidden)
    second_shift[...] = scaled(wide(rows), hidden)
    last_shift[...] = scaled(rows[across : across + 1], outs)[:, 0:outs]


def finish(pixels, total, late, feat, hidden, outs):
    vmem = pl.BlockSpec(memory_space=pltpu.VMEM)
    shapes = [
        pixels.shape, (feat, hidden), (1, hidden), (hidden, hidden), (1, hidden),
        (outs, hidden), (1, outs),
    ]
    return pl.pallas_call(
        functools.partial(finish_kernel, feat, hidden, outs),
        in_specs=[vmem] * 3,
        out_specs=[vmem] * len(shapes),
        out_shape=[jax.ShapeDtypeStruct(shape, f32) for shape in shapes],
        name="normalize_all",
    )(pixels, total, late)


def local(
    features, spacing, counts, depth_rank, target,
    first_weight, first_bias, second_weight, second_bias, last_weight, last_bias,
):
    regions = lax.axis_size("depth")
    views = lax.axis_size("view")
    feat, hidden = first_weight.shape
    outs = last_weight.shape[1]
    feats, gaps, live = jnp.transpose(features[0, 0], (1, 0, 2)), jnp.transpose(spacing[0], (1, 0, 2)), counts[0]
    weights = (
        first_weight, first_bias[None], second_weight, second_bias[None],
        last_weight.T, last_bias[None],
    )
    pixels, total, late = whole_step(views, regions, feats, gaps, live, target[0], depth_rank, weights)
    results = finish(pixels, total, late, feat, hidden, outs)
    return (
        results[0][None], results[1], results[2][0], results[3], results[4][0],
        results[5].T, results[6][0],
    )


def solution(mesh):
    return jax.shard_map(
        local,
        mesh=mesh,
        in_specs=(
            P("view", "depth", None, None, None),
            P("view", "depth", None, None),
            P("view", "depth", None),
            P("view", "depth"),
            P("view", None, "depth"),
            P(), P(), P(), P(), P(), P(),
        ),
        out_specs=(P("view", None, "depth"), P(), P(), P(), P(), P(), P()),
        check_vma=False,
    )
```

```python
import functools

import jax
import jax.numpy as jnp
from jax import lax
from jax.experimental import pallas as pl
from jax.experimental.pallas import tpu as pltpu
from jax.sharding import PartitionSpec as P

epsilon = 1e-05
PAD = 80
PARTS = 2
TURN = ((14, 8, 2, 4, 10, 3, 5, 0), (15, 11, 13, 6, 12, 7, 9, 1))
MESH = pl.DeviceIdType.MESH
f32 = jnp.float32
bf16 = jnp.bfloat16


def split(value):
    high = value.astype(bf16)
    low = (value - high.astype(f32)).astype(bf16)
    return high, low


def mm(left, right):
    return lax.dot_general(left, right, (((1,), (0,)), ((), ())), preferred_element_type=f32)


def mm_nt(left, right):
    return lax.dot_general(left, right, (((1,), (1,)), ((), ())), preferred_element_type=f32)


def opticals(raw, channels, spacing, counts, samples, rays):
    out = []
    for s in range(samples):
        logit = raw[channels : channels + 1, s * rays : (s + 1) * rays]
        density = jnp.maximum(logit, 0.0) + jnp.log1p(jnp.exp(-jnp.abs(logit)))
        length = jnp.where(s < counts, spacing[s], 0.0)
        out.append((logit, density * length, length))
    return out


def remote(src, dst, sems, slot, device):
    return pltpu.make_async_remote_copy(
        src_ref=src,
        dst_ref=dst,
        send_sem=sems[0].at[slot],
        recv_sem=sems[1].at[slot],
        device_id=device,
        device_id_type=MESH,
    )


def lanes(value):
    total = value[:, 0:128]
    for lane in range(128, value.shape[1], 128):
        total = total + value[:, lane : lane + 128]
    return total


def round_up(blocks, devices):
    return -(-blocks // devices) * devices


def block_counts(feat, hidden, views, regions):
    early = (hidden + PAD) // 8 * (hidden // 128) + 1
    return round_up(early, views * regions), round_up(feat + 1, regions)


def fill_blocks(grads, acc2, acc3, bias):
    hidden = acc2.shape[1]
    at = 0
    for acc, blocks in ((acc2, hidden // 8), (acc3, acc3.shape[0] // 8)):
        for lane in range(0, hidden, 128):
            grads[at : at + blocks] = acc[0 : blocks * 8, lane : lane + 128].reshape(blocks, 8, 128)
            at += blocks
    grads[at:] = jnp.zeros((grads.shape[0] - at, 8, 128), f32)
    for i, lane in enumerate(range(0, hidden, 128)):
        grads[at, i : i + 1, :] = acc2[hidden : hidden + 1, lane : lane + 128]
    tall = jnp.concatenate([bias[...], jnp.zeros((128 - bias.shape[0], 128), f32)], axis=0)
    grads[at, hidden // 128 : hidden // 128 + 1, :] = jnp.sum(tall.T, axis=0, keepdims=True)


def fill_rows(grads, acc, feat):
    grads[feat:] = jnp.zeros((grads.shape[0] - feat,) + grads.shape[1:], f32)
    for i, lane in enumerate(range(0, acc.shape[1], 128)):
        part = slice(lane, lane + 128)
        grads[0:feat, i, :] = acc[0:feat, part] + acc[feat : 2 * feat, part]
        grads[feat, i : i + 1, :] = acc[2 * feat : 2 * feat + 1, part]


def stages(moves):
    def stage(n):
        if n > 0:
            copies, after = moves[n - 1]
            for copy in copies():
                copy.wait_recv()
            if after is not None:
                after()
        if n < len(moves):
            for copy in moves[n][0]():
                copy.start()

    def close():
        for copies, _ in moves:
            for copy in copies():
                copy.wait_send()

    return [functools.partial(stage, n) for n in range(len(moves) + 1)] + [close]


def wide_stages(views, regions, grads, total, came, held, landing, sems):
    me = lax.axis_index("depth")
    view = lax.axis_index("view")
    pairs = views // 2
    half = grads.shape[0] // 2
    piece = half // (pairs * regions)
    core = lax.rem(view, 2)
    chip = view // 2
    partner = {"view": view + 1 - 2 * core}
    others = [(a, r) for a in range(pairs) for r in range(regions)][1:]

    def other(a, r):
        return lax.rem(chip + a, pairs), lax.rem(me + r, regions)

    def device(a, r):
        pair, depth = other(a, r)
        return {"view": pair * 2 + core, "depth": depth}

    def swap_half():
        return [remote(grads.at[pl.ds((1 - core) * half, half)], came, sems, 0, partner)]

    def add_half():
        held[...] = grads[pl.ds(core * half, half)] + came[...]

    def scatter():
        out = []
        for n, (a, r) in enumerate(others):
            pair, depth = other(a, r)
            part = held.at[pl.ds((pair * regions + depth) * piece, piece)]
            out.append(remote(part, landing.at[n], sems, 1 + n, device(a, r)))
        return out

    def mine():
        return pl.ds(core * half + (chip * regions + me) * piece, piece)

    def add_pieces():
        value = held[pl.ds((chip * regions + me) * piece, piece)]
        for n in range(len(others)):
            value = value + landing[n]
        total[mine()] = value

    def gather():
        part = total.at[mine()]
        first = 1 + len(others)
        return [remote(part, part, sems, first + n, device(a, r)) for n, (a, r) in enumerate(others)]

    def gather_half():
        part = total.at[pl.ds(core * half, half)]
        return [remote(part, part, sems, 1 + 2 * len(others), partner)]

    return stages([(swap_half, add_half), (scatter, add_pieces), (gather, None), (gather_half, None)])


def small_stages(views, regions, grads, total, landing, slots, sems):
    me = lax.axis_index("depth")
    view = lax.axis_index("view")
    piece = grads.shape[0] // regions

    def peer(r):
        return {"depth": lax.rem(me + r, regions)}

    def scatter():
        return [
            remote(
                grads.at[pl.ds(lax.rem(me + r, regions) * piece, piece)],
                landing.at[r - 1], sems, r - 1, peer(r),
            )
            for r in range(1, regions)
        ]

    def add_depth():
        value = grads[pl.ds(me * piece, piece)]
        for r in range(1, regions):
            value = value + landing[r - 1]
        slots[view] = value

    def exchange():
        part = slots.at[view]
        return [
            remote(part, part, sems, regions - 2 + a, {"view": lax.rem(view + a, views)})
            for a in range(1, views)
        ]

    def add_view():
        value = slots[0]
        for a in range(1, views):
            value = value + slots[a]
        total[pl.ds(me * piece, piece)] = value

    def gather():
        part = total.at[pl.ds(me * piece, piece)]
        first = regions + views - 3
        return [remote(part, part, sems, first + r, peer(r)) for r in range(1, regions)]

    return stages([(scatter, add_depth), (exchange, add_view), (gather, None)])


def make_plan(regions, parts):
    levels = regions.bit_length() - 1
    ahead, back, first = 1.5, 1.1, 0.7
    group = parts
    load = [1.8 / parts * (1 if j < 2 else 1.8) for j in range(levels)]
    lag = [1.5 + 0.3 * (j > 1) for j in range(levels)]
    free = [0.0] * levels
    clock = 0.0
    came = {}
    left = forward_order(regions, parts)
    done, ended, shown, told, walked, closed = [], set(), {}, [], [], []
    steps = []

    def halves(k):
        return [(j, regions >> (j + 1)) for j in range(levels) if k < regions >> (j + 1)]

    def send(j, key):
        free[j] = max(free[j], clock) + load[j]
        came[key] = free[j] + lag[j]

    while len(closed) < parts * regions:
        choices = []
        for h, k in done:
            needs = [came.get(("color", h, k + n2)) for _, n2 in halves(k)]
            if (h, k) not in ended and None not in needs:
                choices.append((max([clock] + needs), 0, h, -k, "fold", [(h, k)]))
        for h in range(parts):
            for k in range(regions):
                when = shown.get(h) if k == 0 else came.get(("misfit", h, k))
                if when is not None and (h, k) not in told:
                    choices.append((max(clock, when), 1, h, k, "tell", [(h, k)]))
        if left:
            choices.append((clock, 2, 0, 0, "forward", left[:group]))
        open_tiles = [at for at in told if at not in walked]
        if len(open_tiles) >= group:
            choices.append((clock, 3, 0, 0, "backward", open_tiles[:group]))
        open_tiles = [at for at in walked if at not in closed]
        if len(open_tiles) >= group:
            choices.append((clock, 4, 0, 0, "first", open_tiles[:group]))
        when, _, _, _, what, tiles = min(choices)
        clock = max(clock, when)
        steps.append((what, tiles))
        h, k = tiles[0]
        if what == "forward":
            clock += ahead
            done += tiles
            left = left[group:]
        elif what == "fold":
            clock += 0.1 * len(halves(k))
            ended.add((h, k))
            if k == 0:
                shown[h] = clock
            else:
                j = levels - k.bit_length()
                send(j, ("color", h, k))
        elif what == "tell":
            told.append((h, k))
            for j, n2 in reversed(halves(k)):
                clock += 0.1
                send(j, ("misfit", h, k + n2))
        elif what == "backward":
            clock += back
            walked += tiles
        else:
            clock += first
            closed += tiles
    return steps


def forward_order(regions, parts):
    tiles = [(h, k) for h in range(parts) for k in range(regions)]
    return sorted(tiles, key=lambda at: (TURN[at[0]][at[1] * len(TURN[0]) // regions], -at[1]))


def pick(i, values):
    out = 0
    for at, value in enumerate(values):
        if value:
            out = out + jnp.where(i == at, value, 0)
    return out


def prepare(feat, w1_ref, b1_ref, w2_ref, b2_ref, w3_ref, b3_ref, w1s, w2f, w2b, w3f, w3b, cols):
    hidden = w2_ref.shape[0]
    outs = w3_ref.shape[0]
    high, low = split(w1_ref[...])
    bias = b1_ref[...]
    bias_a = bias.astype(bf16).astype(f32)
    bias_b = (bias - bias_a).astype(bf16).astype(f32)
    cols[...] = jnp.zeros_like(cols)
    cols[0:feat, :] = high.astype(f32)
    cols[feat : 2 * feat, :] = high.astype(f32)
    cols[2 * feat : 3 * feat, :] = low.astype(f32)
    cols[3 * feat : 3 * feat + 1, :] = bias_a
    cols[3 * feat + 1 : 3 * feat + 2, :] = bias_b
    cols[3 * feat + 2 : 3 * feat + 3, :] = bias - bias_a - bias_b
    cols[3 * feat + 3 : 3 * feat + 4, :] = b2_ref[...]
    cols[3 * feat + 4 : 3 * feat + 5, 0:outs] = b3_ref[...]
    turned = cols[0:128, :].T
    w1s[...] = turned.astype(bf16)
    cols[:, 0:128] = turned
    high, low = split(w2_ref[...].T)
    w2f[:, 0:hidden] = high
    w2f[:, hidden : 2 * hidden] = high
    w2f[:, 2 * hidden : 3 * hidden] = low
    high, low = split(w2_ref[...])
    w2b[:, 0:hidden] = high
    w2b[:, hidden : 2 * hidden] = low
    tall = jnp.concatenate([w3_ref[...], jnp.zeros((PAD - outs, hidden), f32)], axis=0)
    high, low = split(tall)
    w3f[0:PAD, :] = high
    w3f[PAD : 2 * PAD, :] = low
    high = high.astype(f32)
    stack = jnp.concatenate(
        [high, high, tall - high, jnp.zeros((256 - 3 * PAD, hidden), f32)], axis=0
    )
    w3b[...] = stack.T.astype(bf16)


def columns(value, n, wide):
    return value[:, n * wide : (n + 1) * wide]


def forward_tile(feat, channels, x, spacing, counts, w1s, w2f, w3f, cols, keep_x, keep_h, keep_raw):
    samples = len(spacing[0])
    rays = spacing[0][0].shape[1]
    wide = samples * rays
    xh, xl = split(x)
    rows = lax.broadcasted_iota(jnp.int32, x.shape, 0)
    ones = jnp.where(rows < 3, 1.0, 0.0).astype(bf16)
    z1 = mm(w1s[...], jnp.concatenate([xh, xl, xh, ones], axis=0))
    h1h, h1l = split(jnp.maximum(z1, 0.0))
    z2 = mm(w2f[...], jnp.concatenate([h1h, h1l, h1h], axis=0))
    z2 = z2 + cols[:, 3 * feat + 3 : 3 * feat + 4]
    h2h, h2l = split(jnp.maximum(z2, 0.0))
    both = mm(w3f[...], h2h)
    raw = both[0:PAD] + both[PAD:] + mm(w3f[0:PAD, :], h2l)
    raw = raw + cols[0:PAD, 3 * feat + 4 : 3 * feat + 5]
    out = []
    for n in range(len(spacing)):
        keep_x[n][0] = columns(xh, n, wide)
        keep_x[n][1] = columns(xl, n, wide)
        keep_h[n][0] = columns(h1h, n, wide)
        keep_h[n][1] = columns(h2h, n, wide)
        own = columns(raw, n, wide)
        shown = jax.nn.sigmoid(own[0:channels])
        keep_raw[n][0:channels] = shown
        keep_raw[n][channels:PAD] = own[channels:PAD]
        before = None
        color = None
        for s, (_, optical, _) in enumerate(opticals(own, channels, spacing[n], counts[n], samples, rays)):
            weight = 1.0 - jnp.exp(-optical)
            if s:
                weight = jnp.exp(-before) * weight
            shade = weight * shown[:, s * rays : (s + 1) * rays]
            color = shade if s == 0 else color + shade
            before = optical if s == 0 else before + optical
        out.append((color, before))
    return out


def raw_grad(channels, raw, misfit, state, spacing, counts):
    samples = len(spacing)
    rays = spacing[0].shape[1]
    passed = state[0:1]
    parts = opticals(raw, channels, spacing, counts, samples, rays)
    befores, before = [], None
    for s in range(samples):
        befores.append(before)
        before = parts[s][1] if s == 0 else before + parts[s][1]
    tail = -state[1:2]
    pieces = [None] * samples
    for s in reversed(range(samples)):
        logit, optical, length = parts[s]
        gone = jnp.exp(-optical)
        ahead = 1.0 if s == 0 else jnp.exp(-befores[s])
        weight = ahead * (1.0 - gone)
        color = raw[0:channels, s * rays : (s + 1) * rays]
        weight_grad = passed * jnp.sum(misfit * color, axis=0, keepdims=True)
        optical_grad = weight_grad * (ahead * gone) + tail
        tail = tail - weight_grad * weight
        color_grad = (weight * passed) * misfit * (color * (1.0 - color))
        logit_grad = optical_grad * length * jax.nn.sigmoid(logit)
        row = lax.broadcasted_iota(jnp.int32, (PAD - channels, rays), 0)
        rest = jnp.where(row == 0, jnp.broadcast_to(logit_grad, row.shape), 0.0)
        pieces[s] = jnp.concatenate([color_grad, rest], axis=0)
    return pieces


def backward_tile(channels, raws, misfits, states, spacing, counts, keep_h, w3b, acc2, acc3, bias):
    pieces = []
    for at in zip(raws, misfits, states, spacing, counts):
        pieces += raw_grad(channels, *at)
    draw = jnp.concatenate(pieces, axis=1)
    bias[0:PAD, :] += lanes(draw)
    dh, dl = split(draw)
    h2h = jnp.concatenate([keep[1] for keep in keep_h], axis=1)
    acc3[...] += mm_nt(dh, h2h)
    zero = jnp.zeros((256 - 3 * PAD, draw.shape[1]), bf16)
    dh2 = mm(w3b[...], jnp.concatenate([dh, dl, dh, zero], axis=0))
    zh = jnp.where(h2h > 0, dh2.astype(bf16), jnp.zeros_like(h2h))
    h1h = jnp.concatenate([keep[0] for keep in keep_h], axis=1)
    acc2[...] += mm_nt(jnp.concatenate([h1h, jnp.ones((16, h1h.shape[1]), bf16)], axis=0), zh)
    wide = zh.shape[1] // len(keep_h)
    for n, keep in enumerate(keep_h):
        keep[1] = columns(zh, n, wide)


def first_layer_tile(keep_x, keep_h, w2b, acc1):
    h1h = jnp.concatenate([keep[0] for keep in keep_h], axis=1)
    zh = jnp.concatenate([keep[1] for keep in keep_h], axis=1)
    dh1 = mm(w2b[...], jnp.concatenate([zh, zh], axis=0))
    zh = jnp.where(h1h > 0, dh1.astype(bf16), jnp.zeros_like(h1h))
    x = [jnp.concatenate([keep[i] for keep in keep_x], axis=1) for i in (0, 1)]
    x.append(jnp.ones((16, zh.shape[1]), bf16))
    acc1[...] += mm_nt(jnp.concatenate(x, axis=0), zh)


def step_kernel(
    views, regions,
    feats_in, spacing_in, counts_in, target_in, rank_ref, w1_in, b1_in, w2_in, b2_in, w3_in, b3_in,
    pixels, total, total_late,
    feats, spacing, counts, target, w1, b1, w2, b2, w3, b3, load_sem,
    w1s, w2f, w2b, w3f, w3b, cols, keep_x, keep_h, keep_raw, back, grads, grads_late,
    acc1, acc2, acc3, bias, fsend, frecv, msend, mrecv, nsend, nrecv, gsend, grecv, lsend, lrecv,
    *scratch,
):
    samples, feat, rays = feats.shape
    channels, seg = target.shape
    levels = regions.bit_length() - 1
    rows = back.shape[1]
    hidden = w2.shape[0]
    me = lax.axis_index("depth")
    view = lax.axis_index("view")
    work = scratch[0 : levels + 1]
    got = scratch[levels + 1 : 2 * levels + 1]
    notes = scratch[2 * levels + 1 : 3 * levels + 1]
    sums = scratch[3 * levels + 1 :]

    def bit_of(value, b):
        return lax.rem(value // (1 << b), 2)

    def partner(b):
        return {"depth": me + (1 - 2 * bit_of(me, b)) * (1 << b)}

    loads = [
        pltpu.make_async_copy(source, place, load_sem.at[n])
        for n, (source, place) in enumerate(
            (
                (w1_in, w1), (b1_in, b1), (w2_in, w2), (b2_in, b2), (w3_in, w3), (b3_in, b3),
                (feats_in, feats), (spacing_in, spacing), (counts_in, counts), (target_in, target),
            )
        )
    ]
    for load in loads:
        load.start()
    barrier = pltpu.get_barrier_semaphore()
    greeted = [(a, r) for a in range(views) for r in range(regions) if r == 0 or a % 2 == 0][1:]
    for a, r in greeted:
        where = {"view": lax.rem(view + a, views), "depth": lax.rem(me + r, regions)}
        pl.semaphore_signal(barrier, inc=1, device_id=where, device_id_type=MESH)

    for load in loads[:6]:
        load.wait()
    prepare(feat, w1, b1, w2, b2, w3, b3, w1s, w2f, w2b, w3f, w3b, cols)
    for load in loads[6:]:
        load.wait()

    parts = min(PARTS, seg // 128)
    wide = seg // parts

    def span_of(h, k):
        where = 0
        for b in range(levels):
            where = where + lax.rem(bit_of(me, b) + bit_of(k, levels - 1 - b), 2) * (1 << b)
        return pl.ds(pl.multiple_of(where * seg + h * wide, wide), wide)

    rank = rank_ref[0:1, 0:1]
    row = lax.broadcasted_iota(jnp.int32, (rows - channels, wide), 0)

    def first(b):
        return lax.rem(lax.div(rank, jnp.full_like(rank, 1 << b)), jnp.full_like(rank, 2)) == 0

    def halves(k):
        return [(j, regions >> (j + 1)) for j in range(levels) if k < regions >> (j + 1)]

    def color_copy(j, h, kk):
        n2 = regions >> (j + 1)
        return remote(
            work[j].at[h * 2 * n2 + n2 + kk], got[j].at[h * n2 + kk],
            (fsend, frecv), h * regions + n2 + kk, partner(j),
        )

    def misfit_copy(j, h, kk):
        n2 = regions >> (j + 1)
        part = pl.ds(0, channels)
        return remote(
            back.at[h * regions + kk, part], back.at[h * regions + n2 + kk, part],
            (msend, mrecv), h * regions + n2 + kk, partner(j),
        )

    def note_copy(j, h, kk):
        n2 = regions >> (j + 1)
        return remote(
            notes[j].at[h * n2 + kk], back.at[h * regions + n2 + kk, pl.ds(channels, rows - channels)],
            (nsend, nrecv), h * regions + n2 + kk, partner(j),
        )

    def gather_x(span):
        return jnp.concatenate([feats[s, :, span] for s in range(samples)], axis=1)

    def fold(h, k):
        for j, n2 in halves(k):
            color_copy(j, h, k).wait_recv()
            ahead = first(j)
            mine, other = work[j][h * 2 * n2 + k], got[j][h * n2 + k]
            mine_depth = mine[channels : channels + 1]
            other_depth = other[channels : channels + 1]
            mine_clear = jnp.where(ahead, 1.0, jnp.exp(-other_depth))
            other_clear = jnp.where(ahead, jnp.exp(-mine_depth), 1.0)
            at = h * n2 + k
            work[j + 1][at, 0:channels] = mine_clear * mine[0:channels] + other_clear * other[0:channels]
            work[j + 1][at, channels:rows] = mine[channels:rows] + other[channels:rows]
        if k:
            j = levels - k.bit_length()
            color_copy(j, h, k - (regions >> (j + 1))).start()

    def tell(h, k):
        at = h * regions + k
        if k == 0:
            span = pl.ds(h * wide, wide)
            color = work[levels][h, 0:channels]
            pixels[:, span] = color
            back[at, 0:channels] = color - target[:, span]
            back[at, channels:rows] = jnp.where(row == 0, 1.0, 0.0)
        else:
            j = levels - k.bit_length()
            misfit_copy(j, h, k - (regions >> (j + 1))).wait_recv()
        for j, n2 in reversed(halves(k)):
            misfit_copy(j, h, k).start()
        if k:
            j = levels - k.bit_length()
            note_copy(j, h, k - (regions >> (j + 1))).wait_recv()
        for j, n2 in reversed(halves(k)):
            ahead = first(j)
            mine, other = work[j][h * 2 * n2 + k], got[j][h * n2 + k]
            misfit = back[at, 0:channels]
            state = back[at, channels:rows]
            passed, behind = state[0:1], state[1:2]
            mine_depth = mine[channels : channels + 1]
            other_depth = other[channels : channels + 1]
            hind = jnp.where(ahead, other[0:channels], mine[0:channels])
            later = passed * jnp.exp(-jnp.where(ahead, mine_depth, other_depth))
            glow = behind + later * jnp.sum(misfit * hind, axis=0, keepdims=True)
            mine_state = (jnp.where(ahead, passed, later), jnp.where(ahead, glow, behind))
            other_state = (jnp.where(ahead, later, passed), jnp.where(ahead, behind, glow))
            notes[j][h * n2 + k] = jnp.where(row == 0, *other_state)
            note_copy(j, h, k).start()
            back[at, channels:rows] = jnp.where(row == 0, *mine_state)

    plan = make_plan(regions, parts)
    half = regions // 2
    tiles = [at for what, at in plan if what == "forward"]
    passes, events = [], {}
    ready = 0
    for what, at in plan:
        if what == "forward":
            ready += 1
        elif what in ("backward", "first"):
            passes.append((what, at))
        elif at[0][1] < half:
            key = ("ahead", ready - 1) if ready < len(tiles) else ("back", len(passes))
            events.setdefault(key, []).append((fold if what == "fold" else tell,) + at[0])
    last = max(n for n, at in enumerate(passes) if at[0] == "backward")
    passes, lasts = passes[: last + 1], [at for _, at in passes[last + 1 :]]

    def pick_tiles(i, table):
        out = []
        for n in range(parts):
            h = pick(i, [at[n][0] for at in table])
            k = pick(i, [at[n][1] for at in table])
            out.append((h, k, h * regions + k))
        return out

    def lengths(span):
        return [spacing[s, :, span] for s in range(samples)]

    def run_events(name, i):
        for (kind, at), calls in events.items():
            if kind == name:

                @pl.when(i == at)
                def _():
                    for call, h, k in calls:
                        call(h, k)

    def forward_step(i, carry):
        pair = pick_tiles(i, tiles)
        spans = [span_of(h, k) for h, k, _ in pair]
        results = forward_tile(
            feat, channels, jnp.concatenate([gather_x(span) for span in spans], axis=1),
            [lengths(span) for span in spans], [counts[:, span] for span in spans], w1s, w2f, w3f, cols,
            [keep_x.at[at] for _, _, at in pair], [keep_h.at[at] for _, _, at in pair],
            [keep_raw.at[at] for _, _, at in pair],
        )
        for (_, _, at), (color, depth) in zip(pair, results):
            work[0][at, 0:channels] = color
            work[0][at, channels:rows] = jnp.broadcast_to(depth, (rows - channels, wide))

        @pl.when(i == 0)
        def _():
            pl.semaphore_wait(barrier, len(greeted))

        for h, k, _ in pair:

            @pl.when(k >= half)
            def _():
                color_copy(0, h, k - half).start()

        run_events("ahead", i)
        return carry

    lax.fori_loop(0, len(tiles), forward_step, 0)
    for acc in (acc1, acc2, acc3, bias):
        acc[...] = jnp.zeros_like(acc)

    def backward_step(i, carry):
        run_events("back", i)
        pair = pick_tiles(i, [at[1] for at in passes])
        turn = pick(i, [int(at[0] == "backward") for at in passes])
        for h, k, _ in pair:

            @pl.when((turn == 1) & (k >= half))
            def _():
                misfit_copy(0, h, k - half).wait_recv()
                note_copy(0, h, k - half).wait_recv()

        @pl.when(turn == 1)
        def _():
            spans = [span_of(h, k) for h, k, _ in pair]
            backward_tile(
                channels, [keep_raw.at[at] for _, _, at in pair],
                [back[at, 0:channels] for _, _, at in pair], [back[at, channels:rows] for _, _, at in pair],
                [lengths(span) for span in spans], [counts[:, span] for span in spans],
                [keep_h.at[at] for _, _, at in pair], w3b, acc2, acc3, bias,
            )

        @pl.when(turn == 0)
        def _():
            first_layer_tile(
                [keep_x.at[at] for _, _, at in pair], [keep_h.at[at] for _, _, at in pair], w2b, acc1
            )

        return carry

    lax.fori_loop(0, len(passes), backward_step, 0)
    early = wide_stages(views, regions, grads, total, *sums[0:3], (gsend, grecv))
    late = small_stages(views, regions, grads_late, total_late, *sums[3:5], (lsend, lrecv))
    fill_blocks(grads, acc2, acc3, bias)
    early[0]()

    def first_layer_step(i, carry):
        pair = pick_tiles(i, lasts)
        first_layer_tile(
            [keep_x.at[at] for _, _, at in pair], [keep_h.at[at] for _, _, at in pair], w2b, acc1
        )

        @pl.when(i == min(1, len(lasts) - 1))
        def _():
            early[1]()

        return carry

    lax.fori_loop(0, len(lasts), first_layer_step, 0)
    fill_rows(grads_late, acc1, feat)
    early = early[2:]
    for which in "LLELLEE":
        (early if which == "E" else late).pop(0)()
    for h in range(parts):
        for j in range(levels):
            for kk in range(regions >> (j + 1)):
                color_copy(j, h, kk).wait_send()
                misfit_copy(j, h, kk).wait_send()
                note_copy(j, h, kk).wait_send()
    for close in early + late:
        close()


def whole_step(views, regions, feats, spacing, counts, target, rank, weights):
    samples, feat, rays = feats.shape
    channels, seg = target.shape
    hidden = weights[2].shape[0]
    levels = regions.bit_length() - 1
    rows = channels + 8
    parts = min(PARTS, seg // 128)
    tiles = parts * regions
    seg = seg // parts
    wide = samples * seg
    across = hidden // 128
    pairs = views // 2 * regions
    sizes = block_counts(feat, hidden, views, regions)
    inputs = (feats, spacing, counts, target) + tuple(weights)
    scratch = [pltpu.VMEM(value.shape, value.dtype) for value in inputs]
    scratch.append(pltpu.SemaphoreType.DMA((len(inputs),)))
    scratch += [
        pltpu.VMEM((hidden, 128), bf16),
        pltpu.VMEM((hidden, 3 * hidden), bf16),
        pltpu.VMEM((hidden, 2 * hidden), bf16),
        pltpu.VMEM((2 * PAD, hidden), bf16),
        pltpu.VMEM((hidden, 256), bf16),
        pltpu.VMEM((hidden, hidden), f32),
        pltpu.VMEM((tiles, 2, feat, wide), bf16),
        pltpu.VMEM((tiles, 2, hidden, wide), bf16),
        pltpu.VMEM((tiles, PAD, wide), f32),
        pltpu.VMEM((tiles, rows, seg), f32),
        pltpu.VMEM((sizes[0], 8, 128), f32),
        pltpu.VMEM((sizes[1], across, 128), f32),
        pltpu.VMEM((2 * feat + 16, hidden), f32),
        pltpu.VMEM((hidden + 16, hidden), f32),
        pltpu.VMEM((PAD, hidden), f32),
        pltpu.VMEM((PAD, 128), f32),
    ]
    scratch += [pltpu.SemaphoreType.DMA((tiles,))] * 6
    scratch += [pltpu.SemaphoreType.DMA((2 * pairs,))] * 2
    scratch += [pltpu.SemaphoreType.DMA((2 * regions + views - 3,))] * 2
    scratch += [pltpu.VMEM((tiles >> j, rows, seg), f32) for j in range(levels + 1)]
    scratch += [pltpu.VMEM((tiles >> (j + 1), rows, seg), f32) for j in range(levels)]
    scratch += [pltpu.VMEM((tiles >> (j + 1), 8, seg), f32) for j in range(levels)]
    half = sizes[0] // 2
    scratch += [pltpu.VMEM((half, 8, 128), f32)] * 2
    scratch.append(pltpu.VMEM((pairs - 1, half // pairs, 8, 128), f32))
    part = sizes[1] // regions
    scratch.append(pltpu.VMEM((regions - 1, part, across, 128), f32))
    scratch.append(pltpu.VMEM((views, part, across, 128), f32))
    vmem = pl.BlockSpec(memory_space=pltpu.VMEM)
    hbm = pl.BlockSpec(memory_space=pltpu.HBM)
    return pl.pallas_call(
        functools.partial(step_kernel, views, regions),
        in_specs=[hbm] * 4 + [vmem] + [hbm] * 6,
        out_specs=[vmem] * 3,
        out_shape=[
            jax.ShapeDtypeStruct(target.shape, f32),
            jax.ShapeDtypeStruct((sizes[0], 8, 128), f32),
            jax.ShapeDtypeStruct((sizes[1], across, 128), f32),
        ],
        scratch_shapes=scratch,
        compiler_params=pltpu.CompilerParams(
            collective_id=0, has_side_effects=True, vmem_limit_bytes=66000000
        ),
        name="whole_step",
    )(feats, spacing, counts, target, rank, *weights)


def finish_kernel(
    feat, hidden, outs,
    pixels_in, total, late,
    pixels, first_update, first_shift, second_update, second_shift, last_update, last_shift,
):
    def scaled(value, count):
        square = jnp.sum(jnp.sum(value * value, axis=0, keepdims=True), axis=1, keepdims=True)
        return value / jnp.sqrt(square / count + epsilon)

    pixels[...] = pixels_in[...]

    def join(source, at, rows):
        halves = []
        for _ in range(0, hidden, 128):
            halves.append(source[at : at + rows // 8].reshape(rows, 128))
            at += rows // 8
        return jnp.concatenate(halves, axis=1), at

    second, at = join(total, 0, hidden)
    last, at = join(total, at, PAD)
    across = hidden // 128
    first = jnp.concatenate([late[0:feat, i, :] for i in range(across)], axis=1)
    second_update[...] = scaled(second, hidden * hidden)
    first_update[...] = scaled(first, feat * hidden)
    last_update[...] = scaled(last, hidden * outs)[0:outs]
    rows = total[at]
    late_rows = late[feat]
    wide = lambda rows: jnp.concatenate([rows[i : i + 1] for i in range(across)], axis=1)
    first_shift[...] = scaled(wide(late_rows), hidden)
    second_shift[...] = scaled(wide(rows), hidden)
    last_shift[...] = scaled(rows[across : across + 1], outs)[:, 0:outs]


def finish(pixels, total, late, feat, hidden, outs):
    vmem = pl.BlockSpec(memory_space=pltpu.VMEM)
    shapes = [
        pixels.shape, (feat, hidden), (1, hidden), (hidden, hidden), (1, hidden),
        (outs, hidden), (1, outs),
    ]
    return pl.pallas_call(
        functools.partial(finish_kernel, feat, hidden, outs),
        in_specs=[vmem] * 3,
        out_specs=[vmem] * len(shapes),
        out_shape=[jax.ShapeDtypeStruct(shape, f32) for shape in shapes],
        name="normalize_all",
    )(pixels, total, late)


def local(
    features, spacing, counts, depth_rank, target,
    first_weight, first_bias, second_weight, second_bias, last_weight, last_bias,
):
    regions = lax.axis_size("depth")
    views = lax.axis_size("view")
    feat, hidden = first_weight.shape
    outs = last_weight.shape[1]
    feats, gaps, live = jnp.transpose(features[0, 0], (1, 0, 2)), jnp.transpose(spacing[0], (1, 0, 2)), counts[0]
    weights = (
        first_weight, first_bias[None], second_weight, second_bias[None],
        last_weight.T, last_bias[None],
    )
    pixels, total, late = whole_step(views, regions, feats, gaps, live, target[0], depth_rank, weights)
    results = finish(pixels, total, late, feat, hidden, outs)
    return (
        results[0][None], results[1], results[2][0], results[3], results[4][0],
        results[5].T, results[6][0],
    )


def solution(mesh):
    return jax.shard_map(
        local,
        mesh=mesh,
        in_specs=(
            P("view", "depth", None, None, None),
            P("view", "depth", None, None),
            P("view", "depth", None),
            P("view", "depth"),
            P("view", None, "depth"),
            P(), P(), P(), P(), P(), P(),
        ),
        out_specs=(P("view", None, "depth"), P(), P(), P(), P(), P(), P()),
        check_vma=False,
    )
```

```python
import functools

import jax
import jax.numpy as jnp
from jax import lax
from jax.experimental import pallas as pl
from jax.experimental.pallas import tpu as pltpu
from jax.sharding import PartitionSpec as P

epsilon = 1e-05
PAD = 80
PARTS = 2
TURN = ((14, 8, 2, 4, 10, 3, 5, 0), (15, 11, 13, 6, 12, 7, 9, 1))
MESH = pl.DeviceIdType.MESH
f32 = jnp.float32
bf16 = jnp.bfloat16


def split(value):
    high = value.astype(bf16)
    low = (value - high.astype(f32)).astype(bf16)
    return high, low


def mm(left, right):
    return lax.dot_general(left, right, (((1,), (0,)), ((), ())), preferred_element_type=f32)


def mm_nt(left, right):
    return lax.dot_general(left, right, (((1,), (1,)), ((), ())), preferred_element_type=f32)


def opticals(raw, channels, spacing, counts, samples, rays):
    out = []
    for s in range(samples):
        logit = raw[channels : channels + 1, s * rays : (s + 1) * rays]
        density = jnp.maximum(logit, 0.0) + jnp.log1p(jnp.exp(-jnp.abs(logit)))
        length = jnp.where(s < counts, spacing[s], 0.0)
        out.append((logit, density * length, length))
    return out


def remote(src, dst, sems, slot, device):
    return pltpu.make_async_remote_copy(
        src_ref=src,
        dst_ref=dst,
        send_sem=sems[0].at[slot],
        recv_sem=sems[1].at[slot],
        device_id=device,
        device_id_type=MESH,
    )


def lanes(value):
    total = value[:, 0:128]
    for lane in range(128, value.shape[1], 128):
        total = total + value[:, lane : lane + 128]
    return total


def round_up(blocks, devices):
    return -(-blocks // devices) * devices


def block_counts(feat, hidden, views, regions):
    early = (hidden + PAD) // 8 * (hidden // 128) + 1
    return round_up(early, views * regions), round_up(feat + 1, regions)


def fill_blocks(grads, acc2, acc3, bias):
    hidden = acc2.shape[1]
    at = 0
    for acc, blocks in ((acc2, hidden // 8), (acc3, acc3.shape[0] // 8)):
        for lane in range(0, hidden, 128):
            grads[at : at + blocks] = acc[0 : blocks * 8, lane : lane + 128].reshape(blocks, 8, 128)
            at += blocks
    grads[at:] = jnp.zeros((grads.shape[0] - at, 8, 128), f32)
    for i, lane in enumerate(range(0, hidden, 128)):
        grads[at, i : i + 1, :] = acc2[hidden : hidden + 1, lane : lane + 128]
    tall = jnp.concatenate([bias[...], jnp.zeros((128 - bias.shape[0], 128), f32)], axis=0)
    grads[at, hidden // 128 : hidden // 128 + 1, :] = jnp.sum(tall.T, axis=0, keepdims=True)


def fill_rows(grads, acc, feat):
    grads[feat:] = jnp.zeros((grads.shape[0] - feat,) + grads.shape[1:], f32)
    for i, lane in enumerate(range(0, acc.shape[1], 128)):
        part = slice(lane, lane + 128)
        grads[0:feat, i, :] = acc[0:feat, part] + acc[feat : 2 * feat, part]
        grads[feat, i : i + 1, :] = acc[2 * feat : 2 * feat + 1, part]


def stages(moves):
    def stage(n):
        if n > 0:
            copies, after = moves[n - 1]
            for copy in copies():
                copy.wait_recv()
            if after is not None:
                after()
        if n < len(moves):
            for copy in moves[n][0]():
                copy.start()

    def close():
        for copies, _ in moves:
            for copy in copies():
                copy.wait_send()

    return [functools.partial(stage, n) for n in range(len(moves) + 1)] + [close]


def wide_stages(views, regions, grads, total, came, held, landing, sems):
    me = lax.axis_index("depth")
    view = lax.axis_index("view")
    pairs = views // 2
    half = grads.shape[0] // 2
    piece = half // (pairs * regions)
    core = lax.rem(view, 2)
    chip = view // 2
    partner = {"view": view + 1 - 2 * core}
    others = [(a, r) for a in range(pairs) for r in range(regions)][1:]

    def other(a, r):
        return lax.rem(chip + a, pairs), lax.rem(me + r, regions)

    def device(a, r):
        pair, depth = other(a, r)
        return {"view": pair * 2 + core, "depth": depth}

    def swap_half():
        return [remote(grads.at[pl.ds((1 - core) * half, half)], came, sems, 0, partner)]

    def add_half():
        held[...] = grads[pl.ds(core * half, half)] + came[...]

    def scatter():
        out = []
        for n, (a, r) in enumerate(others):
            pair, depth = other(a, r)
            part = held.at[pl.ds((pair * regions + depth) * piece, piece)]
            out.append(remote(part, landing.at[n], sems, 1 + n, device(a, r)))
        return out

    def mine():
        return pl.ds(core * half + (chip * regions + me) * piece, piece)

    def add_pieces():
        value = held[pl.ds((chip * regions + me) * piece, piece)]
        for n in range(len(others)):
            value = value + landing[n]
        total[mine()] = value

    def gather():
        part = total.at[mine()]
        first = 1 + len(others)
        return [remote(part, part, sems, first + n, device(a, r)) for n, (a, r) in enumerate(others)]

    def gather_half():
        part = total.at[pl.ds(core * half, half)]
        return [remote(part, part, sems, 1 + 2 * len(others), partner)]

    return stages([(swap_half, add_half), (scatter, add_pieces), (gather, None), (gather_half, None)])


def small_stages(views, regions, grads, total, landing, slots, sems):
    me = lax.axis_index("depth")
    view = lax.axis_index("view")
    piece = grads.shape[0] // regions

    def peer(r):
        return {"depth": lax.rem(me + r, regions)}

    def scatter():
        return [
            remote(
                grads.at[pl.ds(lax.rem(me + r, regions) * piece, piece)],
                landing.at[r - 1], sems, r - 1, peer(r),
            )
            for r in range(1, regions)
        ]

    def add_depth():
        value = grads[pl.ds(me * piece, piece)]
        for r in range(1, regions):
            value = value + landing[r - 1]
        slots[view] = value

    def exchange():
        part = slots.at[view]
        return [
            remote(part, part, sems, regions - 2 + a, {"view": lax.rem(view + a, views)})
            for a in range(1, views)
        ]

    def add_view():
        value = slots[0]
        for a in range(1, views):
            value = value + slots[a]
        total[pl.ds(me * piece, piece)] = value

    def gather():
        part = total.at[pl.ds(me * piece, piece)]
        first = regions + views - 3
        return [remote(part, part, sems, first + r, peer(r)) for r in range(1, regions)]

    return stages([(scatter, add_depth), (exchange, add_view), (gather, None)])


def make_plan(regions, parts):
    levels = regions.bit_length() - 1
    ahead, back, first = 1.5, 1.1, 0.7
    group = parts
    load = [1.8 / parts * (1 if j < 2 else 1.8) for j in range(levels)]
    lag = [1.5 + 0.3 * (j > 1) for j in range(levels)]
    free = [0.0] * levels
    clock = 0.0
    came = {}
    left = forward_order(regions, parts)
    done, ended, shown, told, walked, closed = [], set(), {}, [], [], []
    steps = []

    def halves(k):
        return [(j, regions >> (j + 1)) for j in range(levels) if k < regions >> (j + 1)]

    def send(j, key):
        free[j] = max(free[j], clock) + load[j]
        came[key] = free[j] + lag[j]

    while len(closed) < parts * regions:
        choices = []
        for h, k in done:
            needs = [came.get(("color", h, k + n2)) for _, n2 in halves(k)]
            if (h, k) not in ended and None not in needs:
                choices.append((max([clock] + needs), 0, h, -k, "fold", [(h, k)]))
        for h in range(parts):
            for k in range(regions):
                when = shown.get(h) if k == 0 else came.get(("misfit", h, k))
                if when is not None and (h, k) not in told:
                    choices.append((max(clock, when), 1, h, k, "tell", [(h, k)]))
        if left:
            choices.append((clock, 2, 0, 0, "forward", left[:group]))
        open_tiles = [at for at in told if at not in walked]
        if len(open_tiles) >= group:
            choices.append((clock, 3, 0, 0, "backward", open_tiles[:group]))
        open_tiles = [at for at in walked if at not in closed]
        if len(open_tiles) >= group:
            choices.append((clock, 4, 0, 0, "first", open_tiles[:group]))
        when, _, _, _, what, tiles = min(choices)
        clock = max(clock, when)
        steps.append((what, tiles))
        h, k = tiles[0]
        if what == "forward":
            clock += ahead
            done += tiles
            left = left[group:]
        elif what == "fold":
            clock += 0.1 * len(halves(k))
            ended.add((h, k))
            if k == 0:
                shown[h] = clock
            else:
                j = levels - k.bit_length()
                send(j, ("color", h, k))
        elif what == "tell":
            told.append((h, k))
            for j, n2 in reversed(halves(k)):
                clock += 0.1
                send(j, ("misfit", h, k + n2))
        elif what == "backward":
            clock += back
            walked += tiles
        else:
            clock += first
            closed += tiles
    return steps


def forward_order(regions, parts):
    tiles = [(h, k) for h in range(parts) for k in range(regions)]
    return sorted(tiles, key=lambda at: (TURN[at[0]][at[1] * len(TURN[0]) // regions], -at[1]))


def pick(i, values):
    out = 0
    for at, value in enumerate(values):
        if value:
            out = out + jnp.where(i == at, value, 0)
    return out


def prepare(feat, w1_ref, b1_ref, w2_ref, b2_ref, w3_ref, b3_ref, w1s, w2f, w2b, w3f, w3b, cols):
    hidden = w2_ref.shape[0]
    outs = w3_ref.shape[0]
    high, low = split(w1_ref[...])
    bias = b1_ref[...]
    bias_a = bias.astype(bf16).astype(f32)
    bias_b = (bias - bias_a).astype(bf16).astype(f32)
    cols[...] = jnp.zeros_like(cols)
    cols[0:feat, :] = high.astype(f32)
    cols[feat : 2 * feat, :] = high.astype(f32)
    cols[2 * feat : 3 * feat, :] = low.astype(f32)
    cols[3 * feat : 3 * feat + 1, :] = bias_a
    cols[3 * feat + 1 : 3 * feat + 2, :] = bias_b
    cols[3 * feat + 2 : 3 * feat + 3, :] = bias - bias_a - bias_b
    cols[3 * feat + 3 : 3 * feat + 4, :] = b2_ref[...]
    cols[3 * feat + 4 : 3 * feat + 5, 0:outs] = b3_ref[...]
    turned = cols[0:128, :].T
    w1s[...] = turned.astype(bf16)
    cols[:, 0:128] = turned
    high, low = split(w2_ref[...].T)
    w2f[:, 0:hidden] = high
    w2f[:, hidden : 2 * hidden] = high
    w2f[:, 2 * hidden : 3 * hidden] = low
    high, low = split(w2_ref[...])
    w2b[:, 0:hidden] = high
    w2b[:, hidden : 2 * hidden] = low
    tall = jnp.concatenate([w3_ref[...], jnp.zeros((PAD - outs, hidden), f32)], axis=0)
    high, low = split(tall)
    w3f[0:PAD, :] = high
    w3f[PAD : 2 * PAD, :] = low
    high = high.astype(f32)
    stack = jnp.concatenate(
        [high, high, tall - high, jnp.zeros((256 - 3 * PAD, hidden), f32)], axis=0
    )
    w3b[...] = stack.T.astype(bf16)


def columns(value, n, wide):
    return value[:, n * wide : (n + 1) * wide]


def forward_tile(feat, channels, x, spacing, counts, w1s, w2f, w3f, cols, keep_x, keep_h, keep_raw):
    samples = len(spacing[0])
    rays = spacing[0][0].shape[1]
    wide = samples * rays
    xh, xl = split(x)
    rows = lax.broadcasted_iota(jnp.int32, x.shape, 0)
    ones = jnp.where(rows < 3, 1.0, 0.0).astype(bf16)
    z1 = mm(w1s[...], jnp.concatenate([xh, xl, xh, ones], axis=0))
    h1h, h1l = split(jnp.maximum(z1, 0.0))
    z2 = mm(w2f[...], jnp.concatenate([h1h, h1l, h1h], axis=0))
    z2 = z2 + cols[:, 3 * feat + 3 : 3 * feat + 4]
    h2h, h2l = split(jnp.maximum(z2, 0.0))
    both = mm(w3f[...], h2h)
    raw = both[0:PAD] + both[PAD:] + mm(w3f[0:PAD, :], h2l)
    raw = raw + cols[0:PAD, 3 * feat + 4 : 3 * feat + 5]
    out = []
    for n in range(len(spacing)):
        keep_x[n][0] = columns(xh, n, wide)
        keep_x[n][1] = columns(xl, n, wide)
        keep_h[n][0] = columns(h1h, n, wide)
        keep_h[n][1] = columns(h2h, n, wide)
        own = columns(raw, n, wide)
        shown = jax.nn.sigmoid(own[0:channels])
        keep_raw[n][0:channels] = shown
        keep_raw[n][channels:PAD] = own[channels:PAD]
        before = None
        color = None
        for s, (_, optical, _) in enumerate(opticals(own, channels, spacing[n], counts[n], samples, rays)):
            weight = 1.0 - jnp.exp(-optical)
            if s:
                weight = jnp.exp(-before) * weight
            shade = weight * shown[:, s * rays : (s + 1) * rays]
            color = shade if s == 0 else color + shade
            before = optical if s == 0 else before + optical
        out.append((color, before))
    return out


def raw_grad(channels, raw, misfit, state, spacing, counts):
    samples = len(spacing)
    rays = spacing[0].shape[1]
    passed = state[0:1]
    parts = opticals(raw, channels, spacing, counts, samples, rays)
    befores, before = [], None
    for s in range(samples):
        befores.append(before)
        before = parts[s][1] if s == 0 else before + parts[s][1]
    tail = -state[1:2]
    pieces = [None] * samples
    for s in reversed(range(samples)):
        logit, optical, length = parts[s]
        gone = jnp.exp(-optical)
        ahead = 1.0 if s == 0 else jnp.exp(-befores[s])
        weight = ahead * (1.0 - gone)
        color = raw[0:channels, s * rays : (s + 1) * rays]
        weight_grad = passed * jnp.sum(misfit * color, axis=0, keepdims=True)
        optical_grad = weight_grad * (ahead * gone) + tail
        tail = tail - weight_grad * weight
        color_grad = (weight * passed) * misfit * (color * (1.0 - color))
        logit_grad = optical_grad * length * jax.nn.sigmoid(logit)
        row = lax.broadcasted_iota(jnp.int32, (PAD - channels, rays), 0)
        rest = jnp.where(row == 0, jnp.broadcast_to(logit_grad, row.shape), 0.0)
        pieces[s] = jnp.concatenate([color_grad, rest], axis=0)
    return pieces


def backward_tile(channels, raws, misfits, states, spacing, counts, keep_h, w3b, acc2, acc3, bias):
    pieces = []
    for at in zip(raws, misfits, states, spacing, counts):
        pieces += raw_grad(channels, *at)
    draw = jnp.concatenate(pieces, axis=1)
    bias[0:PAD, :] += lanes(draw)
    dh, dl = split(draw)
    h2h = jnp.concatenate([keep[1] for keep in keep_h], axis=1)
    acc3[...] += mm_nt(dh, h2h)
    zero = jnp.zeros((256 - 3 * PAD, draw.shape[1]), bf16)
    dh2 = mm(w3b[...], jnp.concatenate([dh, dl, dh, zero], axis=0))
    zh = jnp.where(h2h > 0, dh2.astype(bf16), jnp.zeros_like(h2h))
    h1h = jnp.concatenate([keep[0] for keep in keep_h], axis=1)
    acc2[...] += mm_nt(jnp.concatenate([h1h, jnp.ones((16, h1h.shape[1]), bf16)], axis=0), zh)
    wide = zh.shape[1] // len(keep_h)
    for n, keep in enumerate(keep_h):
        keep[1] = columns(zh, n, wide)


def first_layer_tile(keep_x, keep_h, w2b, acc1):
    h1h = jnp.concatenate([keep[0] for keep in keep_h], axis=1)
    zh = jnp.concatenate([keep[1] for keep in keep_h], axis=1)
    dh1 = mm(w2b[...], jnp.concatenate([zh, zh], axis=0))
    zh = jnp.where(h1h > 0, dh1.astype(bf16), jnp.zeros_like(h1h))
    x = [jnp.concatenate([keep[i] for keep in keep_x], axis=1) for i in (0, 1)]
    x.append(jnp.ones((16, zh.shape[1]), bf16))
    acc1[...] += mm_nt(jnp.concatenate(x, axis=0), zh)


def step_kernel(
    views, regions,
    feats_in, spacing_in, counts_in, target_in, rank_ref, w1_in, b1_in, w2_in, b2_in, w3_in, b3_in,
    pixels, total, total_late,
    feats, spacing, counts, target, w1, b1, w2, b2, w3, b3, load_sem,
    w1s, w2f, w2b, w3f, w3b, cols, keep_x, keep_h, keep_raw, back, grads, grads_late,
    acc1, acc2, acc3, bias, fsend, frecv, msend, mrecv, nsend, nrecv, gsend, grecv, lsend, lrecv,
    *scratch,
):
    samples, feat, rays = feats.shape
    channels, seg = target.shape
    levels = regions.bit_length() - 1
    rows = back.shape[1]
    hidden = w2.shape[0]
    me = lax.axis_index("depth")
    view = lax.axis_index("view")
    work = scratch[0 : levels + 1]
    got = scratch[levels + 1 : 2 * levels + 1]
    notes = scratch[2 * levels + 1 : 3 * levels + 1]
    sums = scratch[3 * levels + 1 :]

    def bit_of(value, b):
        return lax.rem(value // (1 << b), 2)

    def partner(b):
        return {"depth": me + (1 - 2 * bit_of(me, b)) * (1 << b)}

    loads = [
        pltpu.make_async_copy(source, place, load_sem.at[n])
        for n, (source, place) in enumerate(
            (
                (w1_in, w1), (b1_in, b1), (w2_in, w2), (b2_in, b2), (w3_in, w3), (b3_in, b3),
                (feats_in, feats), (spacing_in, spacing), (counts_in, counts), (target_in, target),
            )
        )
    ]
    for load in loads:
        load.start()
    barrier = pltpu.get_barrier_semaphore()
    greeted = [(a, r) for a in range(views) for r in range(regions) if r == 0 or a % 2 == 0][1:]
    for a, r in greeted:
        where = {"view": lax.rem(view + a, views), "depth": lax.rem(me + r, regions)}
        pl.semaphore_signal(barrier, inc=1, device_id=where, device_id_type=MESH)

    for load in loads[:6]:
        load.wait()
    prepare(feat, w1, b1, w2, b2, w3, b3, w1s, w2f, w2b, w3f, w3b, cols)
    for load in loads[6:]:
        load.wait()

    parts = min(PARTS, seg // 128)
    wide = seg // parts

    def span_of(h, k):
        where = 0
        for b in range(levels):
            where = where + lax.rem(bit_of(me, b) + bit_of(k, levels - 1 - b), 2) * (1 << b)
        return pl.ds(pl.multiple_of(where * seg + h * wide, wide), wide)

    rank = rank_ref[0:1, 0:1]
    row = lax.broadcasted_iota(jnp.int32, (rows - channels, wide), 0)

    def first(b):
        return lax.rem(lax.div(rank, jnp.full_like(rank, 1 << b)), jnp.full_like(rank, 2)) == 0

    def halves(k):
        return [(j, regions >> (j + 1)) for j in range(levels) if k < regions >> (j + 1)]

    def color_copy(j, h, kk):
        n2 = regions >> (j + 1)
        return remote(
            work[j].at[h * 2 * n2 + n2 + kk], got[j].at[h * n2 + kk],
            (fsend, frecv), h * regions + n2 + kk, partner(j),
        )

    def misfit_copy(j, h, kk):
        n2 = regions >> (j + 1)
        part = pl.ds(0, channels)
        return remote(
            back.at[h * regions + kk, part], back.at[h * regions + n2 + kk, part],
            (msend, mrecv), h * regions + n2 + kk, partner(j),
        )

    def note_copy(j, h, kk):
        n2 = regions >> (j + 1)
        return remote(
            notes[j].at[h * n2 + kk], back.at[h * regions + n2 + kk, pl.ds(channels, rows - channels)],
            (nsend, nrecv), h * regions + n2 + kk, partner(j),
        )

    def gather_x(span):
        return jnp.concatenate([feats[s, :, span] for s in range(samples)], axis=1)

    def fold(h, k):
        for j, n2 in halves(k):
            color_copy(j, h, k).wait_recv()
            ahead = first(j)
            mine, other = work[j][h * 2 * n2 + k], got[j][h * n2 + k]
            mine_depth = mine[channels : channels + 1]
            other_depth = other[channels : channels + 1]
            mine_clear = jnp.where(ahead, 1.0, jnp.exp(-other_depth))
            other_clear = jnp.where(ahead, jnp.exp(-mine_depth), 1.0)
            at = h * n2 + k
            work[j + 1][at, 0:channels] = mine_clear * mine[0:channels] + other_clear * other[0:channels]
            work[j + 1][at, channels:rows] = mine[channels:rows] + other[channels:rows]
        if k:
            j = levels - k.bit_length()
            color_copy(j, h, k - (regions >> (j + 1))).start()

    def tell(h, k):
        at = h * regions + k
        if k == 0:
            span = pl.ds(h * wide, wide)
            color = work[levels][h, 0:channels]
            pixels[:, span] = color
            back[at, 0:channels] = color - target[:, span]
            back[at, channels:rows] = jnp.where(row == 0, 1.0, 0.0)
        else:
            j = levels - k.bit_length()
            misfit_copy(j, h, k - (regions >> (j + 1))).wait_recv()
        for j, n2 in reversed(halves(k)):
            misfit_copy(j, h, k).start()
        if k:
            j = levels - k.bit_length()
            note_copy(j, h, k - (regions >> (j + 1))).wait_recv()
        for j, n2 in reversed(halves(k)):
            ahead = first(j)
            mine, other = work[j][h * 2 * n2 + k], got[j][h * n2 + k]
            misfit = back[at, 0:channels]
            state = back[at, channels:rows]
            passed, behind = state[0:1], state[1:2]
            mine_depth = mine[channels : channels + 1]
            other_depth = other[channels : channels + 1]
            hind = jnp.where(ahead, other[0:channels], mine[0:channels])
            later = passed * jnp.exp(-jnp.where(ahead, mine_depth, other_depth))
            glow = behind + later * jnp.sum(misfit * hind, axis=0, keepdims=True)
            mine_state = (jnp.where(ahead, passed, later), jnp.where(ahead, glow, behind))
            other_state = (jnp.where(ahead, later, passed), jnp.where(ahead, behind, glow))
            notes[j][h * n2 + k] = jnp.where(row == 0, *other_state)
            note_copy(j, h, k).start()
            back[at, channels:rows] = jnp.where(row == 0, *mine_state)

    plan = make_plan(regions, parts)
    half = regions // 2
    tiles = [at for what, at in plan if what == "forward"]
    passes, events = [], {}
    ready = 0
    for what, at in plan:
        if what == "forward":
            ready += 1
        elif what in ("backward", "first"):
            passes.append((what, at))
        elif at[0][1] < half:
            key = ("ahead", ready - 1) if ready < len(tiles) else ("back", len(passes))
            events.setdefault(key, []).append((fold if what == "fold" else tell,) + at[0])
    last = max(n for n, at in enumerate(passes) if at[0] == "backward")
    passes, lasts = passes[: last + 1], [at for _, at in passes[last + 1 :]]

    def pick_tiles(i, table):
        out = []
        for n in range(parts):
            h = pick(i, [at[n][0] for at in table])
            k = pick(i, [at[n][1] for at in table])
            out.append((h, k, h * regions + k))
        return out

    def lengths(span):
        return [spacing[s, :, span] for s in range(samples)]

    def run_events(name, i):
        for (kind, at), calls in events.items():
            if kind == name:

                @pl.when(i == at)
                def _():
                    for call, h, k in calls:
                        call(h, k)

    def forward_step(i, carry):
        pair = pick_tiles(i, tiles)
        spans = [span_of(h, k) for h, k, _ in pair]
        results = forward_tile(
            feat, channels, jnp.concatenate([gather_x(span) for span in spans], axis=1),
            [lengths(span) for span in spans], [counts[:, span] for span in spans], w1s, w2f, w3f, cols,
            [keep_x.at[at] for _, _, at in pair], [keep_h.at[at] for _, _, at in pair],
            [keep_raw.at[at] for _, _, at in pair],
        )
        for (_, _, at), (color, depth) in zip(pair, results):
            work[0][at, 0:channels] = color
            work[0][at, channels:rows] = jnp.broadcast_to(depth, (rows - channels, wide))

        @pl.when(i == 0)
        def _():
            pl.semaphore_wait(barrier, len(greeted))

        for h, k, _ in pair:

            @pl.when(k >= half)
            def _():
                color_copy(0, h, k - half).start()

        run_events("ahead", i)
        return carry

    for acc in (acc1, acc2, acc3, bias):
        acc[...] = jnp.zeros_like(acc)
    lax.fori_loop(0, len(tiles), forward_step, 0)

    def backward_step(i, carry):
        run_events("back", i)
        pair = pick_tiles(i, [at[1] for at in passes])
        turn = pick(i, [int(at[0] == "backward") for at in passes])
        for h, k, _ in pair:

            @pl.when((turn == 1) & (k >= half))
            def _():
                misfit_copy(0, h, k - half).wait_recv()
                note_copy(0, h, k - half).wait_recv()

        @pl.when(turn == 1)
        def _():
            spans = [span_of(h, k) for h, k, _ in pair]
            backward_tile(
                channels, [keep_raw.at[at] for _, _, at in pair],
                [back[at, 0:channels] for _, _, at in pair], [back[at, channels:rows] for _, _, at in pair],
                [lengths(span) for span in spans], [counts[:, span] for span in spans],
                [keep_h.at[at] for _, _, at in pair], w3b, acc2, acc3, bias,
            )

        @pl.when(turn == 0)
        def _():
            first_layer_tile(
                [keep_x.at[at] for _, _, at in pair], [keep_h.at[at] for _, _, at in pair], w2b, acc1
            )

        return carry

    lax.fori_loop(0, len(passes), backward_step, 0)
    early = wide_stages(views, regions, grads, total, *sums[0:3], (gsend, grecv))
    late = small_stages(views, regions, grads_late, total_late, *sums[3:5], (lsend, lrecv))
    fill_blocks(grads, acc2, acc3, bias)
    early[0]()

    def first_layer_step(i, carry):
        pair = pick_tiles(i, lasts)
        first_layer_tile(
            [keep_x.at[at] for _, _, at in pair], [keep_h.at[at] for _, _, at in pair], w2b, acc1
        )

        @pl.when(i == min(1, len(lasts) - 1))
        def _():
            early[1]()

        return carry

    lax.fori_loop(0, len(lasts), first_layer_step, 0)
    fill_rows(grads_late, acc1, feat)
    early = early[2:]
    for which in "LLELLEE":
        (early if which == "E" else late).pop(0)()
    for h in range(parts):
        for j in range(levels):
            for kk in range(regions >> (j + 1)):
                color_copy(j, h, kk).wait_send()
                misfit_copy(j, h, kk).wait_send()
                note_copy(j, h, kk).wait_send()
    for close in early + late:
        close()


def whole_step(views, regions, feats, spacing, counts, target, rank, weights):
    samples, feat, rays = feats.shape
    channels, seg = target.shape
    hidden = weights[2].shape[0]
    levels = regions.bit_length() - 1
    rows = channels + 8
    parts = min(PARTS, seg // 128)
    tiles = parts * regions
    seg = seg // parts
    wide = samples * seg
    across = hidden // 128
    pairs = views // 2 * regions
    sizes = block_counts(feat, hidden, views, regions)
    inputs = (feats, spacing, counts, target) + tuple(weights)
    scratch = [pltpu.VMEM(value.shape, value.dtype) for value in inputs]
    scratch.append(pltpu.SemaphoreType.DMA((len(inputs),)))
    scratch += [
        pltpu.VMEM((hidden, 128), bf16),
        pltpu.VMEM((hidden, 3 * hidden), bf16),
        pltpu.VMEM((hidden, 2 * hidden), bf16),
        pltpu.VMEM((2 * PAD, hidden), bf16),
        pltpu.VMEM((hidden, 256), bf16),
        pltpu.VMEM((hidden, hidden), f32),
        pltpu.VMEM((tiles, 2, feat, wide), bf16),
        pltpu.VMEM((tiles, 2, hidden, wide), bf16),
        pltpu.VMEM((tiles, PAD, wide), f32),
        pltpu.VMEM((tiles, rows, seg), f32),
        pltpu.VMEM((sizes[0], 8, 128), f32),
        pltpu.VMEM((sizes[1], across, 128), f32),
        pltpu.VMEM((2 * feat + 16, hidden), f32),
        pltpu.VMEM((hidden + 16, hidden), f32),
        pltpu.VMEM((PAD, hidden), f32),
        pltpu.VMEM((PAD, 128), f32),
    ]
    scratch += [pltpu.SemaphoreType.DMA((tiles,))] * 6
    scratch += [pltpu.SemaphoreType.DMA((2 * pairs,))] * 2
    scratch += [pltpu.SemaphoreType.DMA((2 * regions + views - 3,))] * 2
    scratch += [pltpu.VMEM((tiles >> j, rows, seg), f32) for j in range(levels + 1)]
    scratch += [pltpu.VMEM((tiles >> (j + 1), rows, seg), f32) for j in range(levels)]
    scratch += [pltpu.VMEM((tiles >> (j + 1), 8, seg), f32) for j in range(levels)]
    half = sizes[0] // 2
    scratch += [pltpu.VMEM((half, 8, 128), f32)] * 2
    scratch.append(pltpu.VMEM((pairs - 1, half // pairs, 8, 128), f32))
    part = sizes[1] // regions
    scratch.append(pltpu.VMEM((regions - 1, part, across, 128), f32))
    scratch.append(pltpu.VMEM((views, part, across, 128), f32))
    vmem = pl.BlockSpec(memory_space=pltpu.VMEM)
    hbm = pl.BlockSpec(memory_space=pltpu.HBM)
    return pl.pallas_call(
        functools.partial(step_kernel, views, regions),
        in_specs=[hbm] * 4 + [vmem] + [hbm] * 6,
        out_specs=[vmem] * 3,
        out_shape=[
            jax.ShapeDtypeStruct(target.shape, f32),
            jax.ShapeDtypeStruct((sizes[0], 8, 128), f32),
            jax.ShapeDtypeStruct((sizes[1], across, 128), f32),
        ],
        scratch_shapes=scratch,
        compiler_params=pltpu.CompilerParams(
            collective_id=0, has_side_effects=True, vmem_limit_bytes=66000000
        ),
        name="whole_step",
    )(feats, spacing, counts, target, rank, *weights)


def finish_kernel(
    feat, hidden, outs,
    pixels_in, total, late,
    pixels, first_update, first_shift, second_update, second_shift, last_update, last_shift,
):
    def scaled(value, count):
        square = jnp.sum(jnp.sum(value * value, axis=0, keepdims=True), axis=1, keepdims=True)
        return value / jnp.sqrt(square / count + epsilon)

    pixels[...] = pixels_in[...]

    def join(source, at, rows):
        halves = []
        for _ in range(0, hidden, 128):
            halves.append(source[at : at + rows // 8].reshape(rows, 128))
            at += rows // 8
        return jnp.concatenate(halves, axis=1), at

    second, at = join(total, 0, hidden)
    last, at = join(total, at, PAD)
    across = hidden // 128
    first = jnp.concatenate([late[0:feat, i, :] for i in range(across)], axis=1)
    second_update[...] = scaled(second, hidden * hidden)
    first_update[...] = scaled(first, feat * hidden)
    last_update[...] = scaled(last, hidden * outs)[0:outs]
    rows = total[at]
    late_rows = late[feat]
    wide = lambda rows: jnp.concatenate([rows[i : i + 1] for i in range(across)], axis=1)
    first_shift[...] = scaled(wide(late_rows), hidden)
    second_shift[...] = scaled(wide(rows), hidden)
    last_shift[...] = scaled(rows[across : across + 1], outs)[:, 0:outs]


def finish(pixels, total, late, feat, hidden, outs):
    vmem = pl.BlockSpec(memory_space=pltpu.VMEM)
    shapes = [
        pixels.shape, (feat, hidden), (1, hidden), (hidden, hidden), (1, hidden),
        (outs, hidden), (1, outs),
    ]
    return pl.pallas_call(
        functools.partial(finish_kernel, feat, hidden, outs),
        in_specs=[vmem] * 3,
        out_specs=[vmem] * len(shapes),
        out_shape=[jax.ShapeDtypeStruct(shape, f32) for shape in shapes],
        name="normalize_all",
    )(pixels, total, late)


def local(
    features, spacing, counts, depth_rank, target,
    first_weight, first_bias, second_weight, second_bias, last_weight, last_bias,
):
    regions = lax.axis_size("depth")
    views = lax.axis_size("view")
    feat, hidden = first_weight.shape
    outs = last_weight.shape[1]
    feats, gaps, live = jnp.transpose(features[0, 0], (1, 0, 2)), jnp.transpose(spacing[0], (1, 0, 2)), counts[0]
    weights = (
        first_weight, first_bias[None], second_weight, second_bias[None],
        last_weight.T, last_bias[None],
    )
    pixels, total, late = whole_step(views, regions, feats, gaps, live, target[0], depth_rank, weights)
    results = finish(pixels, total, late, feat, hidden, outs)
    return (
        results[0][None], results[1], results[2][0], results[3], results[4][0],
        results[5].T, results[6][0],
    )


def solution(mesh):
    return jax.shard_map(
        local,
        mesh=mesh,
        in_specs=(
            P("view", "depth", None, None, None),
            P("view", "depth", None, None),
            P("view", "depth", None),
            P("view", "depth"),
            P("view", None, "depth"),
            P(), P(), P(), P(), P(), P(),
        ),
        out_specs=(P("view", None, "depth"), P(), P(), P(), P(), P(), P()),
        check_vma=False,
    )
```
